32 devices in a mesh: groups: 2 (over y), by: 4 (over z), bx: 2 (over x), bz: 2 (over core).
Axes of the slice: x: 2, y: 2, z: 4, core: 2. Of those that a mesh axis runs over, the one named last changes fastest.
Arguments:
- estimate: float32 [64, 64, 512], P(('groups', 'bz'), 'bx', 'by'), parts along dimension 0, may hold values from 0.5 to 2
- recorded: bfloat16 [6, 64, 64, 512], P(None, ('groups', 'bz'), ('bx', 'by')), parts along dimension 1, may hold values from 0.099609375 to 4
- profiles: float32 [6, 3, 15], replicated, may hold values from 0.02 to 0.12
- view_boxes: int32 [12, 6], P('groups'), parts along dimension 0, may hold values from 0 to 512, as said below
Outputs:
- refined: float32 [64, 64, 512], P(('groups', 'bz'), 'bx', 'by'), parts along dimension 0
The draws below stay inside these ranges and needn't reach their ends.
There are 2 independent parts, one for each index of `groups`. The reference program is written for one: setup_inputs(seed, part) draws one part's arguments, and reference() takes and returns one part's arrays. A program takes and returns all parts, laid end to end along the dimension named above; an argument that names none is the same for every part. Nothing has to cross between parts.
Inputs may be any that keep to these rules, and one draw needn't show every extreme that they name: `view_boxes`: every box has lower bound below upper bound, within the grid of 32 x 64 x 512 cells; the first view's box is the whole grid.
All inputs are finite; a program needn't handle non-finite values.
Results may differ from the reference program's by a relative error of at most 0.0003.
Values may be sent and summed in bfloat16 or wider, within the bound.
No kernel may reach another device: no remote copies, remote signals or barrier semaphores. Data moves between devices by JAX's collectives and lax.ppermute only.
A program may use at most 128 MiB of HBM per device.

```python
import math
import jax
import jax.numpy as jnp
from jax import lax

VIEWS = 6
TAPS = 15
NZ = 32
NX = 64
NY = 512


def draw_view_boxes(key, part):
    keys = jax.random.split(key, 3)
    first_view = jnp.arange(VIEWS) == 0
    columns = []
    for dimension, extent in enumerate((NZ, NX, NY)):
        low_key, high_key = jax.random.split(keys[dimension])
        lowest = jax.random.randint(low_key, (VIEWS,), 0, extent // 2)
        highest = jax.random.randint(high_key, (VIEWS,), extent // 2 + 1, extent + 1)
        columns.append(jnp.where(first_view, 0, lowest))
        columns.append(jnp.where(first_view, extent, highest))
    return jnp.stack(columns, axis=1).astype(jnp.int32)


def steps_of(key, shape, cuts, low, high):
    gain = 1.0
    for position, shards_of in cuts:
        draws = jax.random.uniform(jax.random.fold_in(jax.random.fold_in(key, 6), position), (shards_of,), jnp.float32, low / len(cuts), high / len(cuts))
        gain = gain * jnp.repeat(jnp.exp(draws), shape[position] // shards_of).reshape((-1,) + (1,) * (len(shape) - 1 - position))
    return gain


def setup_inputs(seed: int = 0, part: int = 0) -> dict:
    streams_of = jax.random.split(jax.random.key(seed), 5)
    part_keys = jax.random.split(jax.random.fold_in(streams_of[4], part), 5)
    estimate = jnp.clip(jnp.exp(math.log(2.0) - 1.3862944 * jax.random.uniform(part_keys[0], (NZ, NX, NY), jnp.float32) ** steps_of(part_keys[0], (NZ, NX, NY), ((0, 2), (1, 2), (2, 4)), -0.2, 0.2)), 0.5, 2.0)
    recorded = jnp.clip(jnp.exp(math.log(4.0) - 3.6927934 * jax.random.uniform(part_keys[1], (VIEWS, NZ, NX, NY), jnp.float32) ** steps_of(part_keys[1], (VIEWS, NZ, NX, NY), ((1, 2), (2, 8)), -0.2, 0.2)), 0.099609375, 4.0).astype(jnp.bfloat16)
    profiles = jnp.clip(jnp.exp(jax.random.uniform(streams_of[2], (VIEWS, 3, TAPS), jnp.float32, math.log(0.02), math.log(0.12))), 0.02, 0.12)
    view_boxes = draw_view_boxes(jax.random.fold_in(jax.random.fold_in(streams_of[4], part), 71), part)
    return dict(estimate=estimate, recorded=recorded, profiles=profiles, view_boxes=view_boxes)


BACKGROUND = 0.05


def smooth_axis(volume, kernel, axis_id):
    extent = volume.shape[axis_id]
    reach = kernel.shape[0] // 2
    widths = [(0, 0), (0, 0), (0, 0)]
    widths[axis_id] = (reach, reach)
    padded = jnp.pad(volume, widths)
    summed = kernel[0] * lax.slice_in_dim(padded, 0, extent, axis=axis_id)
    for offset in range(1, kernel.shape[0]):
        summed = summed + kernel[offset] * lax.slice_in_dim(padded, offset, offset + extent, axis=axis_id)
    return summed


def smooth_all(volume, kernels):
    volume = smooth_axis(volume, kernels[0], 0)
    volume = smooth_axis(volume, kernels[1], 1)
    return smooth_axis(volume, kernels[2], 2)


def box_inside(box):
    planes = jnp.arange(NZ, dtype=jnp.int32)
    rows_x = jnp.arange(NX, dtype=jnp.int32)
    cols_y = jnp.arange(NY, dtype=jnp.int32)
    along_z = ((planes >= box[0]) & (planes < box[1])).astype(jnp.float32)
    along_x = ((rows_x >= box[2]) & (rows_x < box[3])).astype(jnp.float32)
    along_y = ((cols_y >= box[4]) & (cols_y < box[5])).astype(jnp.float32)
    return along_z[:, None, None] * along_x[None, :, None] * along_y[None, None, :]


def reference(estimate, recorded, profiles, view_boxes):
    summed = jnp.zeros(estimate.shape, jnp.float32)
    coverage = jnp.zeros(estimate.shape, jnp.float32)
    for view_id in range(VIEWS):
        kernels = profiles[view_id]
        inside = box_inside(view_boxes[view_id])
        blurred = smooth_all(estimate, kernels)
        quotient = inside * recorded[view_id].astype(jnp.float32) / (blurred + BACKGROUND)
        returned = smooth_all(quotient, kernels[:, ::-1])
        summed = summed + inside * returned
        coverage = coverage + inside
    return estimate * summed / coverage
```

```python
import functools

import jax
import jax.numpy as jnp
from jax import lax
from jax.experimental import pallas as pl
from jax.experimental.pallas import tpu as pltpu
from jax.sharding import PartitionSpec as P

TAPS = 15
REACH = TAPS // 2
PAD = 8
BACKGROUND = 0.05

F32 = jnp.float32
BF16 = jnp.bfloat16

VMEM = pl.BlockSpec(memory_space=pltpu.VMEM)
SMEM = pl.BlockSpec(memory_space=pltpu.SMEM)


def call(body, out_shape, in_specs, scratch=(), flops=0, nbytes=0, name=None):
    many = isinstance(out_shape, (list, tuple))
    return pl.pallas_call(
        body,
        out_shape=out_shape,
        in_specs=in_specs,
        out_specs=[VMEM] * len(out_shape) if many else VMEM,
        scratch_shapes=list(scratch),
        compiler_params=pltpu.CompilerParams(vmem_limit_bytes=40 * 1024 * 1024),
        cost_estimate=pl.CostEstimate(
            flops=flops, bytes_accessed=nbytes, transcendentals=0
        ),
        name=name,
    )


def from_both(to_next, to_prev, axis):
    count = lax.axis_size(axis)
    return (
        lax.ppermute(to_next, axis, [(i, i + 1) for i in range(count - 1)]),
        lax.ppermute(to_prev, axis, [(i + 1, i) for i in range(count - 1)]),
    )


def banded(offset, weights, base):
    matrix = jnp.zeros(offset.shape, F32)
    for tap in range(TAPS):
        matrix = jnp.where(offset == tap, weights[base + tap], matrix)
    return matrix


def halves(matrix):
    high = matrix.astype(BF16).astype(F32)
    return high, matrix - high


def bands_body(views, block, prof_ref, box_ref, start_ref, yf_ref, yfh_ref, yr_ref, yrh_ref, xf_ref, xr_ref):
    _, bx, by = block
    ext = bx + 2 * PAD
    iota = lax.broadcasted_iota
    source = iota(jnp.int32, (by, by), 0)
    target = iota(jnp.int32, (by, by), 1)
    side = iota(jnp.int32, (2 * PAD, by), 0)
    side_source = jnp.where(side < PAD, side - PAD, by - PAD + side)
    side_target = iota(jnp.int32, (2 * PAD, by), 1)
    fx_col = iota(jnp.int32, (bx, 2 * ext), 1)
    fx_low = fx_col >= ext
    fx_off = jnp.where(fx_low, fx_col - ext, fx_col) - PAD - iota(jnp.int32, (bx, 2 * ext), 0)
    rx_col = iota(jnp.int32, (ext, 3 * bx), 1)
    rx_low = rx_col >= 2 * bx
    rx_row = iota(jnp.int32, (ext, 3 * bx), 0) - PAD
    rx_off = lax.rem(rx_col, bx) - rx_row

    def view(k, carry):
        base_x = (k * 3 + 1) * TAPS
        base_y = (k * 3 + 2) * TAPS

        def put(main_ref, halo_ref, matrix, halo):
            high, low = halves(matrix)
            main_ref[k, 0:by, :] = high.astype(BF16)
            main_ref[k, by : 2 * by, :] = low.astype(BF16)
            high, low = halves(halo)
            halo_ref[k, 0 : 2 * PAD, :] = high.astype(BF16)
            halo_ref[k, 2 * PAD : 4 * PAD, :] = low.astype(BF16)

        put(
            yf_ref,
            yfh_ref,
            banded(source - target + REACH, prof_ref, base_y),
            banded(side_source - side_target + REACH, prof_ref, base_y),
        )
        low_y = box_ref[k * 6 + 4] - start_ref[2]
        high_y = box_ref[k * 6 + 5] - start_ref[2]
        within = (target >= low_y) & (target < high_y)
        side_within = (side_target >= low_y) & (side_target < high_y)
        put(
            yr_ref,
            yrh_ref,
            jnp.where(within, banded(REACH - source + target, prof_ref, base_y), 0.0),
            jnp.where(side_within, banded(REACH - side_source + side_target, prof_ref, base_y), 0.0),
        )
        high, low = halves(banded(fx_off + REACH, prof_ref, base_x))
        xf_ref[k] = jnp.where(fx_low, low, high).astype(BF16)
        low_x = box_ref[k * 6 + 2] - start_ref[1]
        high_x = box_ref[k * 6 + 3] - start_ref[1]
        within = (rx_row >= low_x) & (rx_row < high_x)
        high, low = halves(jnp.where(within, banded(REACH - rx_off, prof_ref, base_x), 0.0))
        xr_ref[k] = jnp.where(rx_low, low, high).astype(BF16)
        return carry

    lax.fori_loop(0, views, view, 0)


def pick_columns(by):
    row = lax.broadcasted_iota(jnp.int32, (2 * PAD, by), 0)
    col = lax.broadcasted_iota(jnp.int32, (2 * PAD, by), 1)
    return jnp.where(col == jnp.where(row < PAD, row, by - 2 * PAD + row), 1.0, 0.0).astype(BF16)


def packed(cells):
    return lax.dot_general(
        pick_columns(cells.shape[1]), cells, (((1,), (1,)), ((), ())), preferred_element_type=F32
    ).astype(BF16)


def join_x_body(est_ref, left_ref, right_ref, out_ref):
    out_ref[...] = jnp.concatenate(
        [left_ref[...].astype(F32), est_ref[...], right_ref[...].astype(F32)], axis=1
    ).astype(BF16)


def join_z_body(mid_ref, below_ref, above_ref, cells_ref, first_ref, last_ref):
    depth, ext, by = mid_ref.shape
    cells_ref[0:PAD] = below_ref[...]
    cells_ref[PAD : PAD + depth] = mid_ref[...]
    cells_ref[PAD + depth :] = above_ref[...]
    sides = packed(cells_ref[...].reshape((depth + 2 * PAD) * ext, by))
    first_ref[...] = sides[:PAD]
    last_ref[...] = sides[PAD:]


def column_halo(left, right):
    both = jnp.concatenate([left.astype(F32), right.astype(F32)], axis=0)
    return jnp.concatenate([both, both], axis=0).T.astype(BF16)


def forward_body(views, block, prof_ref, box_ref, start_ref, cells_ref, left_ref, right_ref, yf_ref, yfh_ref, xf_ref, out_ref, halo, rows):
    bz, bx, by = block
    ext = bx + 2 * PAD
    deep = bz + 2 * PAD
    halo[...] = column_halo(left_ref[...], right_ref[...])
    step = 4
    row_x = lax.broadcasted_iota(jnp.int32, (8, by), 0)
    col_y = lax.broadcasted_iota(jnp.int32, (8, by), 1)

    def view(k, carry):
        along_y = yf_ref[k]
        along_side = yfh_ref[k]
        along_x = xf_ref[k]
        for first in range(0, deep, step):
            cells = cells_ref[first : first + step].reshape(step * ext, by)
            wide = jnp.concatenate([cells, cells], axis=1)
            mixed = jnp.dot(wide, along_y, preferred_element_type=F32)
            mixed = mixed + jnp.dot(
                halo[first * ext : (first + step) * ext, :], along_side, preferred_element_type=F32
            )
            mixed = mixed.astype(BF16).reshape(step, ext, by)
            for pair in range(0, step, 2):
                both = jnp.concatenate([mixed[pair], mixed[pair + 1]], axis=1)
                both = jnp.concatenate([both, both], axis=0)
                done = jnp.dot(along_x, both, preferred_element_type=F32)
                rows[first + pair] = done[:, :by]
                rows[first + pair + 1] = done[:, by:]
        taps = [prof_ref[k * 3 * TAPS + tap] for tap in range(TAPS)]
        low_z = box_ref[k * 6] - start_ref[0]
        high_z = box_ref[k * 6 + 1] - start_ref[0]
        low_x = box_ref[k * 6 + 2] - start_ref[1]
        high_x = box_ref[k * 6 + 3] - start_ref[1]
        low_y = box_ref[k * 6 + 4] - start_ref[2]
        high_y = box_ref[k * 6 + 5] - start_ref[2]
        within_y = (col_y >= low_y) & (col_y < high_y)
        for tile in range(0, bx, 8):
            within = within_y & (row_x + tile >= low_x) & (row_x + tile < high_x)
            inside = jnp.where(within, 1.0, 0.0)
            held = [rows[plane, tile : tile + 8, :] for plane in range(1, deep - 1)]
            for plane in range(bz):
                total = taps[0] * held[plane]
                for tap in range(1, TAPS):
                    total = total + taps[tap] * held[plane + tap]
                here = jnp.where((plane >= low_z) & (plane < high_z), 1.0, 0.0)
                out_ref[k, plane, tile : tile + 8, :] = here * inside / (total + BACKGROUND)
        return carry

    lax.fori_loop(0, views, view, 0)


def quotient_body(views, block, count, order_ref, *refs):
    gain_ref, parts = refs[0], refs[1 : 1 + count]
    quot_ref, first_ref, last_ref = refs[1 + count : 4 + count]
    held = refs[4 + count]
    bz, bx, by = block
    rows = bx // count

    def view(k, carry):
        for part, part_ref in enumerate(parts):
            at = pl.ds(pl.multiple_of(order_ref[part] * rows, rows), rows)
            held[:, at, :] = gain_ref[k, :, at, :] * part_ref[k].astype(F32)
        quot_ref[k] = held[...].astype(BF16)
        return carry

    lax.fori_loop(0, views, view, 0)
    sides = packed(quot_ref[...].reshape(views * bz * bx, by))
    first_ref[...] = sides[:PAD]
    last_ref[...] = sides[PAD:]


def return_body(views, block, prof_ref, box_ref, start_ref, quot_ref, left_ref, right_ref, yr_ref, yrh_ref, xr_ref, below_ref, mid_ref, above_ref, halo, rows, total):
    bz, bx, by = block
    ext = bx + 2 * PAD
    deep = bz + 2 * REACH
    halo[...] = column_halo(left_ref[...], right_ref[...])

    def view(k, carry):
        along_y = yr_ref[k]
        along_side = yrh_ref[k]
        along_x = xr_ref[k]
        cells = quot_ref[k].reshape(bz * bx, by)
        wide = jnp.concatenate([cells, cells], axis=1)
        mixed = jnp.dot(wide, along_y, preferred_element_type=F32)
        start = pl.multiple_of(k * (bz * bx), bz * bx)
        mixed = mixed + jnp.dot(
            halo[pl.ds(start, bz * bx), :], along_side, preferred_element_type=F32
        )
        high = mixed.astype(BF16)
        low = (mixed - high.astype(F32)).astype(BF16)
        high = high.reshape(bz, bx, by)
        low = low.reshape(bz, bx, by)
        for pair in range(0, bz, 2):
            upper = jnp.concatenate([high[pair], high[pair + 1]], axis=1)
            lower = jnp.concatenate([low[pair], low[pair + 1]], axis=1)
            both = jnp.concatenate([upper, lower, upper], axis=0)
            done = jnp.dot(along_x, both, preferred_element_type=F32)
            rows[pair] = done[:, :by]
            rows[pair + 1] = done[:, by:]
        taps = [prof_ref[k * 3 * TAPS + tap] for tap in range(TAPS)]
        low_z = box_ref[k * 6] - start_ref[0]
        high_z = box_ref[k * 6 + 1] - start_ref[0]
        for tile in range(0, ext, 8):
            held = [rows[plane, tile : tile + 8, :] for plane in range(bz)]
            for out in range(deep):
                plane = out - REACH
                part = None
                for source in range(max(0, plane - REACH), min(bz, plane + REACH + 1)):
                    term = taps[REACH - source + plane] * held[source]
                    part = term if part is None else part + term
                here = jnp.where((plane >= low_z) & (plane < high_z), 1.0, 0.0)
                part = here * part
                total[out, tile : tile + 8, :] = jnp.where(
                    k == 0, part, total[out, tile : tile + 8, :] + part
                )
        return carry

    total[...] = jnp.zeros_like(total)
    lax.fori_loop(0, views, view, 0)
    below_ref[...] = total[:REACH]
    mid_ref[...] = total[REACH : REACH + bz]
    above_ref[...] = total[REACH + bz :]


def add_z_body(mid_ref, below_ref, above_ref, mid_out, left_out, right_out):
    bz, ext, by = mid_ref.shape
    for plane in range(bz):
        cells = mid_ref[plane]
        if plane < REACH:
            cells = cells + below_ref[plane]
        if plane >= bz - REACH:
            cells = cells + above_ref[plane - (bz - REACH)]
        left_out[plane] = cells[:PAD]
        mid_out[plane] = cells[PAD : ext - PAD]
        right_out[plane] = cells[ext - PAD :]


def finish_body(views, box_ref, start_ref, est_ref, mid_ref, left_ref, right_ref, out_ref):
    bz, bx, by = est_ref.shape
    row_x = lax.broadcasted_iota(jnp.int32, (8, by), 0)
    col_y = lax.broadcasted_iota(jnp.int32, (8, by), 1)
    for tile in range(0, bx, 8):
        flat = []
        for k in range(views):
            low_x = box_ref[k * 6 + 2] - start_ref[1] - tile
            high_x = box_ref[k * 6 + 3] - start_ref[1] - tile
            low_y = box_ref[k * 6 + 4] - start_ref[2]
            high_y = box_ref[k * 6 + 5] - start_ref[2]
            within = (col_y >= low_y) & (col_y < high_y) & (row_x >= low_x) & (row_x < high_x)
            flat.append(jnp.where(within, 1.0, 0.0))
        for plane in range(bz):
            coverage = jnp.zeros((8, by), F32)
            for k in range(views):
                low_z = box_ref[k * 6] - start_ref[0]
                high_z = box_ref[k * 6 + 1] - start_ref[0]
                here = jnp.where((plane >= low_z) & (plane < high_z), 1.0, 0.0)
                coverage = coverage + here * flat[k]
            cells = mid_ref[plane, tile : tile + 8, :]
            if tile == 0:
                cells = cells + left_ref[plane]
            if tile == bx - 8:
                cells = cells + right_ref[plane]
            out_ref[plane, tile : tile + 8, :] = est_ref[plane, tile : tile + 8, :] * cells / coverage


def local(estimate, recorded, profiles, view_boxes):
    block = estimate.shape
    bz, bx, by = block
    views = recorded.shape[0]
    part_rows = recorded.shape[2]
    count = lax.axis_size("by")
    mine = lax.axis_index("by")
    ext = bx + 2 * PAD
    deep = bz + 2 * PAD
    shape = jax.ShapeDtypeStruct

    start = jnp.stack(
        [lax.axis_index("bz") * bz, lax.axis_index("bx") * bx, mine * by]
    ).astype(jnp.int32)
    taps = profiles.reshape(-1)
    boxes = view_boxes.reshape(-1)

    if count == 4 and part_rows % 8 == 0:
        pieces = [recorded[:, :, :, i * by : (i + 1) * by] for i in range(count)]
        stacked = jnp.stack(pieces)
        parts = [lax.dynamic_index_in_dim(stacked, mine, 0, keepdims=False)]
        for other in range(1, count):
            piece = lax.dynamic_index_in_dim(stacked, mine ^ other, 0, keepdims=False)
            parts.append(lax.ppermute(piece, "by", [(i, i ^ other) for i in range(count)]))
        order = jnp.stack([mine ^ other for other in range(count)]).astype(jnp.int32)
    else:
        parts = [lax.all_to_all(recorded, "by", split_axis=3, concat_axis=2, tiled=True)]
        order = jnp.zeros((1,), jnp.int32)

    head = estimate[:, :PAD].astype(BF16)
    tail = estimate[:, bx - PAD :].astype(BF16)
    left, right = from_both(tail, head, "bx")
    wide = call(
        join_x_body, shape((bz, ext, by), BF16), [VMEM] * 3, nbytes=bz * ext * by * 4, name="join_x"
    )(estimate, left, right)
    below, above = from_both(wide[bz - PAD :], wide[:PAD], "bz")
    cells, first, last = call(
        join_z_body,
        [shape((deep, ext, by), BF16), shape((PAD, deep * ext), BF16), shape((PAD, deep * ext), BF16)],
        [VMEM] * 3,
        nbytes=deep * ext * by * 4,
        name="join_z",
    )(wide, below, above)
    left, right = from_both(last, first, "by")

    yf, yfh, yr, yrh, xf, xr = call(
        functools.partial(bands_body, views, block),
        [
            shape((views, 2 * by, by), BF16),
            shape((views, 4 * PAD, by), BF16),
            shape((views, 2 * by, by), BF16),
            shape((views, 4 * PAD, by), BF16),
            shape((views, bx, 2 * ext), BF16),
            shape((views, ext, 3 * bx), BF16),
        ],
        [SMEM] * 3,
        flops=views * 64 * by * by,
        nbytes=views * by * by * 8,
        name="bands",
    )(taps, boxes, start)

    gain = call(
        functools.partial(forward_body, views, block),
        shape((views, bz, bx, by), F32),
        [SMEM] * 3 + [VMEM] * 6,
        [pltpu.VMEM((deep * ext, 4 * PAD), BF16), pltpu.VMEM((deep, bx, by), F32)],
        flops=views * deep * ext * by * 600,
        nbytes=views * bz * bx * by * 8,
        name="forward",
    )(taps, boxes, start, cells, left, right, yf, yfh, xf)

    quot, first, last = call(
        functools.partial(quotient_body, views, block, len(parts)),
        [
            shape((views, bz, bx, by), BF16),
            shape((PAD, views * bz * bx), BF16),
            shape((PAD, views * bz * bx), BF16),
        ],
        [SMEM] + [VMEM] * (1 + len(parts)),
        [pltpu.VMEM((bz, bx, by), F32)],
        flops=views * bz * bx * by * 40,
        nbytes=views * bz * bx * by * 8,
        name="quotient",
    )(order, gain, *parts)
    left, right = from_both(last, first, "by")

    below, mid, above = call(
        functools.partial(return_body, views, block),
        [
            shape((REACH, ext, by), F32),
            shape((bz, ext, by), F32),
            shape((REACH, ext, by), F32),
        ],
        [SMEM] * 3 + [VMEM] * 6,
        [
            pltpu.VMEM((views * bz * bx, 4 * PAD), BF16),
            pltpu.VMEM((bz, ext, by), F32),
            pltpu.VMEM((bz + 2 * REACH, ext, by), F32),
        ],
        flops=views * bz * ext * by * 600,
        nbytes=views * bz * bx * by * 8,
        name="returned",
    )(taps, boxes, start, quot, left, right, yr, yrh, xr)
    below, above = from_both(above, below, "bz")
    mid, left, right = call(
        add_z_body,
        [shape((bz, bx, by), F32), shape((bz, PAD, by), F32), shape((bz, PAD, by), F32)],
        [VMEM] * 3,
        nbytes=bz * ext * by * 8,
        name="add_z",
    )(mid, below, above)
    left, right = from_both(right, left, "bx")
    return call(
        functools.partial(finish_body, views),
        shape(block, F32),
        [SMEM] * 2 + [VMEM] * 4,
        nbytes=bz * bx * by * 12,
        name="finish",
    )(boxes, start, estimate, mid, left, right)


def solution(mesh):
    placed = (
        P(("groups", "bz"), "bx", "by"),
        P(None, ("groups", "bz"), ("bx", "by"), None),
        P(),
        P("groups", None),
    )
    return jax.shard_map(
        local,
        mesh=mesh,
        in_specs=placed,
        out_specs=P(("groups", "bz"), "bx", "by"),
        check_vma=False,
    )
```

```python
import functools

import jax
import jax.numpy as jnp
from jax import lax
from jax.experimental import pallas as pl
from jax.experimental.pallas import tpu as pltpu
from jax.sharding import PartitionSpec as P

TAPS = 15
REACH = TAPS // 2
PAD = 8
BACKGROUND = 0.05

F32 = jnp.float32
BF16 = jnp.bfloat16

VMEM = pl.BlockSpec(memory_space=pltpu.VMEM)
SMEM = pl.BlockSpec(memory_space=pltpu.SMEM)


def call(body, out_shape, in_specs, scratch=(), flops=0, nbytes=0, name=None):
    many = isinstance(out_shape, (list, tuple))
    return pl.pallas_call(
        body,
        out_shape=out_shape,
        in_specs=in_specs,
        out_specs=[VMEM] * len(out_shape) if many else VMEM,
        scratch_shapes=list(scratch),
        compiler_params=pltpu.CompilerParams(vmem_limit_bytes=40 * 1024 * 1024),
        cost_estimate=pl.CostEstimate(
            flops=flops, bytes_accessed=nbytes, transcendentals=0
        ),
        name=name,
    )


def partner(index, count, swap):
    other = index ^ 1 if swap == 0 else ((index + 1) ^ 1) - 1
    return other if 0 <= other < count else index


def swaps_of(count):
    return {1: [], 2: [0]}.get(count, [0, 1])


def meets_next(index, swap):
    return lax.rem(index + swap, 2) == 0


def has_partner(index, count, swap):
    after = meets_next(index, swap)
    return jnp.where(after, index < count - 1, index > 0)


def links_of(count_x, count_z):
    along_x, along_z = [None, *swaps_of(count_x)], [None, *swaps_of(count_z)]
    return [(x, z) for x in along_x for z in along_z if (x, z) != (None, None)]


def exchange(cells, link, count_x, count_z):
    x, z = link
    pairs = []
    for i in range(count_x):
        for j in range(count_z):
            to_x = i if x is None else partner(i, count_x, x)
            to_z = j if z is None else partner(j, count_z, z)
            pairs.append((i * count_z + j, to_x * count_z + to_z))
    return lax.ppermute(cells, ("bx", "bz"), pairs)


def exchange_y(first, second):
    count = lax.axis_size("by")
    return [
        lax.ppermute(cells, "by", [(i, partner(i, count, swap)) for i in range(count)])
        for swap, cells in enumerate((first, second))
    ]


def banded(offset, tap_of):
    matrix = jnp.zeros(offset.shape, F32)
    for tap in range(TAPS):
        matrix = jnp.where(offset == tap, tap_of(tap), matrix)
    return matrix


def halves(matrix):
    high = matrix.astype(BF16)
    return high, (matrix - high.astype(F32)).astype(BF16)


def prepare_body(views, count, counts, links, est_ref, rec_ref, *out_refs):
    bz, bx, by = est_ref.shape
    mine = lax.axis_index("by")
    for other in range(count):
        at = pl.ds(pl.multiple_of((mine ^ other) * by, by), by)
        out_refs[other][...] = rec_ref[:, :, :, at]
    for (x, z), out_ref in zip(links, out_refs[count:]):
        at_x, at_z = slice(None), slice(None)
        if x is not None:
            begin = jnp.where(meets_next(lax.axis_index("bx"), x), bx - PAD, 0)
            at_x = pl.ds(pl.multiple_of(begin, PAD), PAD)
        if z is not None:
            begin = jnp.where(meets_next(lax.axis_index("bz"), z), bz - PAD, 0)
            at_z = pl.ds(begin, PAD)
        out_ref[...] = est_ref[at_z, at_x, :].astype(BF16)


def packed(cells, begin):
    by = cells.shape[1]
    row = lax.broadcasted_iota(jnp.int32, (PAD, by), 0)
    col = lax.broadcasted_iota(jnp.int32, (PAD, by), 1)
    pick = jnp.where(col == row + begin, 1.0, 0.0).astype(BF16)
    return lax.dot_general(
        pick, cells, (((1,), (1,)), ((), ())), preferred_element_type=F32
    ).astype(BF16)


def pack_both(cells, by, first_ref, second_ref):
    last = by - PAD
    mine = lax.axis_index("by")
    first_ref[...] = packed(cells, jnp.where(meets_next(mine, 0), last, 0))
    second_ref[...] = packed(cells, jnp.where(meets_next(mine, 1), last, 0))


def unpack_both(count, first_ref, second_ref):
    mine = lax.axis_index("by")
    first, second = first_ref[...].astype(F32), second_ref[...].astype(F32)
    even = meets_next(mine, 0)
    before = jnp.where(even, second, first)
    after = jnp.where(even, first, second)
    before = jnp.where(mine > 0, before, 0.0)
    after = jnp.where(mine < count - 1, after, 0.0)
    return jnp.concatenate([before, after], axis=0).T.astype(BF16)


def join_body(counts, links, est_ref, *refs):
    bz, bx, by = est_ref.shape
    ext = bx + 2 * PAD
    deep = bz + 2 * PAD
    link_refs = refs[: len(links)]
    cells_ref, first_ref, second_ref, wide = refs[len(links) :]
    wide[...] = jnp.zeros_like(wide)
    wide[PAD : PAD + bz, PAD : PAD + bx, :] = est_ref[...]
    for (x, z), link_ref in zip(links, link_refs):
        at_x, at_z, known = slice(PAD, PAD + bx), slice(PAD, PAD + bz), None
        if x is not None:
            index = lax.axis_index("bx")
            begin = jnp.where(meets_next(index, x), PAD + bx, 0)
            at_x = pl.ds(pl.multiple_of(begin, PAD), PAD)
            known = has_partner(index, counts[0], x)
        if z is not None:
            index = lax.axis_index("bz")
            at_z = pl.ds(jnp.where(meets_next(index, z), PAD + bz, 0), PAD)
            there = has_partner(index, counts[1], z)
            known = there if known is None else known & there

        @pl.when(known)
        def _():
            wide[at_z, at_x, :] = link_ref[...].astype(F32)

    cells_ref[...] = wide[...].astype(BF16)
    pack_both(cells_ref[...].reshape(deep * ext, by), by, first_ref, second_ref)


def bands_body(views, prof_ref, box_ref, est_ref, yf_ref, yr_ref, xf_ref, xr_ref, share_ref):
    bz, bx, by = est_ref.shape
    ext = bx + 2 * PAD
    start_z = lax.axis_index("bz") * bz
    start_x = lax.axis_index("bx") * bx
    start_y = lax.axis_index("by") * by

    def iota(shape, dim):
        return lax.broadcasted_iota(jnp.int32, shape, dim)

    shape_y = (by + 2 * PAD, by)
    row = iota(shape_y, 0)
    source = jnp.where(row < by, row, jnp.where(row < by + PAD, row - by - PAD, row - PAD))
    target = iota(shape_y, 1)
    shape_x = (bx, 2 * ext)
    col = iota(shape_x, 1)
    is_low = col >= ext
    forward_x = jnp.where(is_low, col - ext, col) - PAD - iota(shape_x, 0)

    def view(k, carry):
        forward = banded(source - target + REACH, lambda tap: prof_ref[k, 2, tap])
        high, low = halves(forward)
        yf_ref[k, :, :by] = high
        yf_ref[k, :, by:] = low
        back = banded(REACH - source + target, lambda tap: prof_ref[k, 2, tap])
        within = (target >= box_ref[k, 4] - start_y) & (target < box_ref[k, 5] - start_y)
        high, low = halves(jnp.where(within, back, 0.0))
        yr_ref[k, :, :by] = high
        yr_ref[k, :, by:] = low
        high, low = halves(banded(forward_x + REACH, lambda tap: prof_ref[k, 1, tap]))
        at = pl.ds(pl.multiple_of(k * bx, bx), bx)
        xf_ref[at, :] = jnp.where(is_low, low.astype(F32), high.astype(F32)).astype(BF16)
        return carry

    lax.fori_loop(0, views, view, 0)

    shape_x = (ext, views * bx)
    target = iota(shape_x, 0) - PAD
    col = iota(shape_x, 1)

    def back_view(k, matrix):
        source = col - k * bx
        back = banded(REACH - source + target, lambda tap: prof_ref[k, 1, tap])
        within = (source >= 0) & (source < bx)
        within = within & (target >= box_ref[k, 2] - start_x) & (target < box_ref[k, 3] - start_x)
        return jnp.where(within, back, matrix)

    high, low = halves(lax.fori_loop(0, views, back_view, jnp.zeros(shape_x, F32)))
    xr_ref[:ext] = high
    xr_ref[ext:] = low

    row_x = iota((bx, by), 0) + start_x
    col_y = iota((bx, by), 1) + start_y
    flat = []
    for k in range(views):
        within = (col_y >= box_ref[k, 4]) & (col_y < box_ref[k, 5])
        within = within & (row_x >= box_ref[k, 2]) & (row_x < box_ref[k, 3])
        flat.append(jnp.where(within, 1.0, 0.0))
    for plane in range(bz):
        coverage = jnp.zeros((bx, by), F32)
        for k in range(views):
            at = plane + start_z
            here = (at >= box_ref[k, 0]) & (at < box_ref[k, 1])
            coverage = coverage + jnp.where(here, 1.0, 0.0) * flat[k]
        share_ref[plane] = est_ref[plane] / coverage


def forward_body(views, block, count, prof_ref, box_ref, cells_ref, first_ref, second_ref, yf_ref, xf_ref, gain_ref, halo, blurred_x, rows):
    bz, bx, by = block
    ext = bx + 2 * PAD
    deep = bz + 2 * PAD
    halo[...] = unpack_both(count, first_ref, second_ref)
    for plane in range(1, deep - 1):
        cells = jnp.concatenate([cells_ref[plane], halo[plane * ext : (plane + 1) * ext, :]], axis=1)
        cells = jnp.concatenate([cells, cells], axis=0)
        mixed = jnp.dot(xf_ref[...], cells, preferred_element_type=F32).astype(BF16)
        for k in range(views):
            blurred_x[k, plane * bx : (plane + 1) * bx, :] = mixed[k * bx : (k + 1) * bx]
    row_x = lax.broadcasted_iota(jnp.int32, (8, by), 0) + lax.axis_index("bx") * bx
    col_y = lax.broadcasted_iota(jnp.int32, (8, by), 1) + lax.axis_index("by") * by
    start_z = lax.axis_index("bz") * bz
    step = 10

    def view(k, carry):
        along_y = yf_ref[k]
        for first in range(1, deep - 1, step):
            mixed = jnp.dot(
                blurred_x[k, first * bx : (first + step) * bx, :], along_y, preferred_element_type=F32
            )
            rows[first : first + step] = (mixed[:, :by] + mixed[:, by:]).reshape(step, bx, by)
        taps = [prof_ref[k, 0, tap] for tap in range(TAPS)]
        within_y = (col_y >= box_ref[k, 4]) & (col_y < box_ref[k, 5])
        inside = []
        for tile in range(0, bx, 8):
            at = row_x + tile
            inside.append(jnp.where(within_y & (at >= box_ref[k, 2]) & (at < box_ref[k, 3]), 1.0, 0.0))
        gain_ref[k] = jnp.zeros((bz, bx, by), F32)

        def plane_of(plane, carry):
            for tile in range(0, bx, 8):
                total = taps[0] * rows[plane + 1, tile : tile + 8, :]
                for tap in range(1, TAPS):
                    total = total + taps[tap] * rows[plane + 1 + tap, tile : tile + 8, :]
                gain_ref[k, plane, tile : tile + 8, :] = inside[tile // 8] / (total + BACKGROUND)
            return carry

        begin = jnp.clip(box_ref[k, 0] - start_z, 0, bz)
        end = jnp.clip(box_ref[k, 1] - start_z, 0, bz)
        lax.fori_loop(begin, end, plane_of, 0)
        return carry

    lax.fori_loop(0, views, view, 0)


def quotient_body(views, block, count, gain_ref, *refs):
    parts = refs[:count]
    quot_ref, first_ref, second_ref, held = refs[count:]
    bz, bx, by = block
    rows = bx // count
    mine = lax.axis_index("by") if count > 1 else 0

    def view(k, carry):
        for part, part_ref in enumerate(parts):
            at = pl.ds(pl.multiple_of((mine ^ part) * rows, rows), rows)
            held[:, at, :] = gain_ref[k, :, at, :] * part_ref[k].astype(F32)
        quot_ref[k] = held[...].astype(BF16)
        return carry

    lax.fori_loop(0, views, view, 0)
    pack_both(quot_ref[...].reshape(views * bz * bx, by), by, first_ref, second_ref)


def return_body(views, block, count, counts, links, prof_ref, box_ref, quot_ref, first_ref, second_ref, yr_ref, xr_ref, mid_ref, *refs):
    bz, bx, by = block
    ext = bx + 2 * PAD
    deep = bz + 2 * REACH
    link_refs = refs[: len(links)]
    halo, rows, high_rows, low_rows, total = refs[len(links) :]
    halo[...] = unpack_both(count, first_ref, second_ref)
    start_z = lax.axis_index("bz") * bz

    def view(k, carry):
        start = pl.multiple_of(k * (bz * bx), bz * bx)
        cells = quot_ref[k].reshape(bz * bx, by)
        cells = jnp.concatenate([cells, halo[pl.ds(start, bz * bx), :]], axis=1)
        mixed = jnp.dot(cells, yr_ref[k], preferred_element_type=F32)
        rows[...] = (mixed[:, :by] + mixed[:, by:]).reshape(bz, bx, by)
        taps = [prof_ref[k, 0, tap] for tap in range(TAPS)]
        at = pl.ds(pl.multiple_of(k * bx, bx), bx)
        for out in range(deep):
            plane = out - REACH
            here = (plane + start_z >= box_ref[k, 0]) & (plane + start_z < box_ref[k, 1])

            @pl.when(here)
            def _():
                sums = []
                for tile in range(0, bx, 8):
                    part = None
                    for source in range(max(0, plane - REACH), min(bz, plane + REACH + 1)):
                        term = taps[REACH - source + plane] * rows[source, tile : tile + 8, :]
                        part = term if part is None else part + term
                    sums.append(part)
                high, low = halves(jnp.concatenate(sums, axis=0))
                high_rows[out, at, :] = high
                low_rows[out, at, :] = low

            @pl.when(jnp.logical_not(here))
            def _():
                high_rows[out, at, :] = jnp.zeros((bx, by), BF16)
                low_rows[out, at, :] = jnp.zeros((bx, by), BF16)

        return carry

    lax.fori_loop(0, views, view, 0)
    for out in range(0, deep, 2):
        high = jnp.concatenate([high_rows[out], high_rows[out + 1]], axis=1)
        low = jnp.concatenate([low_rows[out], low_rows[out + 1]], axis=1)
        mixed = jnp.dot(xr_ref[...], high, preferred_element_type=F32)
        mixed = mixed[:ext] + mixed[ext:] + jnp.dot(xr_ref[:ext], low, preferred_element_type=F32)
        total[out] = mixed[:, :by]
        total[out + 1] = mixed[:, by:]
    mid_ref[...] = total[REACH : REACH + bz, PAD : PAD + bx, :]
    for (x, z), link_ref in zip(links, link_refs):
        at_x, at_z = slice(PAD, PAD + bx), slice(REACH, REACH + bz)
        if x is not None:
            begin = jnp.where(meets_next(lax.axis_index("bx"), x), PAD + bx, 0)
            at_x = pl.ds(pl.multiple_of(begin, PAD), PAD)
        if z is not None:
            at_z = pl.ds(jnp.where(meets_next(lax.axis_index("bz"), z), REACH + bz, 0), REACH)
        link_ref[...] = total[at_z, at_x, :]


def finish_body(counts, links, share_ref, mid_ref, *refs):
    bz, bx, by = share_ref.shape
    link_refs, out_ref = refs[: len(links)], refs[len(links)]
    out_ref[...] = share_ref[...] * mid_ref[...]
    for (x, z), link_ref in zip(links, link_refs):
        at_x, at_z, known = slice(None), slice(None), None
        if x is not None:
            index = lax.axis_index("bx")
            begin = jnp.where(meets_next(index, x), bx - PAD, 0)
            at_x = pl.ds(pl.multiple_of(begin, PAD), PAD)
            known = has_partner(index, counts[0], x)
        if z is not None:
            index = lax.axis_index("bz")
            at_z = pl.ds(jnp.where(meets_next(index, z), bz - REACH, 0), REACH)
            there = has_partner(index, counts[1], z)
            known = there if known is None else known & there

        @pl.when(known)
        def _():
            out_ref[at_z, at_x, :] = out_ref[at_z, at_x, :] + share_ref[at_z, at_x, :] * link_ref[...]


def local(estimate, recorded, profiles, view_boxes):
    block = estimate.shape
    bz, bx, by = block
    views = recorded.shape[0]
    part_rows = recorded.shape[2]
    count = lax.axis_size("by")
    counts = (lax.axis_size("bx"), lax.axis_size("bz"))
    links = links_of(*counts)
    ext = bx + 2 * PAD
    deep = bz + 2 * PAD
    shape = jax.ShapeDtypeStruct

    def link_shape(link, reach, dtype):
        x, z = link
        return shape((bz if z is None else reach, bx if x is None else PAD, by), dtype)

    swapped = count & (count - 1) == 0 and count <= 4 and part_rows % 8 == 0
    holders = count if swapped else 0
    sent = call(
        functools.partial(prepare_body, views, holders, counts, links),
        [shape((views, bz, part_rows, by), BF16)] * holders
        + [link_shape(link, PAD, BF16) for link in links],
        [VMEM] * 2,
        nbytes=views * bz * bx * by * 4,
        name="prepare",
    )(estimate, recorded)
    if swapped:
        parts = [sent[0]] + [
            lax.ppermute(sent[other], "by", [(i, i ^ other) for i in range(count)])
            for other in range(1, count)
        ]
    else:
        parts = [lax.all_to_all(recorded, "by", split_axis=3, concat_axis=2, tiled=True)]

    came = [exchange(cells, link, *counts) for link, cells in zip(links, sent[holders:])]
    side = shape((PAD, deep * ext), BF16)
    cells, first, second = call(
        functools.partial(join_body, counts, links),
        [shape((deep, ext, by), BF16), side, side],
        [VMEM] * (1 + len(links)),
        [pltpu.VMEM((deep, ext, by), F32)],
        nbytes=deep * ext * by * 4,
        name="join",
    )(estimate, *came)
    first, second = exchange_y(first, second)

    yf, yr, xf, xr, share = call(
        functools.partial(bands_body, views),
        [
            shape((views, by + 2 * PAD, 2 * by), BF16),
            shape((views, by + 2 * PAD, 2 * by), BF16),
            shape((views * bx, 2 * ext), BF16),
            shape((2 * ext, views * bx), BF16),
            shape(block, F32),
        ],
        [SMEM] * 2 + [VMEM],
        flops=views * 64 * by * by,
        nbytes=views * by * by * 8,
        name="bands",
    )(profiles, view_boxes, estimate)

    gain = call(
        functools.partial(forward_body, views, block, count),
        shape((views, bz, bx, by), F32),
        [SMEM] * 2 + [VMEM] * 5,
        [
            pltpu.VMEM((deep * ext, 2 * PAD), BF16),
            pltpu.VMEM((views, deep * bx, by + 2 * PAD), BF16),
            pltpu.VMEM((deep, bx, by), F32),
        ],
        flops=views * deep * ext * by * 600,
        nbytes=views * bz * bx * by * 8,
        name="forward",
    )(profiles, view_boxes, cells, first, second, yf, xf)

    side = shape((PAD, views * bz * bx), BF16)
    quot, first, second = call(
        functools.partial(quotient_body, views, block, len(parts)),
        [shape((views, bz, bx, by), BF16), side, side],
        [VMEM] * (1 + len(parts)),
        [pltpu.VMEM((bz, bx, by), F32)],
        flops=views * bz * bx * by * 40,
        nbytes=views * bz * bx * by * 8,
        name="quotient",
    )(gain, *parts)
    first, second = exchange_y(first, second)

    mid, *sums = call(
        functools.partial(return_body, views, block, count, counts, links),
        [shape(block, F32)] + [link_shape(link, REACH, F32) for link in links],
        [SMEM] * 2 + [VMEM] * 5,
        [
            pltpu.VMEM((views * bz * bx, 2 * PAD), BF16),
            pltpu.VMEM((bz, bx, by), F32),
            pltpu.VMEM((bz + 2 * REACH, views * bx, by), BF16),
            pltpu.VMEM((bz + 2 * REACH, views * bx, by), BF16),
            pltpu.VMEM((bz + 2 * REACH, ext, by), F32),
        ],
        flops=views * bz * ext * by * 600,
        nbytes=views * bz * bx * by * 8,
        name="returned",
    )(profiles, view_boxes, quot, first, second, yr, xr)
    sums = [exchange(cells, link, *counts) for link, cells in zip(links, sums)]
    return call(
        functools.partial(finish_body, counts, links),
        shape(block, F32),
        [VMEM] * (2 + len(links)),
        nbytes=bz * bx * by * 12,
        name="finish",
    )(share, mid, *sums)


def solution(mesh):
    placed = (
        P(("groups", "bz"), "bx", "by"),
        P(None, ("groups", "bz"), ("bx", "by"), None),
        P(),
        P("groups", None),
    )
    return jax.shard_map(
        local,
        mesh=mesh,
        in_specs=placed,
        out_specs=P(("groups", "bz"), "bx", "by"),
        check_vma=False,
    )
```

```python
import functools

import jax
import jax.numpy as jnp
from jax import lax
from jax.experimental import pallas as pl
from jax.experimental.pallas import tpu as pltpu
from jax.sharding import PartitionSpec as P

TAPS = 15
REACH = TAPS // 2
PAD = 8
BACKGROUND = 0.05
WEIGHT = 0.7

F32 = jnp.float32
BF16 = jnp.bfloat16

VMEM = pl.BlockSpec(memory_space=pltpu.VMEM)
SMEM = pl.BlockSpec(memory_space=pltpu.SMEM)
ANY = pl.BlockSpec(memory_space=pl.ANY)
HBM = pl.BlockSpec(memory_space=pltpu.HBM)


def call(body, out_shape, in_specs, scratch=(), flops=0, nbytes=0, name=None):
    many = isinstance(out_shape, (list, tuple))
    return pl.pallas_call(
        body,
        out_shape=out_shape,
        in_specs=in_specs,
        out_specs=[VMEM] * len(out_shape) if many else VMEM,
        scratch_shapes=list(scratch),
        compiler_params=pltpu.CompilerParams(vmem_limit_bytes=40 * 1024 * 1024),
        cost_estimate=pl.CostEstimate(
            flops=int(WEIGHT * flops), bytes_accessed=int(WEIGHT * nbytes), transcendentals=0
        ),
        name=name,
    )


def partner(index, count, swap):
    other = index ^ 1 if swap == 0 else ((index + 1) ^ 1) - 1
    return other if 0 <= other < count else index


def swaps_of(count):
    return {1: [], 2: [0]}.get(count, [0, 1])


def meets_next(index, swap):
    return lax.rem(index + swap, 2) == 0


def has_partner(index, count, swap):
    after = meets_next(index, swap)
    return jnp.where(after, index < count - 1, index > 0)


def links_of(count_x, count_z):
    along_x, along_z = [None, *swaps_of(count_x)], [None, *swaps_of(count_z)]
    return [(x, z) for x in along_x for z in along_z if (x, z) != (None, None)]


def exchange(cells, link, count_x, count_z):
    x, z = link
    pairs = []
    for i in range(count_x):
        for j in range(count_z):
            to_x = i if x is None else partner(i, count_x, x)
            to_z = j if z is None else partner(j, count_z, z)
            pairs.append((i * count_z + j, to_x * count_z + to_z))
    return lax.ppermute(cells, ("bx", "bz"), pairs)


def exchange_y(first, second):
    count = lax.axis_size("by")
    return [
        lax.ppermute(cells, "by", [(i, partner(i, count, swap)) for i in range(count)])
        for swap, cells in enumerate((first, second))
    ]


def banded(offset, tap_of):
    matrix = jnp.zeros(offset.shape, F32)
    for tap in range(TAPS):
        matrix = jnp.where(offset == tap, tap_of(tap), matrix)
    return matrix


def halves(matrix):
    high = matrix.astype(BF16)
    return high, (matrix - high.astype(F32)).astype(BF16)


def packed(cells, begin):
    by = cells.shape[1]
    row = lax.broadcasted_iota(jnp.int32, (PAD, by), 0)
    col = lax.broadcasted_iota(jnp.int32, (PAD, by), 1)
    pick = jnp.where(col == row + begin, 1.0, 0.0).astype(BF16)
    return lax.dot_general(
        pick, cells, (((1,), (1,)), ((), ())), preferred_element_type=F32
    ).astype(BF16)


def pack_both(cells, by, first_ref, second_ref):
    last = by - PAD
    mine = lax.axis_index("by")
    first_ref[...] = packed(cells, jnp.where(meets_next(mine, 0), last, 0))
    second_ref[...] = packed(cells, jnp.where(meets_next(mine, 1), last, 0))


def unpack_both(count, first_ref, second_ref):
    mine = lax.axis_index("by")
    first, second = first_ref[...].astype(F32), second_ref[...].astype(F32)
    even = meets_next(mine, 0)
    before = jnp.where(even, second, first)
    after = jnp.where(even, first, second)
    before = jnp.where(mine > 0, before, 0.0)
    after = jnp.where(mine < count - 1, after, 0.0)
    return jnp.concatenate([before, after], axis=0).T.astype(BF16)


def columns_body(rec_ref, est_ref, cells_ref, first_ref, second_ref):
    bz, bx, by = est_ref.shape
    cells_ref[...] = est_ref[...].astype(BF16)
    pack_both(cells_ref[...].reshape(bz * bx, by), by, first_ref, second_ref)


def pieces_body(order_ref, rec_ref, *out_refs):
    by = out_refs[0].shape[3]
    for other, out_ref in enumerate(out_refs):
        at = pl.ds(pl.multiple_of((lax.axis_index("by") ^ other) * by, by), by)
        out_ref[...] = rec_ref[:, :, :, at]


def upright(cells):
    return cells.astype(F32).T


def lying(cells):
    wide = cells.shape[1]
    row = lax.broadcasted_iota(jnp.int32, (wide, wide), 0)
    col = lax.broadcasted_iota(jnp.int32, (wide, wide), 1)
    same = jnp.where(row == col, 1.0, 0.0).astype(BF16)
    return lax.dot_general(
        same, cells.astype(BF16), (((1,), (1,)), ((), ())), preferred_element_type=F32
    )


def edges_body(count, est_ref, first_ref, second_ref, halo_ref, *out_refs):
    bz, bx, by = est_ref.shape
    halo_ref[...] = unpack_both(count, first_ref, second_ref)
    for swap, out_ref in enumerate(out_refs):
        begin = jnp.where(meets_next(lax.axis_index("bz"), swap), bz - PAD, 0)
        out_ref[:PAD] = est_ref[pl.ds(begin, PAD)]
        rows = halo_ref[pl.ds(pl.multiple_of(begin * bx, PAD * bx), PAD * bx), :]
        flat = lying(rows).astype(BF16)
        for i in range(PAD * bx // by):
            out_ref[PAD, 2 * PAD * i : 2 * PAD * (i + 1), :] = flat[:, i * by : (i + 1) * by]


def deep_body(counts, count_z, order_ref, est_ref, halo_ref, *refs):
    bz, bx, by = est_ref.shape
    deep = bz + 2 * PAD
    z_refs, (cells_ref, halos_ref, *out_refs) = refs[:count_z], refs[count_z:]
    cells_ref[...] = jnp.zeros_like(cells_ref)
    halos_ref[...] = jnp.zeros_like(halos_ref)
    cells_ref[PAD : PAD + bz] = est_ref[...].astype(F32)
    halos_ref[PAD : PAD + bz] = halo_ref[...].astype(F32).reshape(bz, bx, 2 * PAD)
    for swap, z_ref in enumerate(z_refs):
        index = lax.axis_index("bz")
        at = pl.ds(jnp.where(meets_next(index, swap), PAD + bz, 0), PAD)

        @pl.when(has_partner(index, counts[1], swap))
        def _():
            cells_ref[at] = z_ref[:PAD].astype(F32)
            flat = jnp.concatenate(
                [z_ref[PAD, 2 * PAD * i : 2 * PAD * (i + 1), :] for i in range(PAD * bx // by)], axis=1
            )
            halos_ref[at] = upright(flat).reshape(PAD, bx, 2 * PAD)

    for swap, out_ref in enumerate(out_refs):
        begin = jnp.where(meets_next(lax.axis_index("bx"), swap), bx - PAD, 0)
        at = pl.ds(pl.multiple_of(begin, PAD), PAD)
        out_ref[:deep] = cells_ref[:, at, :].astype(BF16)
        flat = lying(halos_ref[:, at, :].reshape(deep * PAD, 2 * PAD))
        for i in range(deep * PAD // by):
            part = flat[:, i * by : (i + 1) * by]
            out_ref[deep + 2 * i] = part[:PAD].astype(BF16)
            out_ref[deep + 2 * i + 1] = part[PAD:].astype(BF16)


def bands_body(views, order_ref, prof_ref, box_ref, est_ref, yf_ref, yr_ref, xf_ref, xr_ref, share_ref):
    bz, bx, by = est_ref.shape
    ext = bx + 2 * PAD
    start_z = lax.axis_index("bz") * bz
    start_x = lax.axis_index("bx") * bx
    start_y = lax.axis_index("by") * by

    def iota(shape, dim):
        return lax.broadcasted_iota(jnp.int32, shape, dim)

    shape_y = (by + 2 * PAD, by)
    row = iota(shape_y, 0)
    source = jnp.where(row < by, row, jnp.where(row < by + PAD, row - by - PAD, row - PAD))
    target = iota(shape_y, 1)
    shape_x = (bx, 2 * ext)
    col = iota(shape_x, 1)
    is_low = col >= ext
    forward_x = jnp.where(is_low, col - ext, col) - PAD - iota(shape_x, 0)

    def view(k, carry):
        forward = banded(source - target + REACH, lambda tap: prof_ref[k, 2, tap])
        high, low = halves(forward)
        yf_ref[k, :, :by] = high
        yf_ref[k, :, by:] = low
        back = banded(REACH - source + target, lambda tap: prof_ref[k, 2, tap])
        within = (target >= box_ref[k, 4] - start_y) & (target < box_ref[k, 5] - start_y)
        high, low = halves(jnp.where(within, back, 0.0))
        yr_ref[k, :, :by] = high
        yr_ref[k, :, by:] = low
        high, low = halves(banded(forward_x + REACH, lambda tap: prof_ref[k, 1, tap]))
        at = pl.ds(pl.multiple_of(k * bx, bx), bx)
        xf_ref[at, :] = jnp.where(is_low, low.astype(F32), high.astype(F32)).astype(BF16)
        return carry

    lax.fori_loop(0, views, view, 0)

    shape_x = (ext, views * bx)
    target = iota(shape_x, 0) - PAD
    col = iota(shape_x, 1)

    def back_view(k, matrix):
        source = col - k * bx
        back = banded(REACH - source + target, lambda tap: prof_ref[k, 1, tap])
        within = (source >= 0) & (source < bx)
        within = within & (target >= box_ref[k, 2] - start_x) & (target < box_ref[k, 3] - start_x)
        return jnp.where(within, back, matrix)

    high, low = halves(lax.fori_loop(0, views, back_view, jnp.zeros(shape_x, F32)))
    xr_ref[:ext] = high
    xr_ref[ext:] = low

    row_x = iota((bx, by), 0) + start_x
    col_y = iota((bx, by), 1) + start_y
    flat = []
    for k in range(views):
        within = (col_y >= box_ref[k, 4]) & (col_y < box_ref[k, 5])
        within = within & (row_x >= box_ref[k, 2]) & (row_x < box_ref[k, 3])
        flat.append(jnp.where(within, 1.0, 0.0))
    for plane in range(bz):
        coverage = jnp.zeros((bx, by), F32)
        for k in range(views):
            at = plane + start_z
            here = (at >= box_ref[k, 0]) & (at < box_ref[k, 1])
            coverage = coverage + jnp.where(here, 1.0, 0.0) * flat[k]
        share_ref[plane] = est_ref[plane] / coverage


def forward_body(views, block, counts, count_x, prof_ref, box_ref, cells_ref, halos_ref, yf_ref, xf_ref, *refs):
    x_refs, (gain_ref, side_halo, blurred_x, rows) = refs[:count_x], refs[count_x:]
    bz, bx, by = block
    deep = bz + 2 * PAD
    sides = []
    for swap, x_ref in enumerate(x_refs):
        index = lax.axis_index("bx")
        known = has_partner(index, counts[0], swap)
        after = meets_next(index, swap)
        sides.append((known & jnp.logical_not(after), known & after))
        flat = [
            jnp.concatenate([x_ref[deep + 2 * i].astype(F32), x_ref[deep + 2 * i + 1].astype(F32)], axis=0)
            for i in range(deep * PAD // by)
        ]
        side_halo[swap] = jnp.concatenate(flat, axis=1).T.reshape(deep, PAD, 2 * PAD)
    for plane in range(1, deep - 1):
        left = right = jnp.zeros((PAD, by), F32)
        left_halo = right_halo = jnp.zeros((PAD, 2 * PAD), F32)
        for swap, (is_left, is_right) in enumerate(sides):
            came, came_halo = x_refs[swap][plane].astype(F32), side_halo[swap, plane]
            left = jnp.where(is_left, came, left)
            right = jnp.where(is_right, came, right)
            left_halo = jnp.where(is_left, came_halo, left_halo)
            right_halo = jnp.where(is_right, came_halo, right_halo)
        cells = jnp.concatenate([left, cells_ref[plane], right], axis=0).astype(BF16)
        halo = jnp.concatenate([left_halo, halos_ref[plane], right_halo], axis=0).astype(BF16)
        cells = jnp.concatenate([cells, halo], axis=1)
        cells = jnp.concatenate([cells, cells], axis=0)
        mixed = jnp.dot(xf_ref[...], cells, preferred_element_type=F32).astype(BF16)
        for k in range(views):
            blurred_x[k, plane * bx : (plane + 1) * bx, :] = mixed[k * bx : (k + 1) * bx]
    row_x = lax.broadcasted_iota(jnp.int32, (8, by), 0) + lax.axis_index("bx") * bx
    col_y = lax.broadcasted_iota(jnp.int32, (8, by), 1) + lax.axis_index("by") * by
    start_z = lax.axis_index("bz") * bz
    step = 10

    def view(k, carry):
        along_y = yf_ref[k]
        for first in range(1, deep - 1, step):
            mixed = jnp.dot(
                blurred_x[k, first * bx : (first + step) * bx, :], along_y, preferred_element_type=F32
            )
            rows[first : first + step] = (mixed[:, :by] + mixed[:, by:]).reshape(step, bx, by)
        taps = [prof_ref[k, 0, tap] for tap in range(TAPS)]
        within_y = (col_y >= box_ref[k, 4]) & (col_y < box_ref[k, 5])
        inside = []
        for tile in range(0, bx, 8):
            at = row_x + tile
            inside.append(jnp.where(within_y & (at >= box_ref[k, 2]) & (at < box_ref[k, 3]), 1.0, 0.0))
        gain_ref[k] = jnp.zeros((bz, bx, by), F32)

        def plane_of(plane, carry):
            for tile in range(0, bx, 8):
                total = taps[0] * rows[plane + 1, tile : tile + 8, :]
                for tap in range(1, TAPS):
                    total = total + taps[tap] * rows[plane + 1 + tap, tile : tile + 8, :]
                gain_ref[k, plane, tile : tile + 8, :] = inside[tile // 8] / (total + BACKGROUND)
            return carry

        begin = jnp.clip(box_ref[k, 0] - start_z, 0, bz)
        end = jnp.clip(box_ref[k, 1] - start_z, 0, bz)
        lax.fori_loop(begin, end, plane_of, 0)
        return carry

    lax.fori_loop(0, views, view, 0)


def quotient_body(views, block, count, gain_ref, *refs):
    parts = refs[:count]
    quot_ref, first_ref, second_ref, held = refs[count:]
    bz, bx, by = block
    rows = bx // count
    mine = lax.axis_index("by") if count > 1 else 0

    def view(k, carry):
        for part, part_ref in enumerate(parts):
            at = pl.ds(pl.multiple_of((mine ^ part) * rows, rows), rows)
            held[:, at, :] = gain_ref[k, :, at, :] * part_ref[k].astype(F32)
        quot_ref[k] = held[...].astype(BF16)
        return carry

    lax.fori_loop(0, views, view, 0)
    pack_both(quot_ref[...].reshape(views * bz * bx, by), by, first_ref, second_ref)


def return_body(views, block, count, counts, links, prof_ref, box_ref, quot_ref, first_ref, second_ref, yr_ref, xr_ref, mid_ref, *refs):
    bz, bx, by = block
    ext = bx + 2 * PAD
    deep = bz + 2 * REACH
    link_refs = refs[: len(links)]
    halo, rows, high_rows, low_rows, total = refs[len(links) :]
    halo[...] = unpack_both(count, first_ref, second_ref)
    start_z = lax.axis_index("bz") * bz

    def view(k, carry):
        start = pl.multiple_of(k * (bz * bx), bz * bx)
        cells = quot_ref[k].reshape(bz * bx, by)
        cells = jnp.concatenate([cells, halo[pl.ds(start, bz * bx), :]], axis=1)
        mixed = jnp.dot(cells, yr_ref[k], preferred_element_type=F32)
        rows[...] = (mixed[:, :by] + mixed[:, by:]).reshape(bz, bx, by)
        taps = [prof_ref[k, 0, tap] for tap in range(TAPS)]
        at = pl.ds(pl.multiple_of(k * bx, bx), bx)
        for out in range(deep):
            plane = out - REACH
            here = (plane + start_z >= box_ref[k, 0]) & (plane + start_z < box_ref[k, 1])

            @pl.when(here)
            def _():
                sums = []
                for tile in range(0, bx, 8):
                    part = None
                    for source in range(max(0, plane - REACH), min(bz, plane + REACH + 1)):
                        term = taps[REACH - source + plane] * rows[source, tile : tile + 8, :]
                        part = term if part is None else part + term
                    sums.append(part)
                high, low = halves(jnp.concatenate(sums, axis=0))
                high_rows[out, at, :] = high
                low_rows[out, at, :] = low

            @pl.when(jnp.logical_not(here))
            def _():
                high_rows[out, at, :] = jnp.zeros((bx, by), BF16)
                low_rows[out, at, :] = jnp.zeros((bx, by), BF16)

        return carry

    lax.fori_loop(0, views, view, 0)
    for out in range(0, deep, 2):
        high = jnp.concatenate([high_rows[out], high_rows[out + 1]], axis=1)
        low = jnp.concatenate([low_rows[out], low_rows[out + 1]], axis=1)
        mixed = jnp.dot(xr_ref[...], high, preferred_element_type=F32)
        mixed = mixed[:ext] + mixed[ext:] + jnp.dot(xr_ref[:ext], low, preferred_element_type=F32)
        total[out] = mixed[:, :by]
        total[out + 1] = mixed[:, by:]
    mid_ref[...] = total[REACH : REACH + bz, PAD : PAD + bx, :]
    for (x, z), link_ref in zip(links, link_refs):
        at_x, at_z = slice(PAD, PAD + bx), slice(REACH, REACH + bz)
        if x is not None:
            begin = jnp.where(meets_next(lax.axis_index("bx"), x), PAD + bx, 0)
            at_x = pl.ds(pl.multiple_of(begin, PAD), PAD)
        if z is not None:
            at_z = pl.ds(jnp.where(meets_next(lax.axis_index("bz"), z), REACH + bz, 0), REACH)
        link_ref[...] = total[at_z, at_x, :]


def finish_body(counts, links, share_ref, mid_ref, *refs):
    bz, bx, by = share_ref.shape
    link_refs, out_ref = refs[: len(links)], refs[len(links)]
    out_ref[...] = share_ref[...] * mid_ref[...]
    for (x, z), link_ref in zip(links, link_refs):
        at_x, at_z, known = slice(None), slice(None), None
        if x is not None:
            index = lax.axis_index("bx")
            begin = jnp.where(meets_next(index, x), bx - PAD, 0)
            at_x = pl.ds(pl.multiple_of(begin, PAD), PAD)
            known = has_partner(index, counts[0], x)
        if z is not None:
            index = lax.axis_index("bz")
            at_z = pl.ds(jnp.where(meets_next(index, z), bz - REACH, 0), REACH)
            there = has_partner(index, counts[1], z)
            known = there if known is None else known & there

        @pl.when(known)
        def _():
            out_ref[at_z, at_x, :] = out_ref[at_z, at_x, :] + share_ref[at_z, at_x, :] * link_ref[...]


def local(estimate, recorded, profiles, view_boxes):
    block = estimate.shape
    bz, bx, by = block
    views = recorded.shape[0]
    part_rows = recorded.shape[2]
    count = lax.axis_size("by")
    counts = (lax.axis_size("bx"), lax.axis_size("bz"))
    links = links_of(*counts)
    ext = bx + 2 * PAD
    deep = bz + 2 * PAD
    shape = jax.ShapeDtypeStruct

    def link_shape(link, reach, dtype):
        x, z = link
        return shape((bz if z is None else reach, bx if x is None else PAD, by), dtype)

    side = shape((PAD, bz * bx), BF16)
    own, order, second = call(
        columns_body,
        [shape(block, BF16), side, side],
        [ANY, VMEM],
        nbytes=bz * bx * by * 4,
        name="columns",
    )(recorded, estimate)
    first, second = exchange_y(order, second)

    if count & (count - 1) == 0 and count <= 4 and part_rows % 8 == 0:
        parts = [*call(
            pieces_body,
            [shape((views, bz, part_rows, by), BF16)] * count,
            [ANY, VMEM],
            nbytes=views * bz * bx * by * 4,
            name="pieces",
        )(order, recorded)]
        for other in range(1, count):
            parts[other] = lax.ppermute(parts[other], "by", [(i, i ^ other) for i in range(count)])
    else:
        parts = [lax.all_to_all(recorded, "by", split_axis=3, concat_axis=2, tiled=True)]

    along_x, along_z = swaps_of(counts[0]), swaps_of(counts[1])
    halo, *edges = call(
        functools.partial(edges_body, count),
        [shape((bz * bx, 2 * PAD), BF16)] + [shape((PAD + 1, bx, by), BF16)] * len(along_z),
        [VMEM] * 3,
        nbytes=bz * bx * by * 4,
        name="edges",
    )(own, first, second)
    edges = [exchange(cells, (None, swap), *counts) for swap, cells in zip(along_z, edges)]

    cells, halos, *edges = call(
        functools.partial(deep_body, counts, len(along_z)),
        [shape((deep, bx, by), F32), shape((deep, bx, 2 * PAD), F32)]
        + [shape((deep + 2 * deep * PAD // by, PAD, by), BF16)] * len(along_x),
        [ANY] + [VMEM] * (2 + len(along_z)),
        nbytes=deep * bx * by * 4,
        name="deep",
    )(own, own, halo, *edges)
    edges = [exchange(cells, (swap, None), *counts) for swap, cells in zip(along_x, edges)]

    yf, yr, xf, xr, share = call(
        functools.partial(bands_body, views),
        [
            shape((views, by + 2 * PAD, 2 * by), BF16),
            shape((views, by + 2 * PAD, 2 * by), BF16),
            shape((views * bx, 2 * ext), BF16),
            shape((2 * ext, views * bx), BF16),
            shape(block, F32),
        ],
        [ANY] + [SMEM] * 2 + [VMEM],
        flops=views * 64 * by * by,
        nbytes=views * by * by * 8,
        name="bands",
    )(order, profiles, view_boxes, estimate)

    gain = call(
        functools.partial(forward_body, views, block, counts, len(along_x)),
        shape((views, bz, bx, by), F32),
        [SMEM] * 2 + [VMEM] * (4 + len(along_x)),
        [
            pltpu.VMEM((max(1, len(along_x)), deep, PAD, 2 * PAD), F32),
            pltpu.VMEM((views, deep * bx, by + 2 * PAD), BF16),
            pltpu.VMEM((deep, bx, by), F32),
        ],
        flops=views * deep * ext * by * 600,
        nbytes=views * bz * bx * by * 8,
        name="forward",
    )(profiles, view_boxes, cells, halos, yf, xf, *edges)

    side = shape((PAD, views * bz * bx), BF16)
    quot, first, second = call(
        functools.partial(quotient_body, views, block, len(parts)),
        [shape((views, bz, bx, by), BF16), side, side],
        [VMEM] * (1 + len(parts)),
        [pltpu.VMEM((bz, bx, by), F32)],
        flops=views * bz * bx * by * 40,
        nbytes=views * bz * bx * by * 8,
        name="quotient",
    )(gain, *parts)
    first, second = exchange_y(first, second)

    mid, *sums = call(
        functools.partial(return_body, views, block, count, counts, links),
        [shape(block, F32)] + [link_shape(link, REACH, F32) for link in links],
        [SMEM] * 2 + [VMEM] * 5,
        [
            pltpu.VMEM((views * bz * bx, 2 * PAD), BF16),
            pltpu.VMEM((bz, bx, by), F32),
            pltpu.VMEM((bz + 2 * REACH, views * bx, by), BF16),
            pltpu.VMEM((bz + 2 * REACH, views * bx, by), BF16),
            pltpu.VMEM((bz + 2 * REACH, ext, by), F32),
        ],
        flops=views * bz * ext * by * 600,
        nbytes=views * bz * bx * by * 8,
        name="returned",
    )(profiles, view_boxes, quot, first, second, yr, xr)
    sums = [exchange(cells, link, *counts) for link, cells in zip(links, sums)]
    return call(
        functools.partial(finish_body, counts, links),
        shape(block, F32),
        [VMEM] * (2 + len(links)),
        nbytes=bz * bx * by * 12,
        name="finish",
    )(share, mid, *sums)


def solution(mesh):
    placed = (
        P(("groups", "bz"), "bx", "by"),
        P(None, ("groups", "bz"), ("bx", "by"), None),
        P(),
        P("groups", None),
    )
    return jax.shard_map(
        local,
        mesh=mesh,
        in_specs=placed,
        out_specs=P(("groups", "bz"), "bx", "by"),
        check_vma=False,
    )
```

```python
import functools

import jax
import jax.numpy as jnp
from jax import lax
from jax.experimental import pallas as pl
from jax.experimental.pallas import tpu as pltpu
from jax.sharding import PartitionSpec as P

TAPS = 15
REACH = TAPS // 2
PAD = 8
SIDE = 2 * PAD
BACKGROUND = 0.05
WEIGHT = 0.8

F32 = jnp.float32
BF16 = jnp.bfloat16

VMEM = pl.BlockSpec(memory_space=pltpu.VMEM)
SMEM = pl.BlockSpec(memory_space=pltpu.SMEM)
ANY = pl.BlockSpec(memory_space=pl.ANY)
HBM = pl.BlockSpec(memory_space=pltpu.HBM)


def call(body, out_shape, in_specs, scratch=(), flops=0, nbytes=0, name=None):
    many = isinstance(out_shape, (list, tuple))
    return pl.pallas_call(
        body,
        out_shape=out_shape,
        in_specs=in_specs,
        out_specs=[VMEM] * len(out_shape) if many else VMEM,
        scratch_shapes=list(scratch),
        compiler_params=pltpu.CompilerParams(vmem_limit_bytes=40 * 1024 * 1024),
        cost_estimate=pl.CostEstimate(
            flops=int(WEIGHT * flops), bytes_accessed=int(WEIGHT * nbytes), transcendentals=0
        ),
        name=name,
    )


def partner(index, count, swap):
    other = index ^ 1 if swap == 0 else ((index + 1) ^ 1) - 1
    return other if 0 <= other < count else index


def swaps_of(count):
    return {1: [], 2: [0]}.get(count, [0, 1])


def meets_next(index, swap):
    return lax.rem(index + swap, 2) == 0


def has_partner(index, count, swap):
    after = meets_next(index, swap)
    return jnp.where(after, index < count - 1, index > 0)


def links_of(count_x, count_z):
    along_x, along_z = [None, *swaps_of(count_x)], [None, *swaps_of(count_z)]
    return [(x, z) for x in along_x for z in along_z if (x, z) != (None, None)]


def exchange(cells, link, count_x, count_z):
    x, z = link
    pairs = []
    for i in range(count_x):
        for j in range(count_z):
            to_x = i if x is None else partner(i, count_x, x)
            to_z = j if z is None else partner(j, count_z, z)
            pairs.append((i * count_z + j, to_x * count_z + to_z))
    return lax.ppermute(cells, ("bx", "bz"), pairs)


def exchange_y(first, second):
    count = lax.axis_size("by")
    return [
        lax.ppermute(cells, "by", [(i, partner(i, count, swap)) for i in range(count)])
        for swap, cells in enumerate((first, second))
    ]


def banded(offset, tap_of):
    matrix = jnp.zeros(offset.shape, F32)
    for tap in range(TAPS):
        matrix = jnp.where(offset == tap, tap_of(tap), matrix)
    return matrix


def halves(matrix):
    high = matrix.astype(BF16)
    return high, (matrix - high.astype(F32)).astype(BF16)


def packed(cells, begin):
    by = cells.shape[1]
    row = lax.broadcasted_iota(jnp.int32, (SIDE, by), 0)
    col = lax.broadcasted_iota(jnp.int32, (SIDE, by), 1)
    pick = jnp.where(col == row + begin, 1.0, 0.0).astype(BF16)
    return lax.dot_general(
        pick, cells, (((1,), (1,)), ((), ())), preferred_element_type=F32
    ).astype(BF16)


def unpack_both(count, first_ref, second_ref):
    mine = lax.axis_index("by")
    first, second = first_ref[...].astype(F32), second_ref[...].astype(F32)
    even = meets_next(mine, 0)
    before = jnp.where(even, second, first)
    after = jnp.where(even, first, second)
    before = jnp.where(mine > 0, before, 0.0)
    after = jnp.where(mine < count - 1, after, 0.0)
    return jnp.concatenate([before, after], axis=0).T.astype(BF16)


def columns_body(rec_ref, est_ref, cells_ref, first_ref, second_ref):
    bz, bx, by = est_ref.shape
    cells_ref[...] = est_ref[...].astype(BF16)
    cells = cells_ref[...].reshape(bz * bx, by)
    mine = lax.axis_index("by")
    first_ref[...] = packed(cells, jnp.where(meets_next(mine, 0), by - SIDE, 0))
    second_ref[...] = packed(cells, jnp.where(meets_next(mine, 1), by - SIDE, 0))


def pieces_body(order_ref, rec_ref, *out_refs):
    views, bz, rows, width = rec_ref.shape
    count = len(out_refs)
    by = width // count
    row = lax.broadcasted_iota(jnp.int32, (by, by), 0)
    col = lax.broadcasted_iota(jnp.int32, (by, by), 1)
    picks = []
    for k in range(views):
        lane = col - 2 * PAD * k
        picks.append((lane >= 0) & (lane < PAD) & (row == by - PAD + lane))
        picks.append((lane >= PAD) & (lane < 2 * PAD) & (row == lane - PAD))
    picks = jnp.concatenate([jnp.where(pick, 1.0, 0.0).astype(BF16) for pick in picks], axis=0)
    for other, out_ref in enumerate(out_refs):
        target = lax.axis_index("by") ^ other

        def columns(tile):
            return pl.ds(pl.multiple_of(jnp.clip(tile, 0, count - 1) * by, by), by)

        out_ref[:views] = rec_ref[:, :, :, columns(target)]
        beside = []
        for k in range(views):
            for tile in (target - 1, target + 1):
                cells = rec_ref[k, :, :, columns(tile)]
                beside.append(cells.astype(F32).reshape(bz * rows, by).astype(BF16))
        beside = jnp.dot(jnp.concatenate(beside, axis=1), picks, preferred_element_type=F32)
        out_ref[views] = beside.reshape(bz, rows, by).astype(BF16)


def upright(cells):
    return cells.astype(F32).T


def lying(cells):
    wide = cells.shape[1]
    row = lax.broadcasted_iota(jnp.int32, (wide, wide), 0)
    col = lax.broadcasted_iota(jnp.int32, (wide, wide), 1)
    same = jnp.where(row == col, 1.0, 0.0).astype(BF16)
    return lax.dot_general(
        same, cells.astype(BF16), (((1,), (1,)), ((), ())), preferred_element_type=F32
    )


def edges_body(count, est_ref, first_ref, second_ref, halo_ref, *out_refs):
    bz, bx, by = est_ref.shape
    halo_ref[...] = unpack_both(count, first_ref, second_ref)
    for swap, out_ref in enumerate(out_refs):
        begin = jnp.where(meets_next(lax.axis_index("bz"), swap), bz - PAD, 0)
        out_ref[:PAD] = est_ref[pl.ds(begin, PAD)]
        rows = halo_ref[pl.ds(pl.multiple_of(begin * bx, PAD * bx), PAD * bx), :]
        flat = lying(rows).astype(BF16)
        for i in range(PAD * bx // by):
            out_ref[PAD + i, : 2 * SIDE, :] = flat[:, i * by : (i + 1) * by]


def deep_body(counts, count_z, order_ref, est_ref, halo_ref, *refs):
    bz, bx, by = est_ref.shape
    deep = bz + 2 * PAD
    z_refs, (cells_ref, halos_ref, *out_refs) = refs[:count_z], refs[count_z:]
    cells_ref[...] = jnp.zeros_like(cells_ref)
    halos_ref[...] = jnp.zeros_like(halos_ref)
    cells_ref[PAD : PAD + bz] = est_ref[...].astype(F32)
    halos_ref[PAD : PAD + bz] = halo_ref[...].astype(F32).reshape(bz, bx, 2 * SIDE)
    for swap, z_ref in enumerate(z_refs):
        index = lax.axis_index("bz")
        at = pl.ds(jnp.where(meets_next(index, swap), PAD + bz, 0), PAD)

        @pl.when(has_partner(index, counts[1], swap))
        def _():
            cells_ref[at] = z_ref[:PAD].astype(F32)
            flat = jnp.concatenate(
                [z_ref[PAD + i, : 2 * SIDE, :] for i in range(PAD * bx // by)], axis=1
            )
            halos_ref[at] = upright(flat).reshape(PAD, bx, 2 * SIDE)

    for swap, out_ref in enumerate(out_refs):
        begin = jnp.where(meets_next(lax.axis_index("bx"), swap), bx - PAD, 0)
        at = pl.ds(pl.multiple_of(begin, PAD), PAD)
        out_ref[:deep] = cells_ref[:, at, :].astype(BF16)
        flat = lying(halos_ref[:, at, :].reshape(deep * PAD, 2 * SIDE))
        groups = 2 * SIDE // PAD
        for i in range(deep * PAD // by):
            for j in range(groups):
                part = flat[j * PAD : (j + 1) * PAD, i * by : (i + 1) * by]
                out_ref[deep + groups * i + j] = part.astype(BF16)


def bands_body(views, order_ref, prof_ref, box_ref, est_ref, yf_ref, yh_ref, yr_ref, xf_ref, xr_ref, share_ref):
    bz, bx, by = est_ref.shape
    ext = bx + 2 * PAD
    start_z = lax.axis_index("bz") * bz
    start_x = lax.axis_index("bx") * bx
    start_y = lax.axis_index("by") * by

    def iota(shape, dim):
        return lax.broadcasted_iota(jnp.int32, shape, dim)

    shape_y = (by + 2 * SIDE, by)
    row = iota(shape_y, 0)
    source = jnp.where(row < by, row, jnp.where(row < by + SIDE, row - by - SIDE, row - SIDE))
    target = iota(shape_y, 1)
    beside_view = lax.div(target, 2 * PAD)
    beside = lax.rem(target, 2 * PAD)
    beside = jnp.where(beside < PAD, beside - PAD, by + beside - PAD)
    back_row, back_target = iota((by, by), 0), iota((by, by), 1)
    side_row, side_target = iota((2 * PAD, by), 0), iota((2 * PAD, by), 1)
    side_row = jnp.where(side_row < PAD, side_row - PAD, by + side_row - PAD)
    shape_x = (bx, 2 * ext)
    col = iota(shape_x, 1)
    is_low = col >= ext
    forward_x = jnp.where(is_low, col - ext, col) - PAD - iota(shape_x, 0)

    def view(k, carry):
        forward = banded(source - target + REACH, lambda tap: prof_ref[k, 2, tap])
        high, low = halves(forward)
        yf_ref[k, :, :by] = high
        yf_ref[k, :, by:] = low
        forward = banded(source - beside + REACH, lambda tap: prof_ref[k, 2, tap])
        high, low = halves(jnp.where(beside_view == k, forward, 0.0))
        yh_ref[k, :, :by] = high
        yh_ref[k, :, by:] = low

        def back(row, target):
            within = (target >= box_ref[k, 4] - start_y) & (target < box_ref[k, 5] - start_y)
            matrix = banded(REACH - row + target, lambda tap: prof_ref[k, 2, tap])
            return halves(jnp.where(within, matrix, 0.0))

        high, low = back(back_row, back_target)
        yr_ref[k, :by, :by] = high
        yr_ref[k, :by, by:] = low
        yr_ref[k, by:, :] = jnp.zeros((by, 2 * by), BF16)
        at = pl.ds(pl.multiple_of(by + 2 * PAD * k, 2 * PAD), 2 * PAD)
        high, low = back(side_row, side_target)
        yr_ref[k, at, :by] = high
        yr_ref[k, at, by:] = low
        high, low = halves(banded(forward_x + REACH, lambda tap: prof_ref[k, 1, tap]))
        at = pl.ds(pl.multiple_of(k * bx, bx), bx)
        xf_ref[at, :] = jnp.where(is_low, low.astype(F32), high.astype(F32)).astype(BF16)
        return carry

    lax.fori_loop(0, views, view, 0)

    shape_x = (ext, views * bx)
    target = iota(shape_x, 0) - PAD
    col = iota(shape_x, 1)

    def back_view(k, matrix):
        source = col - k * bx
        back = banded(REACH - source + target, lambda tap: prof_ref[k, 1, tap])
        within = (source >= 0) & (source < bx)
        within = within & (target >= box_ref[k, 2] - start_x) & (target < box_ref[k, 3] - start_x)
        return jnp.where(within, back, matrix)

    high, low = halves(lax.fori_loop(0, views, back_view, jnp.zeros(shape_x, F32)))
    xr_ref[:ext] = high
    xr_ref[ext:] = low

    row_x = iota((bx, by), 0) + start_x
    col_y = iota((bx, by), 1) + start_y
    flat = []
    for k in range(views):
        within = (col_y >= box_ref[k, 4]) & (col_y < box_ref[k, 5])
        within = within & (row_x >= box_ref[k, 2]) & (row_x < box_ref[k, 3])
        flat.append(jnp.where(within, 1.0, 0.0))
    for plane in range(bz):
        coverage = jnp.zeros((bx, by), F32)
        for k in range(views):
            at = plane + start_z
            here = (at >= box_ref[k, 0]) & (at < box_ref[k, 1])
            coverage = coverage + jnp.where(here, 1.0, 0.0) * flat[k]
        share_ref[plane] = est_ref[plane] / coverage


def forward_body(views, block, counts, count_x, prof_ref, box_ref, cells_ref, halos_ref, yf_ref, yh_ref, xf_ref, *refs):
    x_refs, (gain_ref, side_halo, blurred_x, rows) = refs[:count_x], refs[count_x:]
    bz, bx, by = block
    deep = bz + 2 * PAD
    sides = []
    for swap, x_ref in enumerate(x_refs):
        index = lax.axis_index("bx")
        known = has_partner(index, counts[0], swap)
        after = meets_next(index, swap)
        sides.append((known & jnp.logical_not(after), known & after))
        groups = 2 * SIDE // PAD
        flat = [
            jnp.concatenate([x_ref[deep + groups * i + j].astype(F32) for j in range(groups)], axis=0)
            for i in range(deep * PAD // by)
        ]
        side_halo[swap] = jnp.concatenate(flat, axis=1).T.reshape(deep, PAD, 2 * SIDE)
    for plane in range(1, deep - 1):
        left = right = jnp.zeros((PAD, by), F32)
        left_halo = right_halo = jnp.zeros((PAD, 2 * SIDE), F32)
        for swap, (is_left, is_right) in enumerate(sides):
            came, came_halo = x_refs[swap][plane].astype(F32), side_halo[swap, plane]
            left = jnp.where(is_left, came, left)
            right = jnp.where(is_right, came, right)
            left_halo = jnp.where(is_left, came_halo, left_halo)
            right_halo = jnp.where(is_right, came_halo, right_halo)
        cells = jnp.concatenate([left, cells_ref[plane], right], axis=0).astype(BF16)
        halo = jnp.concatenate([left_halo, halos_ref[plane], right_halo], axis=0).astype(BF16)
        cells = jnp.concatenate([cells, halo], axis=1)
        cells = jnp.concatenate([cells, cells], axis=0)
        mixed = jnp.dot(xf_ref[...], cells, preferred_element_type=F32).astype(BF16)
        for k in range(views):
            blurred_x[k, plane * bx : (plane + 1) * bx, :] = mixed[k * bx : (k + 1) * bx]
    row_x = lax.broadcasted_iota(jnp.int32, (8, by), 0) + lax.axis_index("bx") * bx
    col_y = lax.broadcasted_iota(jnp.int32, (8, by), 1) + lax.axis_index("by") * by
    start_z = lax.axis_index("bz") * bz
    step = 10

    def view(k, carry):
        along_y = yf_ref[k]
        for first in range(1, deep - 1, step):
            mixed = jnp.dot(
                blurred_x[k, first * bx : (first + step) * bx, :], along_y, preferred_element_type=F32
            )
            rows[first : first + step] = (mixed[:, :by] + mixed[:, by:]).reshape(step, bx, by)
        taps = [prof_ref[k, 0, tap] for tap in range(TAPS)]
        within_y = (col_y >= box_ref[k, 4]) & (col_y < box_ref[k, 5])
        inside = []
        for tile in range(0, bx, 8):
            at = row_x + tile
            inside.append(jnp.where(within_y & (at >= box_ref[k, 2]) & (at < box_ref[k, 3]), 1.0, 0.0))
        gain_ref[k] = jnp.zeros((bz, bx, by), F32)

        def plane_of(plane, carry):
            for tile in range(0, bx, 8):
                total = taps[0] * rows[plane + 1, tile : tile + 8, :]
                for tap in range(1, TAPS):
                    total = total + taps[tap] * rows[plane + 1 + tap, tile : tile + 8, :]
                gain_ref[k, plane, tile : tile + 8, :] = inside[tile // 8] / (total + BACKGROUND)
            return carry

        begin = jnp.clip(box_ref[k, 0] - start_z, 0, bz)
        end = jnp.clip(box_ref[k, 1] - start_z, 0, bz)
        lax.fori_loop(begin, end, plane_of, 0)
        return carry

    lax.fori_loop(0, views, view, 0)

    lane = lax.broadcasted_iota(jnp.int32, (8, by), 1)
    owner = lax.div(lane, 2 * PAD)
    col_y = lax.rem(lane, 2 * PAD)
    col_y = jnp.where(col_y < PAD, col_y - PAD, by + col_y - PAD) + lax.axis_index("by") * by

    def by_lane(value, start):
        for k in range(views):
            start = jnp.where(owner == k, value(k), start)
        return start

    taps = [by_lane(lambda k: prof_ref[k, 0, tap], jnp.zeros((8, by), F32)) for tap in range(TAPS)]
    box = [by_lane(lambda k: box_ref[k, i], jnp.zeros((8, by), jnp.int32)) for i in range(6)]
    within_y = (col_y >= box[4]) & (col_y < box[5])
    step = 5
    for first in range(1, deep - 1, step):
        at = slice(first * bx, (first + step) * bx)
        mixed = jnp.dot(blurred_x[0, at, :], yh_ref[0], preferred_element_type=F32)
        for k in range(1, views):
            mixed = mixed + jnp.dot(blurred_x[k, at, :], yh_ref[k], preferred_element_type=F32)
        rows[first : first + step] = (mixed[:, :by] + mixed[:, by:]).reshape(step, bx, by)

    def beside_plane(plane, carry):
        at_z = plane + start_z
        within_z = within_y & (at_z >= box[0]) & (at_z < box[1])
        for tile in range(0, bx, 8):
            at_x = row_x + tile
            total = taps[0] * rows[plane + 1, tile : tile + 8, :]
            for tap in range(1, TAPS):
                total = total + taps[tap] * rows[plane + 1 + tap, tile : tile + 8, :]
            within = within_z & (at_x >= box[2]) & (at_x < box[3])
            gain_ref[views, plane, tile : tile + 8, :] = jnp.where(within, 1.0, 0.0) / (total + BACKGROUND)
        return carry

    lax.fori_loop(0, bz, beside_plane, 0)


def quotient_body(views, block, count, gain_ref, *refs):
    parts = refs[:count]
    quot_ref, held = refs[count:]
    bz, bx, by = block
    rows = bx // count
    mine = lax.axis_index("by") if count > 1 else 0

    def view(k, carry):
        for part, part_ref in enumerate(parts):
            at = pl.ds(pl.multiple_of((mine ^ part) * rows, rows), rows)
            held[:, at, :] = gain_ref[k, :, at, :] * part_ref[k].astype(F32)
        quot_ref[k] = held[...].astype(BF16)
        return carry

    lax.fori_loop(0, views + 1, view, 0)


def return_body(views, block, links, prof_ref, box_ref, quot_ref, yr_ref, xr_ref, mid_ref, *refs):
    bz, bx, by = block
    ext = bx + 2 * PAD
    deep = bz + 2 * REACH
    link_refs = refs[: len(links)]
    rows, high_rows, low_rows, total = refs[len(links) :]
    start_z = lax.axis_index("bz") * bz

    def view(k, carry):
        cells = [quot_ref[i].reshape(bz * bx, by) for i in (k, views)]
        cells = jnp.concatenate(cells, axis=1)
        mixed = jnp.dot(cells, yr_ref[k], preferred_element_type=F32)
        rows[...] = (mixed[:, :by] + mixed[:, by:]).reshape(bz, bx, by)
        taps = [prof_ref[k, 0, tap] for tap in range(TAPS)]
        at = pl.ds(pl.multiple_of(k * bx, bx), bx)
        for out in range(deep):
            plane = out - REACH
            here = (plane + start_z >= box_ref[k, 0]) & (plane + start_z < box_ref[k, 1])

            @pl.when(here)
            def _():
                sums = []
                for tile in range(0, bx, 8):
                    part = None
                    for source in range(max(0, plane - REACH), min(bz, plane + REACH + 1)):
                        term = taps[REACH - source + plane] * rows[source, tile : tile + 8, :]
                        part = term if part is None else part + term
                    sums.append(part)
                high, low = halves(jnp.concatenate(sums, axis=0))
                high_rows[out, at, :] = high
                low_rows[out, at, :] = low

            @pl.when(jnp.logical_not(here))
            def _():
                high_rows[out, at, :] = jnp.zeros((bx, by), BF16)
                low_rows[out, at, :] = jnp.zeros((bx, by), BF16)

        return carry

    lax.fori_loop(0, views, view, 0)
    for out in range(0, deep, 2):
        high = jnp.concatenate([high_rows[out], high_rows[out + 1]], axis=1)
        low = jnp.concatenate([low_rows[out], low_rows[out + 1]], axis=1)
        mixed = jnp.dot(xr_ref[...], high, preferred_element_type=F32)
        mixed = mixed[:ext] + mixed[ext:] + jnp.dot(xr_ref[:ext], low, preferred_element_type=F32)
        total[out] = mixed[:, :by]
        total[out + 1] = mixed[:, by:]
    mid_ref[...] = total[REACH : REACH + bz, PAD : PAD + bx, :]
    for (x, z), link_ref in zip(links, link_refs):
        at_x, at_z = slice(PAD, PAD + bx), slice(REACH, REACH + bz)
        if x is not None:
            begin = jnp.where(meets_next(lax.axis_index("bx"), x), PAD + bx, 0)
            at_x = pl.ds(pl.multiple_of(begin, PAD), PAD)
        if z is not None:
            at_z = pl.ds(jnp.where(meets_next(lax.axis_index("bz"), z), REACH + bz, 0), REACH)
        link_ref[...] = total[at_z, at_x, :]


def finish_body(counts, links, share_ref, mid_ref, *refs):
    bz, bx, by = share_ref.shape
    link_refs, out_ref = refs[: len(links)], refs[len(links)]
    out_ref[...] = share_ref[...] * mid_ref[...]
    for (x, z), link_ref in zip(links, link_refs):
        at_x, at_z, known = slice(None), slice(None), None
        if x is not None:
            index = lax.axis_index("bx")
            begin = jnp.where(meets_next(index, x), bx - PAD, 0)
            at_x = pl.ds(pl.multiple_of(begin, PAD), PAD)
            known = has_partner(index, counts[0], x)
        if z is not None:
            index = lax.axis_index("bz")
            at_z = pl.ds(jnp.where(meets_next(index, z), bz - REACH, 0), REACH)
            there = has_partner(index, counts[1], z)
            known = there if known is None else known & there

        @pl.when(known)
        def _():
            out_ref[at_z, at_x, :] = out_ref[at_z, at_x, :] + share_ref[at_z, at_x, :] * link_ref[...]


def local(estimate, recorded, profiles, view_boxes):
    block = estimate.shape
    bz, bx, by = block
    views = recorded.shape[0]
    part_rows = recorded.shape[2]
    count = lax.axis_size("by")
    counts = (lax.axis_size("bx"), lax.axis_size("bz"))
    links = links_of(*counts)
    ext = bx + 2 * PAD
    deep = bz + 2 * PAD
    shape = jax.ShapeDtypeStruct

    def link_shape(link, reach, dtype):
        x, z = link
        return shape((bz if z is None else reach, bx if x is None else PAD, by), dtype)

    side = shape((SIDE, bz * bx), BF16)
    own, order, second = call(
        columns_body,
        [shape(block, BF16), side, side],
        [ANY, VMEM],
        nbytes=bz * bx * by * 4,
        name="columns",
    )(recorded, estimate)
    first, second = exchange_y(order, second)

    if count & (count - 1) == 0 and count <= 4 and part_rows % 8 == 0:
        parts = [*call(
            pieces_body,
            [shape((views + 1, bz, part_rows, by), BF16)] * count,
            [ANY, VMEM],
            nbytes=views * bz * bx * by * 4,
            name="pieces",
        )(order, recorded)]
        for other in range(1, count):
            parts[other] = lax.ppermute(parts[other], "by", [(i, i ^ other) for i in range(count)])
    else:
        tiles = jnp.moveaxis(recorded.reshape(views, bz, part_rows, count, by), 3, 0)
        before = jnp.roll(tiles[..., by - PAD :], 1, axis=0)
        after = jnp.roll(tiles[..., :PAD], -1, axis=0)
        beside = jnp.moveaxis(jnp.concatenate([before, after], axis=-1), 1, 3)
        beside = beside.reshape(count, 1, bz, part_rows, views * 2 * PAD)
        beside = jnp.pad(beside, [(0, 0)] * 4 + [(0, by - views * 2 * PAD)])
        tiles = jnp.concatenate([tiles, beside], axis=1)
        tiles = lax.all_to_all(tiles, "by", split_axis=0, concat_axis=0, tiled=True)
        parts = [jnp.moveaxis(tiles, 0, 2).reshape(views + 1, bz, bx, by)]

    along_x, along_z = swaps_of(counts[0]), swaps_of(counts[1])
    halo, *edges = call(
        functools.partial(edges_body, count),
        [shape((bz * bx, 2 * SIDE), BF16)]
        + [shape((PAD + PAD * bx // by, bx, by), BF16)] * len(along_z),
        [VMEM] * 3,
        nbytes=bz * bx * by * 4,
        name="edges",
    )(own, first, second)
    edges = [exchange(cells, (None, swap), *counts) for swap, cells in zip(along_z, edges)]

    cells, halos, *edges = call(
        functools.partial(deep_body, counts, len(along_z)),
        [shape((deep, bx, by), F32), shape((deep, bx, 2 * SIDE), F32)]
        + [shape((deep + 2 * SIDE * deep // by, PAD, by), BF16)] * len(along_x),
        [ANY] + [VMEM] * (2 + len(along_z)),
        nbytes=deep * bx * by * 4,
        name="deep",
    )(own, own, halo, *edges)
    edges = [exchange(cells, (swap, None), *counts) for swap, cells in zip(along_x, edges)]

    yf, yh, yr, xf, xr, share = call(
        functools.partial(bands_body, views),
        [
            shape((views, by + 2 * SIDE, 2 * by), BF16),
            shape((views, by + 2 * SIDE, 2 * by), BF16),
            shape((views, 2 * by, 2 * by), BF16),
            shape((views * bx, 2 * ext), BF16),
            shape((2 * ext, views * bx), BF16),
            shape(block, F32),
        ],
        [ANY] + [SMEM] * 2 + [VMEM],
        flops=views * 64 * by * by,
        nbytes=views * by * by * 8,
        name="bands",
    )(order, profiles, view_boxes, estimate)

    gain = call(
        functools.partial(forward_body, views, block, counts, len(along_x)),
        shape((views + 1, bz, bx, by), F32),
        [SMEM] * 2 + [VMEM] * (5 + len(along_x)),
        [
            pltpu.VMEM((max(1, len(along_x)), deep, PAD, 2 * SIDE), F32),
            pltpu.VMEM((views, deep * bx, by + 2 * SIDE), BF16),
            pltpu.VMEM((deep, bx, by), F32),
        ],
        flops=views * deep * ext * by * 600,
        nbytes=views * bz * bx * by * 8,
        name="forward",
    )(profiles, view_boxes, cells, halos, yf, yh, xf, *edges)

    quot = call(
        functools.partial(quotient_body, views, block, len(parts)),
        shape((views + 1, bz, bx, by), BF16),
        [VMEM] * (1 + len(parts)),
        [pltpu.VMEM((bz, bx, by), F32)],
        flops=views * bz * bx * by * 40,
        nbytes=views * bz * bx * by * 8,
        name="quotient",
    )(gain, *parts)

    mid, *sums = call(
        functools.partial(return_body, views, block, links),
        [shape(block, F32)] + [link_shape(link, REACH, F32) for link in links],
        [SMEM] * 2 + [VMEM] * 3,
        [
            pltpu.VMEM((bz, bx, by), F32),
            pltpu.VMEM((bz + 2 * REACH, views * bx, by), BF16),
            pltpu.VMEM((bz + 2 * REACH, views * bx, by), BF16),
            pltpu.VMEM((bz + 2 * REACH, ext, by), F32),
        ],
        flops=views * bz * ext * by * 600,
        nbytes=views * bz * bx * by * 8,
        name="returned",
    )(profiles, view_boxes, quot, yr, xr)
    sums = [exchange(cells, link, *counts) for link, cells in zip(links, sums)]
    return call(
        functools.partial(finish_body, counts, links),
        shape(block, F32),
        [VMEM] * (2 + len(links)),
        nbytes=bz * bx * by * 12,
        name="finish",
    )(share, mid, *sums)


def solution(mesh):
    placed = (
        P(("groups", "bz"), "bx", "by"),
        P(None, ("groups", "bz"), ("bx", "by"), None),
        P(),
        P("groups", None),
    )
    return jax.shard_map(
        local,
        mesh=mesh,
        in_specs=placed,
        out_specs=P(("groups", "bz"), "bx", "by"),
        check_vma=False,
    )
```

```python
import functools

import jax
import jax.numpy as jnp
from jax import lax
from jax.experimental import pallas as pl
from jax.experimental.pallas import tpu as pltpu
from jax.sharding import PartitionSpec as P

TAPS = 15
REACH = TAPS // 2
PAD = 8
SIDE = 2 * PAD
BACKGROUND = 0.05
GROUP = 6
WEIGHT = 0.5

F32 = jnp.float32
BF16 = jnp.bfloat16

VMEM = pl.BlockSpec(memory_space=pltpu.VMEM)
SMEM = pl.BlockSpec(memory_space=pltpu.SMEM)
ANY = pl.BlockSpec(memory_space=pl.ANY)
HBM = pl.BlockSpec(memory_space=pltpu.HBM)


def call(body, out_shape, in_specs, scratch=(), flops=0, nbytes=0, name=None):
    many = isinstance(out_shape, (list, tuple))
    return pl.pallas_call(
        body,
        out_shape=out_shape,
        in_specs=in_specs,
        out_specs=[VMEM] * len(out_shape) if many else VMEM,
        scratch_shapes=list(scratch),
        compiler_params=pltpu.CompilerParams(vmem_limit_bytes=40 * 1024 * 1024),
        cost_estimate=pl.CostEstimate(
            flops=int(WEIGHT * flops), bytes_accessed=int(WEIGHT * nbytes), transcendentals=0
        ),
        name=name,
    )


def partner(index, count, swap):
    other = index ^ 1 if swap == 0 else ((index + 1) ^ 1) - 1
    return other if 0 <= other < count else index


def swaps_of(count):
    return {1: [], 2: [0]}.get(count, [0, 1])


def meets_next(index, swap):
    return lax.rem(index + swap, 2) == 0


def has_partner(index, count, swap):
    after = meets_next(index, swap)
    return jnp.where(after, index < count - 1, index > 0)


def links_of(count_x, count_z):
    along_x, along_z = [None, *swaps_of(count_x)], [None, *swaps_of(count_z)]
    return [(x, z) for x in along_x for z in along_z if (x, z) != (None, None)]


def exchange(cells, link, count_x, count_z):
    x, z = link
    pairs = []
    for i in range(count_x):
        for j in range(count_z):
            to_x = i if x is None else partner(i, count_x, x)
            to_z = j if z is None else partner(j, count_z, z)
            pairs.append((i * count_z + j, to_x * count_z + to_z))
    return lax.ppermute(cells, ("bx", "bz"), pairs)


def exchange_y(first, second):
    count = lax.axis_size("by")
    return [
        lax.ppermute(cells, "by", [(i, partner(i, count, swap)) for i in range(count)])
        for swap, cells in enumerate((first, second))
    ]


def banded(offset, tap_of):
    matrix = jnp.zeros(offset.shape, F32)
    for tap in range(TAPS):
        matrix = jnp.where(offset == tap, tap_of(tap), matrix)
    return matrix


def halves(matrix):
    high = matrix.astype(BF16)
    return high, (matrix - high.astype(F32)).astype(BF16)


def packed(cells, begin):
    by = cells.shape[1]
    row = lax.broadcasted_iota(jnp.int32, (SIDE, by), 0)
    col = lax.broadcasted_iota(jnp.int32, (SIDE, by), 1)
    pick = jnp.where(col == row + begin, 1.0, 0.0).astype(BF16)
    return lax.dot_general(
        pick, cells, (((1,), (1,)), ((), ())), preferred_element_type=F32
    ).astype(BF16)


def unpack_both(count, first_ref, second_ref):
    mine = lax.axis_index("by")
    first, second = first_ref[...].astype(F32), second_ref[...].astype(F32)
    even = meets_next(mine, 0)
    before = jnp.where(even, second, first)
    after = jnp.where(even, first, second)
    before = jnp.where(mine > 0, before, 0.0)
    after = jnp.where(mine < count - 1, after, 0.0)
    return jnp.concatenate([before, after], axis=0).T.astype(BF16)


def columns_body(est_ref, cells_ref, first_ref, second_ref):
    bz, bx, by = est_ref.shape
    cells_ref[...] = est_ref[...].astype(BF16)
    cells = cells_ref[...].reshape(bz * bx, by)
    mine = lax.axis_index("by")
    first_ref[...] = packed(cells, jnp.where(meets_next(mine, 0), by - SIDE, 0))
    second_ref[...] = packed(cells, jnp.where(meets_next(mine, 1), by - SIDE, 0))


def pieces_body(order_ref, rec_ref, *out_refs):
    views, bz, rows, width = rec_ref.shape
    count = len(out_refs)
    by = width // count
    row = lax.broadcasted_iota(jnp.int32, (by, by), 0)
    col = lax.broadcasted_iota(jnp.int32, (by, by), 1)
    picks = []
    for k in range(views):
        lane = col - 2 * PAD * k
        picks.append((lane >= 0) & (lane < PAD) & (row == by - PAD + lane))
        picks.append((lane >= PAD) & (lane < 2 * PAD) & (row == lane - PAD))
    picks = jnp.concatenate([jnp.where(pick, 1.0, 0.0).astype(BF16) for pick in picks], axis=0)
    for other, out_ref in enumerate(out_refs):
        target = lax.axis_index("by") ^ other

        def columns(tile):
            return pl.ds(pl.multiple_of(jnp.clip(tile, 0, count - 1) * by, by), by)

        out_ref[:views] = rec_ref[:, :, :, columns(target)]
        beside = []
        for k in range(views):
            for tile in (target - 1, target + 1):
                cells = rec_ref[k, :, :, columns(tile)]
                beside.append(cells.astype(F32).reshape(bz * rows, by).astype(BF16))
        beside = jnp.dot(jnp.concatenate(beside, axis=1), picks, preferred_element_type=F32)
        out_ref[views] = beside.reshape(bz, rows, by).astype(BF16)


def upright(cells):
    return cells.astype(F32).T


def lying(cells):
    wide = cells.shape[1]
    row = lax.broadcasted_iota(jnp.int32, (wide, wide), 0)
    col = lax.broadcasted_iota(jnp.int32, (wide, wide), 1)
    same = jnp.where(row == col, 1.0, 0.0).astype(BF16)
    return lax.dot_general(
        same, cells.astype(BF16), (((1,), (1,)), ((), ())), preferred_element_type=F32
    )


def edges_body(count, est_ref, first_ref, second_ref, halo_ref, *out_refs):
    bz, bx, by = est_ref.shape
    halo_ref[...] = unpack_both(count, first_ref, second_ref)
    for swap, out_ref in enumerate(out_refs):
        begin = jnp.where(meets_next(lax.axis_index("bz"), swap), bz - PAD, 0)
        out_ref[:PAD] = est_ref[pl.ds(begin, PAD)]
        rows = halo_ref[pl.ds(pl.multiple_of(begin * bx, PAD * bx), PAD * bx), :]
        flat = lying(rows).astype(BF16)
        for i in range(PAD * bx // by):
            out_ref[PAD + i, : 2 * SIDE, :] = flat[:, i * by : (i + 1) * by]


def deep_body(counts, count_z, order_ref, est_ref, halo_ref, *refs):
    bz, bx, by = est_ref.shape
    deep = bz + 2 * PAD
    z_refs, (cells_ref, halos_ref, *out_refs) = refs[:count_z], refs[count_z:]
    cells_ref[...] = jnp.zeros_like(cells_ref)
    halos_ref[...] = jnp.zeros_like(halos_ref)
    cells_ref[PAD : PAD + bz] = est_ref[...].astype(F32)
    halos_ref[PAD : PAD + bz] = halo_ref[...].astype(F32).reshape(bz, bx, 2 * SIDE)
    for swap, z_ref in enumerate(z_refs):
        index = lax.axis_index("bz")
        at = pl.ds(jnp.where(meets_next(index, swap), PAD + bz, 0), PAD)

        @pl.when(has_partner(index, counts[1], swap))
        def _():
            cells_ref[at] = z_ref[:PAD].astype(F32)
            flat = jnp.concatenate(
                [z_ref[PAD + i, : 2 * SIDE, :] for i in range(PAD * bx // by)], axis=1
            )
            halos_ref[at] = upright(flat).reshape(PAD, bx, 2 * SIDE)

    for swap, out_ref in enumerate(out_refs):
        begin = jnp.where(meets_next(lax.axis_index("bx"), swap), bx - PAD, 0)
        at = pl.ds(pl.multiple_of(begin, PAD), PAD)
        out_ref[:deep] = cells_ref[:, at, :].astype(BF16)
        flat = lying(halos_ref[:, at, :].reshape(deep * PAD, 2 * SIDE))
        groups = 2 * SIDE // PAD
        for i in range(deep * PAD // by):
            for j in range(groups):
                part = flat[j * PAD : (j + 1) * PAD, i * by : (i + 1) * by]
                out_ref[deep + groups * i + j] = part.astype(BF16)


def iota(shape, dim):
    return lax.broadcasted_iota(jnp.int32, shape, dim)


def forward_bands_body(views, block, order_ref, prof_ref, yf_ref, yh_ref, xf_ref):
    bz, bx, by = block
    ext = bx + 2 * PAD
    shape_y = (by + 2 * SIDE, by)
    row = iota(shape_y, 0)
    source = jnp.where(row < by, row, jnp.where(row < by + SIDE, row - by - SIDE, row - SIDE))
    target = iota(shape_y, 1)
    beside_view = lax.div(target, 2 * PAD)
    beside = lax.rem(target, 2 * PAD)
    beside = jnp.where(beside < PAD, beside - PAD, by + beside - PAD)
    shape_x = (bx, 2 * ext)
    col = iota(shape_x, 1)
    is_low = col >= ext
    forward_x = jnp.where(is_low, col - ext, col) - PAD - iota(shape_x, 0)

    def view(k, carry):
        forward = banded(source - target + REACH, lambda tap: prof_ref[k, 2, tap])
        high, low = halves(forward)
        yf_ref[k, :, :by] = high
        yf_ref[k, :, by:] = low
        forward = banded(source - beside + REACH, lambda tap: prof_ref[k, 2, tap])
        high, low = halves(jnp.where(beside_view == k, forward, 0.0))
        yh_ref[k, :, :by] = high
        yh_ref[k, :, by:] = low
        high, low = halves(banded(forward_x + REACH, lambda tap: prof_ref[k, 1, tap]))
        at = pl.ds(pl.multiple_of(k * bx, bx), bx)
        xf_ref[at, :] = jnp.where(is_low, low.astype(F32), high.astype(F32)).astype(BF16)
        return carry

    lax.fori_loop(0, views, view, 0)


def return_bands_body(views, order_ref, prof_ref, box_ref, est_ref, yr_ref, xr_ref, share_ref):
    bz, bx, by = est_ref.shape
    ext = bx + 2 * PAD
    start_z = lax.axis_index("bz") * bz
    start_x = lax.axis_index("bx") * bx
    start_y = lax.axis_index("by") * by
    back_row, back_target = iota((by, by), 0), iota((by, by), 1)
    side_row, side_target = iota((2 * PAD, by), 0), iota((2 * PAD, by), 1)
    side_row = jnp.where(side_row < PAD, side_row - PAD, by + side_row - PAD)

    def view(k, carry):
        def back(row, target):
            within = (target >= box_ref[k, 4] - start_y) & (target < box_ref[k, 5] - start_y)
            matrix = banded(REACH - row + target, lambda tap: prof_ref[k, 2, tap])
            return halves(jnp.where(within, matrix, 0.0))

        high, low = back(back_row, back_target)
        yr_ref[k, :by, :by] = high
        yr_ref[k, :by, by:] = low
        yr_ref[k, by:, :] = jnp.zeros((by, 2 * by), BF16)
        at = pl.ds(pl.multiple_of(by + 2 * PAD * k, 2 * PAD), 2 * PAD)
        high, low = back(side_row, side_target)
        yr_ref[k, at, :by] = high
        yr_ref[k, at, by:] = low
        return carry

    lax.fori_loop(0, views, view, 0)

    shape_x = (ext, views * bx)
    target = iota(shape_x, 0) - PAD
    col = iota(shape_x, 1)

    def back_view(k, matrix):
        source = col - k * bx
        back = banded(REACH - source + target, lambda tap: prof_ref[k, 1, tap])
        within = (source >= 0) & (source < bx)
        within = within & (target >= box_ref[k, 2] - start_x) & (target < box_ref[k, 3] - start_x)
        return jnp.where(within, back, matrix)

    high, low = halves(lax.fori_loop(0, views, back_view, jnp.zeros(shape_x, F32)))
    xr_ref[:ext] = high
    xr_ref[ext:] = low

    row_x = iota((bx, by), 0) + start_x
    col_y = iota((bx, by), 1) + start_y
    flat = []
    for k in range(views):
        within = (col_y >= box_ref[k, 4]) & (col_y < box_ref[k, 5])
        within = within & (row_x >= box_ref[k, 2]) & (row_x < box_ref[k, 3])
        flat.append(jnp.where(within, 1.0, 0.0))
    for plane in range(bz):
        coverage = jnp.zeros((bx, by), F32)
        for k in range(views):
            at = plane + start_z
            here = (at >= box_ref[k, 0]) & (at < box_ref[k, 1])
            coverage = coverage + jnp.where(here, 1.0, 0.0) * flat[k]
        share_ref[plane] = est_ref[plane] / coverage


def forward_body(views, block, counts, count_x, prof_ref, box_ref, cells_ref, halos_ref, yf_ref, yh_ref, xf_ref, *refs):
    x_refs, (gain_ref, side_halo, blurred_x, rows) = refs[:count_x], refs[count_x:]
    bz, bx, by = block
    deep = bz + 2 * PAD
    sides = []
    for swap, x_ref in enumerate(x_refs):
        index = lax.axis_index("bx")
        known = has_partner(index, counts[0], swap)
        after = meets_next(index, swap)
        sides.append((known & jnp.logical_not(after), known & after))
        groups = 2 * SIDE // PAD
        flat = [
            jnp.concatenate([x_ref[deep + groups * i + j].astype(F32) for j in range(groups)], axis=0)
            for i in range(deep * PAD // by)
        ]
        side_halo[swap] = jnp.concatenate(flat, axis=1).T.reshape(deep, PAD, 2 * SIDE)
    for plane in range(1, deep - 1):
        left = right = jnp.zeros((PAD, by), F32)
        left_halo = right_halo = jnp.zeros((PAD, 2 * SIDE), F32)
        for swap, (is_left, is_right) in enumerate(sides):
            came, came_halo = x_refs[swap][plane].astype(F32), side_halo[swap, plane]
            left = jnp.where(is_left, came, left)
            right = jnp.where(is_right, came, right)
            left_halo = jnp.where(is_left, came_halo, left_halo)
            right_halo = jnp.where(is_right, came_halo, right_halo)
        cells = jnp.concatenate([left, cells_ref[plane], right], axis=0).astype(BF16)
        halo = jnp.concatenate([left_halo, halos_ref[plane], right_halo], axis=0).astype(BF16)
        cells = jnp.concatenate([cells, halo], axis=1)
        cells = jnp.concatenate([cells, cells], axis=0)
        mixed = jnp.dot(xf_ref[...], cells, preferred_element_type=F32).astype(BF16)
        for k in range(views):
            blurred_x[k, plane * bx : (plane + 1) * bx, :] = mixed[k * bx : (k + 1) * bx]
    row_x = lax.broadcasted_iota(jnp.int32, (8, by), 0) + lax.axis_index("bx") * bx
    col_y = lax.broadcasted_iota(jnp.int32, (8, by), 1) + lax.axis_index("by") * by
    start_z = lax.axis_index("bz") * bz
    step = 10

    def view(k, carry):
        along_y = yf_ref[k]
        for first in range(1, deep - 1, step):
            mixed = jnp.dot(
                blurred_x[k, first * bx : (first + step) * bx, :], along_y, preferred_element_type=F32
            )
            rows[first : first + step] = (mixed[:, :by] + mixed[:, by:]).reshape(step, bx, by)
        taps = [prof_ref[k, 0, tap] for tap in range(TAPS)]
        within_y = (col_y >= box_ref[k, 4]) & (col_y < box_ref[k, 5])
        inside = []
        for tile in range(0, bx, 8):
            at = row_x + tile
            inside.append(jnp.where(within_y & (at >= box_ref[k, 2]) & (at < box_ref[k, 3]), 1.0, 0.0))
        low_z = box_ref[k, 0] - start_z
        high_z = box_ref[k, 1] - start_z
        for first in range(0, bz, 4):
            some = (first + 4 > low_z) & (first < high_z)

            @pl.when(some)
            def _():
                for tile in range(0, bx, 8):
                    for plane in range(first, first + 4):
                        total = taps[0] * rows[plane + 1, tile : tile + 8, :]
                        for tap in range(1, TAPS):
                            total = total + taps[tap] * rows[plane + 1 + tap, tile : tile + 8, :]
                        here = jnp.where((plane >= low_z) & (plane < high_z), 1.0, 0.0)
                        gain_ref[k, plane, tile : tile + 8, :] = here * inside[tile // 8] / (total + BACKGROUND)

            @pl.when(jnp.logical_not(some))
            def _():
                gain_ref[k, first : first + 4] = jnp.zeros((4, bx, by), F32)

        return carry

    lax.fori_loop(0, views, view, 0)

    lane = lax.broadcasted_iota(jnp.int32, (8, by), 1)
    owner = lax.div(lane, 2 * PAD)
    col_y = lax.rem(lane, 2 * PAD)
    col_y = jnp.where(col_y < PAD, col_y - PAD, by + col_y - PAD) + lax.axis_index("by") * by

    def by_lane(value, start):
        for k in range(views):
            start = jnp.where(owner == k, value(k), start)
        return start

    taps = [by_lane(lambda k: prof_ref[k, 0, tap], jnp.zeros((8, by), F32)) for tap in range(TAPS)]
    box = [by_lane(lambda k: box_ref[k, i], jnp.zeros((8, by), jnp.int32)) for i in range(6)]
    within_y = (col_y >= box[4]) & (col_y < box[5])
    step = 5
    for first in range(1, deep - 1, step):
        at = slice(first * bx, (first + step) * bx)
        mixed = jnp.dot(blurred_x[0, at, :], yh_ref[0], preferred_element_type=F32)
        for k in range(1, views):
            mixed = mixed + jnp.dot(blurred_x[k, at, :], yh_ref[k], preferred_element_type=F32)
        rows[first : first + step] = (mixed[:, :by] + mixed[:, by:]).reshape(step, bx, by)

    def beside_plane(plane, carry):
        at_z = plane + start_z
        within_z = within_y & (at_z >= box[0]) & (at_z < box[1])
        for tile in range(0, bx, 8):
            at_x = row_x + tile
            total = taps[0] * rows[plane + 1, tile : tile + 8, :]
            for tap in range(1, TAPS):
                total = total + taps[tap] * rows[plane + 1 + tap, tile : tile + 8, :]
            within = within_z & (at_x >= box[2]) & (at_x < box[3])
            gain_ref[views, plane, tile : tile + 8, :] = jnp.where(within, 1.0, 0.0) / (total + BACKGROUND)
        return carry

    lax.fori_loop(0, bz, beside_plane, 0)


def quotient_body(views, block, count, gain_ref, *refs):
    parts = refs[:count]
    quot_ref, held = refs[count:]
    bz, bx, by = block
    rows = bx // count
    mine = lax.axis_index("by") if count > 1 else 0

    def view(k, carry):
        for part, part_ref in zip(range(count - 1, -1, -1), parts):
            at = pl.ds(pl.multiple_of((mine ^ part) * rows, rows), rows)
            held[:, at, :] = gain_ref[k, :, at, :] * part_ref[k].astype(F32)
        quot_ref[k] = held[...].astype(BF16)
        return carry

    lax.fori_loop(0, views + 1, view, 0)


def return_body(views, block, links, prof_ref, box_ref, quot_ref, yr_ref, xr_ref, mid_ref, *refs):
    bz, bx, by = block
    ext = bx + 2 * PAD
    deep = bz + 2 * REACH
    link_refs = refs[: len(links)]
    rows, high_rows, low_rows, total = refs[len(links) :]
    start_z = lax.axis_index("bz") * bz

    def view(k, carry):
        cells = [quot_ref[i].reshape(bz * bx, by) for i in (k, views)]
        cells = jnp.concatenate(cells, axis=1)
        mixed = jnp.dot(cells, yr_ref[k], preferred_element_type=F32)
        rows[...] = (mixed[:, :by] + mixed[:, by:]).reshape(bz, bx, by)
        taps = [prof_ref[k, 0, tap] for tap in range(TAPS)]
        at = pl.ds(pl.multiple_of(k * bx, bx), bx)
        low_z = box_ref[k, 0] - start_z + REACH
        high_z = box_ref[k, 1] - start_z + REACH
        for first in range(0, deep, GROUP):
            some = (first + GROUP > low_z) & (first < high_z)

            @pl.when(some)
            def _():
                for tile in range(0, bx, 16):
                    for out in range(first, first + GROUP):
                        plane = out - REACH
                        parts = []
                        for half in (tile, tile + 8):
                            part = None
                            for source in range(max(0, plane - REACH), min(bz, plane + REACH + 1)):
                                term = taps[REACH - source + plane] * rows[source, half : half + 8, :]
                                part = term if part is None else part + term
                            parts.append(part)
                        here = jnp.where((out >= low_z) & (out < high_z), 1.0, 0.0)
                        high, low = halves(here * jnp.concatenate(parts, axis=0))
                        at_x = pl.ds(pl.multiple_of(k * bx + tile, 16), 16)
                        high_rows[out, at_x, :] = high
                        low_rows[out, at_x, :] = low

            @pl.when(jnp.logical_not(some))
            def _():
                high_rows[first : first + GROUP, at, :] = jnp.zeros((GROUP, bx, by), BF16)
                low_rows[first : first + GROUP, at, :] = jnp.zeros((GROUP, bx, by), BF16)

        return carry

    lax.fori_loop(0, views, view, 0)
    for out in range(0, deep, 2):
        high = jnp.concatenate([high_rows[out], high_rows[out + 1]], axis=1)
        low = jnp.concatenate([low_rows[out], low_rows[out + 1]], axis=1)
        mixed = jnp.dot(xr_ref[...], high, preferred_element_type=F32)
        mixed = mixed[:ext] + mixed[ext:] + jnp.dot(xr_ref[:ext], low, preferred_element_type=F32)
        total[out] = mixed[:, :by]
        total[out + 1] = mixed[:, by:]
    mid_ref[...] = total[REACH : REACH + bz, PAD : PAD + bx, :]
    for (x, z), link_ref in zip(links, link_refs):
        at_x, at_z = slice(PAD, PAD + bx), slice(REACH, REACH + bz)
        if x is not None:
            begin = jnp.where(meets_next(lax.axis_index("bx"), x), PAD + bx, 0)
            at_x = pl.ds(pl.multiple_of(begin, PAD), PAD)
        if z is not None:
            at_z = pl.ds(jnp.where(meets_next(lax.axis_index("bz"), z), REACH + bz, 0), REACH)
        link_ref[...] = total[at_z, at_x, :]


def finish_body(counts, links, share_ref, mid_ref, *refs):
    bz, bx, by = share_ref.shape
    link_refs, out_ref = refs[: len(links)], refs[len(links)]
    out_ref[...] = share_ref[...] * mid_ref[...]
    for (x, z), link_ref in zip(links, link_refs):
        at_x, at_z, known = slice(None), slice(None), None
        if x is not None:
            index = lax.axis_index("bx")
            begin = jnp.where(meets_next(index, x), bx - PAD, 0)
            at_x = pl.ds(pl.multiple_of(begin, PAD), PAD)
            known = has_partner(index, counts[0], x)
        if z is not None:
            index = lax.axis_index("bz")
            at_z = pl.ds(jnp.where(meets_next(index, z), bz - REACH, 0), REACH)
            there = has_partner(index, counts[1], z)
            known = there if known is None else known & there

        @pl.when(known)
        def _():
            out_ref[at_z, at_x, :] = out_ref[at_z, at_x, :] + share_ref[at_z, at_x, :] * link_ref[...]


def local(estimate, recorded, profiles, view_boxes):
    block = estimate.shape
    bz, bx, by = block
    views = recorded.shape[0]
    part_rows = recorded.shape[2]
    count = lax.axis_size("by")
    counts = (lax.axis_size("bx"), lax.axis_size("bz"))
    links = links_of(*counts)
    ext = bx + 2 * PAD
    deep = bz + 2 * PAD
    shape = jax.ShapeDtypeStruct

    def link_shape(link, reach, dtype):
        x, z = link
        return shape((bz if z is None else reach, bx if x is None else PAD, by), dtype)

    side = shape((SIDE, bz * bx), BF16)
    own, order, second = call(
        columns_body,
        [shape(block, BF16), side, side],
        [VMEM],
        nbytes=bz * bx * by * 4,
        name="columns",
    )(estimate)
    first, second = exchange_y(order, second)

    if count & (count - 1) == 0 and count <= 4 and part_rows % 8 == 0:
        parts = [*call(
            pieces_body,
            [shape((views + 1, bz, part_rows, by), BF16)] * count,
            [ANY, VMEM],
            nbytes=views * bz * bx * by * 4,
            name="pieces",
        )(order, recorded)]
        parts, first, second = lax.optimization_barrier((parts, first, second))
        for other in range(1, count):
            parts[other] = lax.ppermute(parts[other], "by", [(i, i ^ other) for i in range(count)])
    else:
        tiles = jnp.moveaxis(recorded.reshape(views, bz, part_rows, count, by), 3, 0)
        before = jnp.roll(tiles[..., by - PAD :], 1, axis=0)
        after = jnp.roll(tiles[..., :PAD], -1, axis=0)
        beside = jnp.moveaxis(jnp.concatenate([before, after], axis=-1), 1, 3)
        beside = beside.reshape(count, 1, bz, part_rows, views * 2 * PAD)
        beside = jnp.pad(beside, [(0, 0)] * 4 + [(0, by - views * 2 * PAD)])
        tiles = jnp.concatenate([tiles, beside], axis=1)
        tiles = lax.all_to_all(tiles, "by", split_axis=0, concat_axis=0, tiled=True)
        parts = [jnp.moveaxis(tiles, 0, 2).reshape(views + 1, bz, bx, by)]

    along_x, along_z = swaps_of(counts[0]), swaps_of(counts[1])
    halo, *edges = call(
        functools.partial(edges_body, count),
        [shape((bz * bx, 2 * SIDE), BF16)]
        + [shape((PAD + PAD * bx // by, bx, by), BF16)] * len(along_z),
        [VMEM] * 3,
        nbytes=bz * bx * by * 4,
        name="edges",
    )(own, first, second)
    edges = [exchange(cells, (None, swap), *counts) for swap, cells in zip(along_z, edges)]

    cells, halos, *edges = call(
        functools.partial(deep_body, counts, len(along_z)),
        [shape((deep, bx, by), F32), shape((deep, bx, 2 * SIDE), F32)]
        + [shape((deep + 2 * SIDE * deep // by, PAD, by), BF16)] * len(along_x),
        [ANY] + [VMEM] * (2 + len(along_z)),
        nbytes=deep * bx * by * 4,
        name="deep",
    )(own, own, halo, *edges)
    edges = [exchange(cells, (swap, None), *counts) for swap, cells in zip(along_x, edges)]

    yf, yh, xf = call(
        functools.partial(forward_bands_body, views, block),
        [
            shape((views, by + 2 * SIDE, 2 * by), BF16),
            shape((views, by + 2 * SIDE, 2 * by), BF16),
            shape((views * bx, 2 * ext), BF16),
        ],
        [ANY, SMEM],
        flops=views * 32 * by * by,
        nbytes=views * by * by * 4,
        name="forward_bands",
    )(order, profiles)

    gain = call(
        functools.partial(forward_body, views, block, counts, len(along_x)),
        shape((views + 1, bz, bx, by), F32),
        [SMEM] * 2 + [VMEM] * (5 + len(along_x)),
        [
            pltpu.VMEM((max(1, len(along_x)), deep, PAD, 2 * SIDE), F32),
            pltpu.VMEM((views, deep * bx, by + 2 * SIDE), BF16),
            pltpu.VMEM((deep, bx, by), F32),
        ],
        flops=views * deep * ext * by * 600,
        nbytes=views * bz * bx * by * 8,
        name="forward",
    )(profiles, view_boxes, cells, halos, yf, yh, xf, *edges)

    yr, xr, share = call(
        functools.partial(return_bands_body, views),
        [
            shape((views, 2 * by, 2 * by), BF16),
            shape((2 * ext, views * bx), BF16),
            shape(block, F32),
        ],
        [ANY] + [SMEM] * 2 + [VMEM],
        flops=views * 32 * by * by,
        nbytes=views * by * by * 4,
        name="return_bands",
    )(gain, profiles, view_boxes, estimate)
    quot = call(
        functools.partial(quotient_body, views, block, len(parts)),
        shape((views + 1, bz, bx, by), BF16),
        [VMEM] * (1 + len(parts)),
        [pltpu.VMEM((bz, bx, by), F32)],
        flops=views * bz * bx * by * 40,
        nbytes=views * bz * bx * by * 8,
        name="quotient",
    )(gain, *parts[::-1])

    mid, *sums = call(
        functools.partial(return_body, views, block, links),
        [shape(block, F32)] + [link_shape(link, REACH, F32) for link in links],
        [SMEM] * 2 + [VMEM] * 3,
        [
            pltpu.VMEM((bz, bx, by), F32),
            pltpu.VMEM((bz + 2 * REACH, views * bx, by), BF16),
            pltpu.VMEM((bz + 2 * REACH, views * bx, by), BF16),
            pltpu.VMEM((bz + 2 * REACH, ext, by), F32),
        ],
        flops=views * bz * ext * by * 600,
        nbytes=views * bz * bx * by * 8,
        name="returned",
    )(profiles, view_boxes, quot, yr, xr)
    sums = [exchange(cells, link, *counts) for link, cells in zip(links, sums)]
    return call(
        functools.partial(finish_body, counts, links),
        shape(block, F32),
        [VMEM] * (2 + len(links)),
        nbytes=bz * bx * by * 12,
        name="finish",
    )(share, mid, *sums)


def solution(mesh):
    placed = (
        P(("groups", "bz"), "bx", "by"),
        P(None, ("groups", "bz"), ("bx", "by"), None),
        P(),
        P("groups", None),
    )
    return jax.shard_map(
        local,
        mesh=mesh,
        in_specs=placed,
        out_specs=P(("groups", "bz"), "bx", "by"),
        check_vma=False,
    )
```

```python
import functools

import jax
import jax.numpy as jnp
from jax import lax
from jax.experimental import pallas as pl
from jax.experimental.pallas import tpu as pltpu
from jax.sharding import PartitionSpec as P

TAPS = 15
REACH = TAPS // 2
PAD = 8
SIDE = 2 * PAD
BACKGROUND = 0.05
GROUP = 6
WEIGHT = 0.8

F32 = jnp.float32
BF16 = jnp.bfloat16

VMEM = pl.BlockSpec(memory_space=pltpu.VMEM)
SMEM = pl.BlockSpec(memory_space=pltpu.SMEM)
ANY = pl.BlockSpec(memory_space=pl.ANY)
HBM = pl.BlockSpec(memory_space=pltpu.HBM)


def call(body, out_shape, in_specs, scratch=(), flops=0, nbytes=0, name=None):
    many = isinstance(out_shape, (list, tuple))
    return pl.pallas_call(
        body,
        out_shape=out_shape,
        in_specs=in_specs,
        out_specs=[VMEM] * len(out_shape) if many else VMEM,
        scratch_shapes=list(scratch),
        compiler_params=pltpu.CompilerParams(vmem_limit_bytes=40 * 1024 * 1024),
        cost_estimate=pl.CostEstimate(
            flops=int(WEIGHT * flops), bytes_accessed=int(WEIGHT * nbytes), transcendentals=0
        ),
        name=name,
    )


def partner(index, count, swap):
    other = index ^ 1 if swap == 0 else ((index + 1) ^ 1) - 1
    return other if 0 <= other < count else index


def swaps_of(count):
    return {1: [], 2: [0]}.get(count, [0, 1])


def meets_next(index, swap):
    return lax.rem(index + swap, 2) == 0


def has_partner(index, count, swap):
    after = meets_next(index, swap)
    return jnp.where(after, index < count - 1, index > 0)


def links_of(count_x, count_z):
    along_x, along_z = [None, *swaps_of(count_x)], [None, *swaps_of(count_z)]
    return [(x, z) for x in along_x for z in along_z if (x, z) != (None, None)]


def exchange(cells, link, count_x, count_z):
    x, z = link
    pairs = []
    for i in range(count_x):
        for j in range(count_z):
            to_x = i if x is None else partner(i, count_x, x)
            to_z = j if z is None else partner(j, count_z, z)
            pairs.append((i * count_z + j, to_x * count_z + to_z))
    return lax.ppermute(cells, ("bx", "bz"), pairs)


def exchange_y(first, second):
    count = lax.axis_size("by")
    return [
        lax.ppermute(cells, "by", [(i, partner(i, count, swap)) for i in range(count)])
        for swap, cells in enumerate((first, second))
    ]


def order_of(count):
    return [1, 2, 3, 0] if count == 4 else range(count - 1, -1, -1)


def banded(offset, tap_of):
    matrix = jnp.zeros(offset.shape, F32)
    for tap in range(TAPS):
        matrix = jnp.where(offset == tap, tap_of(tap), matrix)
    return matrix


def halves(matrix):
    high = matrix.astype(BF16)
    return high, (matrix - high.astype(F32)).astype(BF16)


def packed(cells, begin):
    by = cells.shape[1]
    row = lax.broadcasted_iota(jnp.int32, (SIDE, by), 0)
    col = lax.broadcasted_iota(jnp.int32, (SIDE, by), 1)
    pick = jnp.where(col == row + begin, 1.0, 0.0).astype(BF16)
    return lax.dot_general(
        pick, cells, (((1,), (1,)), ((), ())), preferred_element_type=F32
    ).astype(BF16)


def unpack_both(count, first_ref, second_ref):
    mine = lax.axis_index("by")
    first, second = first_ref[...].astype(F32), second_ref[...].astype(F32)
    even = meets_next(mine, 0)
    before = jnp.where(even, second, first)
    after = jnp.where(even, first, second)
    before = jnp.where(mine > 0, before, 0.0)
    after = jnp.where(mine < count - 1, after, 0.0)
    return jnp.concatenate([before, after], axis=0).T.astype(BF16)


def columns_body(est_ref, cells_ref, first_ref, second_ref):
    bz, bx, by = est_ref.shape
    cells_ref[...] = est_ref[...].astype(BF16)
    cells = cells_ref[...].reshape(bz * bx, by)
    mine = lax.axis_index("by")
    first_ref[...] = packed(cells, jnp.where(meets_next(mine, 0), by - SIDE, 0))
    second_ref[...] = packed(cells, jnp.where(meets_next(mine, 1), by - SIDE, 0))


def pieces_body(order_ref, rec_ref, *out_refs):
    views, bz, rows, width = rec_ref.shape
    count = len(out_refs)
    by = width // count
    row = lax.broadcasted_iota(jnp.int32, (by, by), 0)
    col = lax.broadcasted_iota(jnp.int32, (by, by), 1)
    picks = []
    for k in range(views):
        lane = col - 2 * PAD * k
        picks.append((lane >= 0) & (lane < PAD) & (row == by - PAD + lane))
        picks.append((lane >= PAD) & (lane < 2 * PAD) & (row == lane - PAD))
    picks = jnp.concatenate([jnp.where(pick, 1.0, 0.0).astype(BF16) for pick in picks], axis=0)
    for other, out_ref in enumerate(out_refs):
        target = lax.axis_index("by") ^ other

        def columns(tile):
            return pl.ds(pl.multiple_of(jnp.clip(tile, 0, count - 1) * by, by), by)

        out_ref[:views] = rec_ref[:, :, :, columns(target)]
        beside = []
        for k in range(views):
            for tile in (target - 1, target + 1):
                cells = rec_ref[k, :, :, columns(tile)]
                beside.append(cells.astype(F32).reshape(bz * rows, by).astype(BF16))
        beside = jnp.dot(jnp.concatenate(beside, axis=1), picks, preferred_element_type=F32)
        out_ref[views] = beside.reshape(bz, rows, by).astype(BF16)


def upright(cells):
    return cells.astype(F32).T


def lying(cells):
    wide = cells.shape[1]
    row = lax.broadcasted_iota(jnp.int32, (wide, wide), 0)
    col = lax.broadcasted_iota(jnp.int32, (wide, wide), 1)
    same = jnp.where(row == col, 1.0, 0.0).astype(BF16)
    return lax.dot_general(
        same, cells.astype(BF16), (((1,), (1,)), ((), ())), preferred_element_type=F32
    )


def edges_body(count, est_ref, first_ref, second_ref, halo_ref, *out_refs):
    bz, bx, by = est_ref.shape
    halo_ref[...] = unpack_both(count, first_ref, second_ref)
    for swap, out_ref in enumerate(out_refs):
        begin = jnp.where(meets_next(lax.axis_index("bz"), swap), bz - PAD, 0)
        out_ref[:PAD] = est_ref[pl.ds(begin, PAD)]
        rows = halo_ref[pl.ds(pl.multiple_of(begin * bx, PAD * bx), PAD * bx), :]
        flat = lying(rows).astype(BF16)
        for i in range(PAD * bx // by):
            out_ref[PAD + i, : 2 * SIDE, :] = flat[:, i * by : (i + 1) * by]


def deep_body(counts, count_z, order_ref, est_ref, halo_ref, *refs):
    bz, bx, by = est_ref.shape
    deep = bz + 2 * PAD
    z_refs, (cells_ref, halos_ref, *out_refs) = refs[:count_z], refs[count_z:]
    cells_ref[...] = jnp.zeros_like(cells_ref)
    halos_ref[...] = jnp.zeros_like(halos_ref)
    cells_ref[PAD : PAD + bz] = est_ref[...].astype(F32)
    halos_ref[PAD : PAD + bz] = halo_ref[...].astype(F32).reshape(bz, bx, 2 * SIDE)
    for swap, z_ref in enumerate(z_refs):
        index = lax.axis_index("bz")
        at = pl.ds(jnp.where(meets_next(index, swap), PAD + bz, 0), PAD)

        @pl.when(has_partner(index, counts[1], swap))
        def _():
            cells_ref[at] = z_ref[:PAD].astype(F32)
            flat = jnp.concatenate(
                [z_ref[PAD + i, : 2 * SIDE, :] for i in range(PAD * bx // by)], axis=1
            )
            halos_ref[at] = upright(flat).reshape(PAD, bx, 2 * SIDE)

    for swap, out_ref in enumerate(out_refs):
        begin = jnp.where(meets_next(lax.axis_index("bx"), swap), bx - PAD, 0)
        at = pl.ds(pl.multiple_of(begin, PAD), PAD)
        out_ref[:deep] = cells_ref[:, at, :].astype(BF16)
        flat = lying(halos_ref[:, at, :].reshape(deep * PAD, 2 * SIDE))
        groups = 2 * SIDE // PAD
        for i in range(deep * PAD // by):
            for j in range(groups):
                part = flat[j * PAD : (j + 1) * PAD, i * by : (i + 1) * by]
                out_ref[deep + groups * i + j] = part.astype(BF16)


def iota(shape, dim):
    return lax.broadcasted_iota(jnp.int32, shape, dim)


def forward_bands_body(views, block, order_ref, prof_ref, yf_ref, yh_ref, xf_ref):
    bz, bx, by = block
    ext = bx + 2 * PAD
    shape_y = (by + 2 * SIDE, by)
    row = iota(shape_y, 0)
    source = jnp.where(row < by, row, jnp.where(row < by + SIDE, row - by - SIDE, row - SIDE))
    target = iota(shape_y, 1)
    beside_view = lax.div(target, 2 * PAD)
    beside = lax.rem(target, 2 * PAD)
    beside = jnp.where(beside < PAD, beside - PAD, by + beside - PAD)
    shape_x = (bx, 2 * ext)
    col = iota(shape_x, 1)
    is_low = col >= ext
    forward_x = jnp.where(is_low, col - ext, col) - PAD - iota(shape_x, 0)

    def view(k, carry):
        forward = banded(source - target + REACH, lambda tap: prof_ref[(k * 3 + 2) * TAPS + tap])
        high, low = halves(forward)
        yf_ref[k, :, :by] = high
        yf_ref[k, :, by:] = low
        forward = banded(source - beside + REACH, lambda tap: prof_ref[(k * 3 + 2) * TAPS + tap])
        high, low = halves(jnp.where(beside_view == k, forward, 0.0))
        yh_ref[k, :, :by] = high
        yh_ref[k, :, by:] = low
        high, low = halves(banded(forward_x + REACH, lambda tap: prof_ref[(k * 3 + 1) * TAPS + tap]))
        at = pl.ds(pl.multiple_of(k * bx, bx), bx)
        xf_ref[at, :] = jnp.where(is_low, low.astype(F32), high.astype(F32)).astype(BF16)
        return carry

    lax.fori_loop(0, views, view, 0)


def return_bands_body(views, order_ref, prof_ref, box_ref, est_ref, yr_ref, xr_ref, share_ref):
    bz, bx, by = est_ref.shape
    ext = bx + 2 * PAD
    start_z = lax.axis_index("bz") * bz
    start_x = lax.axis_index("bx") * bx
    start_y = lax.axis_index("by") * by
    back_row, back_target = iota((by, by), 0), iota((by, by), 1)
    side_row, side_target = iota((2 * PAD, by), 0), iota((2 * PAD, by), 1)
    side_row = jnp.where(side_row < PAD, side_row - PAD, by + side_row - PAD)

    def view(k, carry):
        def back(row, target):
            within = (target >= box_ref[k * 6 + 4] - start_y) & (target < box_ref[k * 6 + 5] - start_y)
            matrix = banded(REACH - row + target, lambda tap: prof_ref[(k * 3 + 2) * TAPS + tap])
            return halves(jnp.where(within, matrix, 0.0))

        high, low = back(back_row, back_target)
        yr_ref[k, :by, :by] = high
        yr_ref[k, :by, by:] = low
        yr_ref[k, by:, :] = jnp.zeros((by, 2 * by), BF16)
        at = pl.ds(pl.multiple_of(by + 2 * PAD * k, 2 * PAD), 2 * PAD)
        high, low = back(side_row, side_target)
        yr_ref[k, at, :by] = high
        yr_ref[k, at, by:] = low
        return carry

    lax.fori_loop(0, views, view, 0)

    shape_x = (ext, views * bx)
    target = iota(shape_x, 0) - PAD
    col = iota(shape_x, 1)

    def back_view(k, matrix):
        source = col - k * bx
        back = banded(REACH - source + target, lambda tap: prof_ref[(k * 3 + 1) * TAPS + tap])
        within = (source >= 0) & (source < bx)
        within = within & (target >= box_ref[k * 6 + 2] - start_x) & (target < box_ref[k * 6 + 3] - start_x)
        return jnp.where(within, back, matrix)

    high, low = halves(lax.fori_loop(0, views, back_view, jnp.zeros(shape_x, F32)))
    xr_ref[:ext] = high
    xr_ref[ext:] = low

    row_x = iota((bx, by), 0) + start_x
    col_y = iota((bx, by), 1) + start_y
    flat = []
    for k in range(views):
        within = (col_y >= box_ref[k * 6 + 4]) & (col_y < box_ref[k * 6 + 5])
        within = within & (row_x >= box_ref[k * 6 + 2]) & (row_x < box_ref[k * 6 + 3])
        flat.append(jnp.where(within, 1.0, 0.0))
    for plane in range(bz):
        coverage = jnp.zeros((bx, by), F32)
        for k in range(views):
            at = plane + start_z
            here = (at >= box_ref[k * 6 + 0]) & (at < box_ref[k * 6 + 1])
            coverage = coverage + jnp.where(here, 1.0, 0.0) * flat[k]
        share_ref[plane] = est_ref[plane] / coverage


def forward_body(views, block, counts, count_x, prof_ref, box_ref, cells_ref, halos_ref, yf_ref, yh_ref, xf_ref, *refs):
    x_refs, (gain_ref, side_halo, blurred_x, rows) = refs[:count_x], refs[count_x:]
    bz, bx, by = block
    deep = bz + 2 * PAD
    sides = []
    for swap, x_ref in enumerate(x_refs):
        index = lax.axis_index("bx")
        known = has_partner(index, counts[0], swap)
        after = meets_next(index, swap)
        sides.append((known & jnp.logical_not(after), known & after))
        groups = 2 * SIDE // PAD
        flat = [
            jnp.concatenate([x_ref[deep + groups * i + j].astype(F32) for j in range(groups)], axis=0)
            for i in range(deep * PAD // by)
        ]
        side_halo[swap] = jnp.concatenate(flat, axis=1).T.reshape(deep, PAD, 2 * SIDE)
    for plane in range(1, deep - 1):
        left = right = jnp.zeros((PAD, by), F32)
        left_halo = right_halo = jnp.zeros((PAD, 2 * SIDE), F32)
        for swap, (is_left, is_right) in enumerate(sides):
            came, came_halo = x_refs[swap][plane].astype(F32), side_halo[swap, plane]
            left = jnp.where(is_left, came, left)
            right = jnp.where(is_right, came, right)
            left_halo = jnp.where(is_left, came_halo, left_halo)
            right_halo = jnp.where(is_right, came_halo, right_halo)
        cells = jnp.concatenate([left, cells_ref[plane], right], axis=0).astype(BF16)
        halo = jnp.concatenate([left_halo, halos_ref[plane], right_halo], axis=0).astype(BF16)
        cells = jnp.concatenate([cells, halo], axis=1)
        cells = jnp.concatenate([cells, cells], axis=0)
        mixed = jnp.dot(xf_ref[...], cells, preferred_element_type=F32).astype(BF16)
        for k in range(views):
            blurred_x[k, plane * bx : (plane + 1) * bx, :] = mixed[k * bx : (k + 1) * bx]
    row_x = lax.broadcasted_iota(jnp.int32, (8, by), 0) + lax.axis_index("bx") * bx
    col_y = lax.broadcasted_iota(jnp.int32, (8, by), 1) + lax.axis_index("by") * by
    start_z = lax.axis_index("bz") * bz
    step = 10

    def view(k, carry):
        along_y = yf_ref[k]
        for first in range(1, deep - 1, step):
            mixed = jnp.dot(
                blurred_x[k, first * bx : (first + step) * bx, :], along_y, preferred_element_type=F32
            )
            rows[first : first + step] = (mixed[:, :by] + mixed[:, by:]).reshape(step, bx, by)
        taps = [prof_ref[(k * 3 + 0) * TAPS + tap] for tap in range(TAPS)]
        within_y = (col_y >= box_ref[k * 6 + 4]) & (col_y < box_ref[k * 6 + 5])
        inside = []
        for tile in range(0, bx, 8):
            at = row_x + tile
            inside.append(jnp.where(within_y & (at >= box_ref[k * 6 + 2]) & (at < box_ref[k * 6 + 3]), 1.0, 0.0))
        low_z = box_ref[k * 6 + 0] - start_z
        high_z = box_ref[k * 6 + 1] - start_z
        for first in range(0, bz, 4):
            some = (first + 4 > low_z) & (first < high_z)

            @pl.when(some)
            def _():
                for tile in range(0, bx, 8):
                    for plane in range(first, first + 4):
                        total = taps[0] * rows[plane + 1, tile : tile + 8, :]
                        for tap in range(1, TAPS):
                            total = total + taps[tap] * rows[plane + 1 + tap, tile : tile + 8, :]
                        here = jnp.where((plane >= low_z) & (plane < high_z), 1.0, 0.0)
                        gain_ref[k, plane, tile : tile + 8, :] = here * inside[tile // 8] / (total + BACKGROUND)

            @pl.when(jnp.logical_not(some))
            def _():
                gain_ref[k, first : first + 4] = jnp.zeros((4, bx, by), F32)

        return carry

    lax.fori_loop(0, views, view, 0)

    lane = lax.broadcasted_iota(jnp.int32, (8, by), 1)
    owner = lax.div(lane, 2 * PAD)
    col_y = lax.rem(lane, 2 * PAD)
    col_y = jnp.where(col_y < PAD, col_y - PAD, by + col_y - PAD) + lax.axis_index("by") * by

    def by_lane(value, start):
        for k in range(views):
            start = jnp.where(owner == k, value(k), start)
        return start

    taps = [by_lane(lambda k: prof_ref[(k * 3 + 0) * TAPS + tap], jnp.zeros((8, by), F32)) for tap in range(TAPS)]
    box = [by_lane(lambda k: box_ref[k * 6 + i], jnp.zeros((8, by), jnp.int32)) for i in range(6)]
    within_y = (col_y >= box[4]) & (col_y < box[5])
    step = 5
    for first in range(1, deep - 1, step):
        at = slice(first * bx, (first + step) * bx)
        mixed = jnp.dot(blurred_x[0, at, :], yh_ref[0], preferred_element_type=F32)
        for k in range(1, views):
            mixed = mixed + jnp.dot(blurred_x[k, at, :], yh_ref[k], preferred_element_type=F32)
        rows[first : first + step] = (mixed[:, :by] + mixed[:, by:]).reshape(step, bx, by)

    def beside_plane(plane, carry):
        at_z = plane + start_z
        within_z = within_y & (at_z >= box[0]) & (at_z < box[1])
        for tile in range(0, bx, 8):
            at_x = row_x + tile
            total = taps[0] * rows[plane + 1, tile : tile + 8, :]
            for tap in range(1, TAPS):
                total = total + taps[tap] * rows[plane + 1 + tap, tile : tile + 8, :]
            within = within_z & (at_x >= box[2]) & (at_x < box[3])
            gain_ref[views, plane, tile : tile + 8, :] = jnp.where(within, 1.0, 0.0) / (total + BACKGROUND)
        return carry

    lax.fori_loop(0, bz, beside_plane, 0)


def quotient_body(views, block, count, gain_ref, *refs):
    parts = refs[:count]
    quot_ref, held = refs[count:]
    bz, bx, by = block
    rows = bx // count
    mine = lax.axis_index("by") if count > 1 else 0

    def view(k, carry):
        for part, part_ref in zip(order_of(count), parts):
            at = pl.ds(pl.multiple_of((mine ^ part) * rows, rows), rows)
            held[:, at, :] = gain_ref[k, :, at, :] * part_ref[k].astype(F32)
        quot_ref[k] = held[...].astype(BF16)
        return carry

    lax.fori_loop(0, views + 1, view, 0)


def return_body(views, block, links, prof_ref, box_ref, quot_ref, yr_ref, xr_ref, mid_ref, *refs):
    bz, bx, by = block
    ext = bx + 2 * PAD
    deep = bz + 2 * REACH
    link_refs = refs[: len(links)]
    rows, high_rows, low_rows, total = refs[len(links) :]
    start_z = lax.axis_index("bz") * bz

    def view(k, carry):
        cells = [quot_ref[i].reshape(bz * bx, by) for i in (k, views)]
        cells = jnp.concatenate(cells, axis=1)
        mixed = jnp.dot(cells, yr_ref[k], preferred_element_type=F32)
        rows[...] = (mixed[:, :by] + mixed[:, by:]).reshape(bz, bx, by)
        taps = [prof_ref[(k * 3 + 0) * TAPS + tap] for tap in range(TAPS)]
        at = pl.ds(pl.multiple_of(k * bx, bx), bx)
        low_z = box_ref[k * 6 + 0] - start_z + REACH
        high_z = box_ref[k * 6 + 1] - start_z + REACH
        for first in range(0, deep, GROUP):
            some = (first + GROUP > low_z) & (first < high_z)

            @pl.when(some)
            def _():
                for tile in range(0, bx, 16):
                    for out in range(first, first + GROUP):
                        plane = out - REACH
                        parts = []
                        for half in (tile, tile + 8):
                            part = None
                            for source in range(max(0, plane - REACH), min(bz, plane + REACH + 1)):
                                term = taps[REACH - source + plane] * rows[source, half : half + 8, :]
                                part = term if part is None else part + term
                            parts.append(part)
                        here = jnp.where((out >= low_z) & (out < high_z), 1.0, 0.0)
                        high, low = halves(here * jnp.concatenate(parts, axis=0))
                        at_x = pl.ds(pl.multiple_of(k * bx + tile, 16), 16)
                        high_rows[out, at_x, :] = high
                        low_rows[out, at_x, :] = low

            @pl.when(jnp.logical_not(some))
            def _():
                high_rows[first : first + GROUP, at, :] = jnp.zeros((GROUP, bx, by), BF16)
                low_rows[first : first + GROUP, at, :] = jnp.zeros((GROUP, bx, by), BF16)

        return carry

    lax.fori_loop(0, views, view, 0)
    for out in range(0, deep, 2):
        high = jnp.concatenate([high_rows[out], high_rows[out + 1]], axis=1)
        low = jnp.concatenate([low_rows[out], low_rows[out + 1]], axis=1)
        mixed = jnp.dot(xr_ref[...], high, preferred_element_type=F32)
        mixed = mixed[:ext] + mixed[ext:] + jnp.dot(xr_ref[:ext], low, preferred_element_type=F32)
        total[out] = mixed[:, :by]
        total[out + 1] = mixed[:, by:]
    mid_ref[...] = total[REACH : REACH + bz, PAD : PAD + bx, :]
    for (x, z), link_ref in zip(links, link_refs):
        at_x, at_z = slice(PAD, PAD + bx), slice(REACH, REACH + bz)
        if x is not None:
            begin = jnp.where(meets_next(lax.axis_index("bx"), x), PAD + bx, 0)
            at_x = pl.ds(pl.multiple_of(begin, PAD), PAD)
        if z is not None:
            at_z = pl.ds(jnp.where(meets_next(lax.axis_index("bz"), z), REACH + bz, 0), REACH)
        link_ref[...] = total[at_z, at_x, :]


def finish_body(counts, links, share_ref, mid_ref, *refs):
    bz, bx, by = share_ref.shape
    link_refs, out_ref = refs[: len(links)], refs[len(links)]
    out_ref[...] = share_ref[...] * mid_ref[...]
    for (x, z), link_ref in zip(links, link_refs):
        at_x, at_z, known = slice(None), slice(None), None
        if x is not None:
            index = lax.axis_index("bx")
            begin = jnp.where(meets_next(index, x), bx - PAD, 0)
            at_x = pl.ds(pl.multiple_of(begin, PAD), PAD)
            known = has_partner(index, counts[0], x)
        if z is not None:
            index = lax.axis_index("bz")
            at_z = pl.ds(jnp.where(meets_next(index, z), bz - REACH, 0), REACH)
            there = has_partner(index, counts[1], z)
            known = there if known is None else known & there

        @pl.when(known)
        def _():
            out_ref[at_z, at_x, :] = out_ref[at_z, at_x, :] + share_ref[at_z, at_x, :] * link_ref[...]


def local(estimate, recorded, profiles, view_boxes):
    block = estimate.shape
    bz, bx, by = block
    views = recorded.shape[0]
    part_rows = recorded.shape[2]
    count = lax.axis_size("by")
    counts = (lax.axis_size("bx"), lax.axis_size("bz"))
    links = links_of(*counts)
    ext = bx + 2 * PAD
    deep = bz + 2 * PAD
    shape = jax.ShapeDtypeStruct
    profiles, view_boxes = profiles.reshape(-1), view_boxes.reshape(-1)

    def link_shape(link, reach, dtype):
        x, z = link
        return shape((bz if z is None else reach, bx if x is None else PAD, by), dtype)

    side = shape((SIDE, bz * bx), BF16)
    own, order, second = call(
        columns_body,
        [shape(block, BF16), side, side],
        [VMEM],
        nbytes=bz * bx * by * 4,
        name="columns",
    )(estimate)
    first, second = exchange_y(order, second)

    if count & (count - 1) == 0 and count <= 4 and part_rows % 8 == 0:
        parts = [*call(
            pieces_body,
            [shape((views + 1, bz, part_rows, by), BF16)] * count,
            [ANY, VMEM],
            nbytes=views * bz * bx * by * 4,
            name="pieces",
        )(order, recorded)]
        for other in range(1, count):
            parts[other] = lax.ppermute(parts[other], "by", [(i, i ^ other) for i in range(count)])
    else:
        tiles = jnp.moveaxis(recorded.reshape(views, bz, part_rows, count, by), 3, 0)
        before = jnp.roll(tiles[..., by - PAD :], 1, axis=0)
        after = jnp.roll(tiles[..., :PAD], -1, axis=0)
        beside = jnp.moveaxis(jnp.concatenate([before, after], axis=-1), 1, 3)
        beside = beside.reshape(count, 1, bz, part_rows, views * 2 * PAD)
        beside = jnp.pad(beside, [(0, 0)] * 4 + [(0, by - views * 2 * PAD)])
        tiles = jnp.concatenate([tiles, beside], axis=1)
        tiles = lax.all_to_all(tiles, "by", split_axis=0, concat_axis=0, tiled=True)
        parts = [jnp.moveaxis(tiles, 0, 2).reshape(views + 1, bz, bx, by)]

    along_x, along_z = swaps_of(counts[0]), swaps_of(counts[1])
    halo, *edges = call(
        functools.partial(edges_body, count),
        [shape((bz * bx, 2 * SIDE), BF16)]
        + [shape((PAD + PAD * bx // by, bx, by), BF16)] * len(along_z),
        [VMEM] * 3,
        nbytes=bz * bx * by * 4,
        name="edges",
    )(own, first, second)
    edges = [exchange(cells, (None, swap), *counts) for swap, cells in zip(along_z, edges)]

    cells, halos, *edges = call(
        functools.partial(deep_body, counts, len(along_z)),
        [shape((deep, bx, by), F32), shape((deep, bx, 2 * SIDE), F32)]
        + [shape((deep + 2 * SIDE * deep // by, PAD, by), BF16)] * len(along_x),
        [ANY] + [VMEM] * (2 + len(along_z)),
        nbytes=deep * bx * by * 4,
        name="deep",
    )(own, own, halo, *edges)
    edges = [exchange(cells, (swap, None), *counts) for swap, cells in zip(along_x, edges)]

    yf, yh, xf = call(
        functools.partial(forward_bands_body, views, block),
        [
            shape((views, by + 2 * SIDE, 2 * by), BF16),
            shape((views, by + 2 * SIDE, 2 * by), BF16),
            shape((views * bx, 2 * ext), BF16),
        ],
        [ANY, SMEM],
        flops=views * 32 * by * by,
        nbytes=views * by * by * 4,
        name="forward_bands",
    )(order, profiles)

    gain = call(
        functools.partial(forward_body, views, block, counts, len(along_x)),
        shape((views + 1, bz, bx, by), F32),
        [SMEM] * 2 + [VMEM] * (5 + len(along_x)),
        [
            pltpu.VMEM((max(1, len(along_x)), deep, PAD, 2 * SIDE), F32),
            pltpu.VMEM((views, deep * bx, by + 2 * SIDE), BF16),
            pltpu.VMEM((deep, bx, by), F32),
        ],
        flops=views * deep * ext * by * 600,
        nbytes=views * bz * bx * by * 8,
        name="forward",
    )(profiles, view_boxes, cells, halos, yf, yh, xf, *edges)

    yr, xr, share = call(
        functools.partial(return_bands_body, views),
        [
            shape((views, 2 * by, 2 * by), BF16),
            shape((2 * ext, views * bx), BF16),
            shape(block, F32),
        ],
        [ANY] + [SMEM] * 2 + [VMEM],
        flops=views * 32 * by * by,
        nbytes=views * by * by * 4,
        name="return_bands",
    )(gain, profiles, view_boxes, estimate)
    quot = call(
        functools.partial(quotient_body, views, block, len(parts)),
        shape((views + 1, bz, bx, by), BF16),
        [VMEM] * (1 + len(parts)),
        [pltpu.VMEM((bz, bx, by), F32)],
        flops=views * bz * bx * by * 40,
        nbytes=views * bz * bx * by * 8,
        name="quotient",
    )(gain, *[parts[part] for part in order_of(len(parts))])

    mid, *sums = call(
        functools.partial(return_body, views, block, links),
        [shape(block, F32)] + [link_shape(link, REACH, F32) for link in links],
        [SMEM] * 2 + [VMEM] * 3,
        [
            pltpu.VMEM((bz, bx, by), F32),
            pltpu.VMEM((bz + 2 * REACH, views * bx, by), BF16),
            pltpu.VMEM((bz + 2 * REACH, views * bx, by), BF16),
            pltpu.VMEM((bz + 2 * REACH, ext, by), F32),
        ],
        flops=views * bz * ext * by * 600,
        nbytes=views * bz * bx * by * 8,
        name="returned",
    )(profiles, view_boxes, quot, yr, xr)
    sums = [exchange(cells, link, *counts) for link, cells in zip(links, sums)]
    return call(
        functools.partial(finish_body, counts, links),
        shape(block, F32),
        [VMEM] * (2 + len(links)),
        nbytes=bz * bx * by * 12,
        name="finish",
    )(share, mid, *sums)


def solution(mesh):
    placed = (
        P(("groups", "bz"), "bx", "by"),
        P(None, ("groups", "bz"), ("bx", "by"), None),
        P(),
        P("groups", None),
    )
    return jax.shard_map(
        local,
        mesh=mesh,
        in_specs=placed,
        out_specs=P(("groups", "bz"), "bx", "by"),
        check_vma=False,
    )
```

```python
import functools

import jax
import jax.numpy as jnp
from jax import lax
from jax.experimental import pallas as pl
from jax.experimental.pallas import tpu as pltpu
from jax.sharding import PartitionSpec as P

TAPS = 15
REACH = TAPS // 2
PAD = 8
SIDE = 2 * PAD
BACKGROUND = 0.05
GROUP = 6
WEIGHT = 0.5

F32 = jnp.float32
BF16 = jnp.bfloat16

VMEM = pl.BlockSpec(memory_space=pltpu.VMEM)
SMEM = pl.BlockSpec(memory_space=pltpu.SMEM)
ANY = pl.BlockSpec(memory_space=pl.ANY)
HBM = pl.BlockSpec(memory_space=pltpu.HBM)


def call(body, out_shape, in_specs, scratch=(), flops=0, nbytes=0, name=None):
    many = isinstance(out_shape, (list, tuple))
    return pl.pallas_call(
        body,
        out_shape=out_shape,
        in_specs=in_specs,
        out_specs=[VMEM] * len(out_shape) if many else VMEM,
        scratch_shapes=list(scratch),
        compiler_params=pltpu.CompilerParams(vmem_limit_bytes=40 * 1024 * 1024),
        cost_estimate=pl.CostEstimate(
            flops=int(WEIGHT * flops), bytes_accessed=int(WEIGHT * nbytes), transcendentals=0
        ),
        name=name,
    )


def partner(index, count, swap):
    other = index ^ 1 if swap == 0 else ((index + 1) ^ 1) - 1
    return other if 0 <= other < count else index


def swaps_of(count):
    return {1: [], 2: [0]}.get(count, [0, 1])


def meets_next(index, swap):
    return lax.rem(index + swap, 2) == 0


def has_partner(index, count, swap):
    after = meets_next(index, swap)
    return jnp.where(after, index < count - 1, index > 0)


def links_of(count_x, count_z):
    along_x, along_z = [None, *swaps_of(count_x)], [None, *swaps_of(count_z)]
    return [(x, z) for x in along_x for z in along_z if (x, z) != (None, None)]


def exchange(cells, link, count_x, count_z):
    x, z = link
    pairs = []
    for i in range(count_x):
        for j in range(count_z):
            to_x = i if x is None else partner(i, count_x, x)
            to_z = j if z is None else partner(j, count_z, z)
            pairs.append((i * count_z + j, to_x * count_z + to_z))
    return lax.ppermute(cells, ("bx", "bz"), pairs)


def exchange_y(first, second):
    count = lax.axis_size("by")
    return [
        lax.ppermute(cells, "by", [(i, partner(i, count, swap)) for i in range(count)])
        for swap, cells in enumerate((first, second))
    ]


def banded(offset, tap_of):
    matrix = jnp.zeros(offset.shape, F32)
    for tap in range(TAPS):
        matrix = jnp.where(offset == tap, tap_of(tap), matrix)
    return matrix


def halves(matrix):
    high = matrix.astype(BF16)
    return high, (matrix - high.astype(F32)).astype(BF16)


def packed(cells, begin):
    by = cells.shape[1]
    row = lax.broadcasted_iota(jnp.int32, (SIDE, by), 0)
    col = lax.broadcasted_iota(jnp.int32, (SIDE, by), 1)
    pick = jnp.where(col == row + begin, 1.0, 0.0).astype(BF16)
    return lax.dot_general(
        pick, cells, (((1,), (1,)), ((), ())), preferred_element_type=F32
    ).astype(BF16)


def unpack_both(count, first_ref, second_ref):
    mine = lax.axis_index("by")
    first, second = first_ref[...].astype(F32), second_ref[...].astype(F32)
    even = meets_next(mine, 0)
    before = jnp.where(even, second, first)
    after = jnp.where(even, first, second)
    before = jnp.where(mine > 0, before, 0.0)
    after = jnp.where(mine < count - 1, after, 0.0)
    return jnp.concatenate([before, after], axis=0).T.astype(BF16)


def columns_body(est_ref, cells_ref, first_ref, second_ref):
    bz, bx, by = est_ref.shape
    cells_ref[...] = est_ref[...].astype(BF16)
    cells = cells_ref[...].reshape(bz * bx, by)
    mine = lax.axis_index("by")
    first_ref[...] = packed(cells, jnp.where(meets_next(mine, 0), by - SIDE, 0))
    second_ref[...] = packed(cells, jnp.where(meets_next(mine, 1), by - SIDE, 0))


def pieces_body(order_ref, rec_ref, *out_refs):
    views, bz, rows, width = rec_ref.shape
    count = len(out_refs)
    by = width // count
    row = lax.broadcasted_iota(jnp.int32, (by, by), 0)
    col = lax.broadcasted_iota(jnp.int32, (by, by), 1)
    picks = []
    for k in range(views):
        lane = col - 2 * PAD * k
        picks.append((lane >= 0) & (lane < PAD) & (row == by - PAD + lane))
        picks.append((lane >= PAD) & (lane < 2 * PAD) & (row == lane - PAD))
    picks = jnp.concatenate([jnp.where(pick, 1.0, 0.0).astype(BF16) for pick in picks], axis=0)
    for other, out_ref in enumerate(out_refs):
        target = lax.axis_index("by") ^ other

        def columns(tile):
            return pl.ds(pl.multiple_of(jnp.clip(tile, 0, count - 1) * by, by), by)

        out_ref[:views] = rec_ref[:, :, :, columns(target)]
        beside = []
        for k in range(views):
            for tile in (target - 1, target + 1):
                cells = rec_ref[k, :, :, columns(tile)]
                beside.append(cells.astype(F32).reshape(bz * rows, by).astype(BF16))
        beside = jnp.dot(jnp.concatenate(beside, axis=1), picks, preferred_element_type=F32)
        out_ref[views] = beside.reshape(bz, rows, by).astype(BF16)


def upright(cells):
    return cells.astype(F32).T


def lying(cells):
    wide = cells.shape[1]
    row = lax.broadcasted_iota(jnp.int32, (wide, wide), 0)
    col = lax.broadcasted_iota(jnp.int32, (wide, wide), 1)
    same = jnp.where(row == col, 1.0, 0.0).astype(BF16)
    return lax.dot_general(
        same, cells.astype(BF16), (((1,), (1,)), ((), ())), preferred_element_type=F32
    )


def edges_body(count, est_ref, first_ref, second_ref, halo_ref, *out_refs):
    bz, bx, by = est_ref.shape
    halo_ref[...] = unpack_both(count, first_ref, second_ref)
    for swap, out_ref in enumerate(out_refs):
        begin = jnp.where(meets_next(lax.axis_index("bz"), swap), bz - PAD, 0)
        out_ref[:PAD] = est_ref[pl.ds(begin, PAD)]
        rows = halo_ref[pl.ds(pl.multiple_of(begin * bx, PAD * bx), PAD * bx), :]
        flat = lying(rows).astype(BF16)
        for i in range(PAD * bx // by):
            out_ref[PAD + i, : 2 * SIDE, :] = flat[:, i * by : (i + 1) * by]


def deep_body(counts, count_z, order_ref, est_ref, halo_ref, *refs):
    bz, bx, by = est_ref.shape
    deep = bz + 2 * PAD
    z_refs, (cells_ref, halos_ref, *out_refs) = refs[:count_z], refs[count_z:]
    cells_ref[...] = jnp.zeros_like(cells_ref)
    halos_ref[...] = jnp.zeros_like(halos_ref)
    cells_ref[PAD : PAD + bz] = est_ref[...].astype(F32)
    halos_ref[PAD : PAD + bz] = halo_ref[...].astype(F32).reshape(bz, bx, 2 * SIDE)
    for swap, z_ref in enumerate(z_refs):
        index = lax.axis_index("bz")
        at = pl.ds(jnp.where(meets_next(index, swap), PAD + bz, 0), PAD)

        @pl.when(has_partner(index, counts[1], swap))
        def _():
            cells_ref[at] = z_ref[:PAD].astype(F32)
            flat = jnp.concatenate(
                [z_ref[PAD + i, : 2 * SIDE, :] for i in range(PAD * bx // by)], axis=1
            )
            halos_ref[at] = upright(flat).reshape(PAD, bx, 2 * SIDE)

    for swap, out_ref in enumerate(out_refs):
        begin = jnp.where(meets_next(lax.axis_index("bx"), swap), bx - PAD, 0)
        at = pl.ds(pl.multiple_of(begin, PAD), PAD)
        out_ref[:deep] = cells_ref[:, at, :].astype(BF16)
        flat = lying(halos_ref[:, at, :].reshape(deep * PAD, 2 * SIDE))
        groups = 2 * SIDE // PAD
        for i in range(deep * PAD // by):
            for j in range(groups):
                part = flat[j * PAD : (j + 1) * PAD, i * by : (i + 1) * by]
                out_ref[deep + groups * i + j] = part.astype(BF16)


def iota(shape, dim):
    return lax.broadcasted_iota(jnp.int32, shape, dim)


def forward_bands_body(views, block, order_ref, prof_ref, yf_ref, yh_ref, xf_ref):
    bz, bx, by = block
    ext = bx + 2 * PAD
    shape_y = (by + 2 * SIDE, by)
    row = iota(shape_y, 0)
    source = jnp.where(row < by, row, jnp.where(row < by + SIDE, row - by - SIDE, row - SIDE))
    target = iota(shape_y, 1)
    beside_view = lax.div(target, 2 * PAD)
    beside = lax.rem(target, 2 * PAD)
    beside = jnp.where(beside < PAD, beside - PAD, by + beside - PAD)
    shape_x = (bx, 2 * ext)
    col = iota(shape_x, 1)
    is_low = col >= ext
    forward_x = jnp.where(is_low, col - ext, col) - PAD - iota(shape_x, 0)

    def view(k, carry):
        forward = banded(source - target + REACH, lambda tap: prof_ref[(k * 3 + 2) * TAPS + tap])
        high, low = halves(forward)
        yf_ref[k, :, :by] = high
        yf_ref[k, :, by:] = low
        forward = banded(source - beside + REACH, lambda tap: prof_ref[(k * 3 + 2) * TAPS + tap])
        high, low = halves(jnp.where(beside_view == k, forward, 0.0))
        yh_ref[k, :, :by] = high
        yh_ref[k, :, by:] = low
        high, low = halves(banded(forward_x + REACH, lambda tap: prof_ref[(k * 3 + 1) * TAPS + tap]))
        at = pl.ds(pl.multiple_of(k * bx, bx), bx)
        xf_ref[at, :] = jnp.where(is_low, low.astype(F32), high.astype(F32)).astype(BF16)
        return carry

    lax.fori_loop(0, views, view, 0)


def return_bands_body(views, paired, order_ref, prof_ref, box_ref, est_ref, yr_ref, xr_ref, share_ref):
    bz, bx, by = est_ref.shape
    ext = bx + 2 * PAD
    start_z = lax.axis_index("bz") * bz
    start_x = lax.axis_index("bx") * bx
    start_y = lax.axis_index("by") * by
    back_row, back_target = iota((by, by), 0), iota((by, by), 1)
    side_row, side_target = iota((2 * PAD, by), 0), iota((2 * PAD, by), 1)
    side_row = jnp.where(side_row < PAD, side_row - PAD, by + side_row - PAD)

    def view(k, carry):
        def back(row, target):
            within = (target >= box_ref[k * 6 + 4] - start_y) & (target < box_ref[k * 6 + 5] - start_y)
            matrix = banded(REACH - row + target, lambda tap: prof_ref[(k * 3 + 2) * TAPS + tap])
            return halves(jnp.where(within, matrix, 0.0))

        high, low = back(back_row, back_target)
        yr_ref[k, :by, :by] = high
        yr_ref[k, :by, by:] = low
        yr_ref[k, by:, :] = jnp.zeros((by, 2 * by), BF16)
        at = pl.ds(pl.multiple_of(by + 2 * PAD * k, 2 * PAD), 2 * PAD)
        high, low = back(side_row, side_target)
        yr_ref[k, at, :by] = high
        yr_ref[k, at, by:] = low
        return carry

    lax.fori_loop(0, views, view, 0)

    half_rows = bx // 2
    shape_x = (ext, views * bx)
    target = iota(shape_x, 0) - PAD
    col = iota(shape_x, 1)
    slot = lax.div(col, views * half_rows)
    half = jnp.where(slot == 0, half_of(0, paired), half_of(1, paired))
    owner = lax.div(lax.rem(col, views * half_rows), half_rows)
    source = half * half_rows + lax.rem(col, half_rows)

    def back_view(k, matrix):
        back = banded(REACH - source + target, lambda tap: prof_ref[(k * 3 + 1) * TAPS + tap])
        within = (target >= box_ref[k * 6 + 2] - start_x) & (target < box_ref[k * 6 + 3] - start_x)
        return jnp.where(owner == k, jnp.where(within, back, 0.0), matrix)

    high, low = halves(lax.fori_loop(0, views, back_view, jnp.zeros(shape_x, F32)))
    xr_ref[:ext] = high
    xr_ref[ext:] = low

    row_x = iota((bx, by), 0) + start_x
    col_y = iota((bx, by), 1) + start_y
    flat = []
    for k in range(views):
        within = (col_y >= box_ref[k * 6 + 4]) & (col_y < box_ref[k * 6 + 5])
        within = within & (row_x >= box_ref[k * 6 + 2]) & (row_x < box_ref[k * 6 + 3])
        flat.append(jnp.where(within, 1.0, 0.0))
    for plane in range(bz):
        coverage = jnp.zeros((bx, by), F32)
        for k in range(views):
            at = plane + start_z
            here = (at >= box_ref[k * 6 + 0]) & (at < box_ref[k * 6 + 1])
            coverage = coverage + jnp.where(here, 1.0, 0.0) * flat[k]
        share_ref[plane] = est_ref[plane] / coverage


def forward_body(views, block, counts, count_x, prof_ref, box_ref, cells_ref, halos_ref, yf_ref, yh_ref, xf_ref, *refs):
    x_refs, (gain_ref, side_halo, blurred_x, rows) = refs[:count_x], refs[count_x:]
    bz, bx, by = block
    deep = bz + 2 * PAD
    sides = []
    for swap, x_ref in enumerate(x_refs):
        index = lax.axis_index("bx")
        known = has_partner(index, counts[0], swap)
        after = meets_next(index, swap)
        sides.append((known & jnp.logical_not(after), known & after))
        groups = 2 * SIDE // PAD
        flat = [
            jnp.concatenate([x_ref[deep + groups * i + j].astype(F32) for j in range(groups)], axis=0)
            for i in range(deep * PAD // by)
        ]
        side_halo[swap] = jnp.concatenate(flat, axis=1).T.reshape(deep, PAD, 2 * SIDE)
    for plane in range(1, deep - 1):
        left = right = jnp.zeros((PAD, by), F32)
        left_halo = right_halo = jnp.zeros((PAD, 2 * SIDE), F32)
        for swap, (is_left, is_right) in enumerate(sides):
            came, came_halo = x_refs[swap][plane].astype(F32), side_halo[swap, plane]
            left = jnp.where(is_left, came, left)
            right = jnp.where(is_right, came, right)
            left_halo = jnp.where(is_left, came_halo, left_halo)
            right_halo = jnp.where(is_right, came_halo, right_halo)
        cells = jnp.concatenate([left, cells_ref[plane], right], axis=0).astype(BF16)
        halo = jnp.concatenate([left_halo, halos_ref[plane], right_halo], axis=0).astype(BF16)
        cells = jnp.concatenate([cells, halo], axis=1)
        cells = jnp.concatenate([cells, cells], axis=0)
        mixed = jnp.dot(xf_ref[...], cells, preferred_element_type=F32).astype(BF16)
        for k in range(views):
            blurred_x[k, plane * bx : (plane + 1) * bx, :] = mixed[k * bx : (k + 1) * bx]
    row_x = lax.broadcasted_iota(jnp.int32, (8, by), 0) + lax.axis_index("bx") * bx
    col_y = lax.broadcasted_iota(jnp.int32, (8, by), 1) + lax.axis_index("by") * by
    start_z = lax.axis_index("bz") * bz
    step = 10

    def view(k, carry):
        along_y = yf_ref[k]
        for first in range(1, deep - 1, step):
            mixed = jnp.dot(
                blurred_x[k, first * bx : (first + step) * bx, :], along_y, preferred_element_type=F32
            )
            rows[first : first + step] = (mixed[:, :by] + mixed[:, by:]).reshape(step, bx, by)
        taps = [prof_ref[(k * 3 + 0) * TAPS + tap] for tap in range(TAPS)]
        within_y = (col_y >= box_ref[k * 6 + 4]) & (col_y < box_ref[k * 6 + 5])
        inside = []
        for tile in range(0, bx, 8):
            at = row_x + tile
            inside.append(jnp.where(within_y & (at >= box_ref[k * 6 + 2]) & (at < box_ref[k * 6 + 3]), 1.0, 0.0))
        low_z = box_ref[k * 6 + 0] - start_z
        high_z = box_ref[k * 6 + 1] - start_z
        for first in range(0, bz, 4):
            some = (first + 4 > low_z) & (first < high_z)

            @pl.when(some)
            def _():
                for tile in range(0, bx, 8):
                    for plane in range(first, first + 4):
                        total = taps[0] * rows[plane + 1, tile : tile + 8, :]
                        for tap in range(1, TAPS):
                            total = total + taps[tap] * rows[plane + 1 + tap, tile : tile + 8, :]
                        here = jnp.where((plane >= low_z) & (plane < high_z), 1.0, 0.0)
                        gain_ref[k, plane, tile : tile + 8, :] = here * inside[tile // 8] / (total + BACKGROUND)

            @pl.when(jnp.logical_not(some))
            def _():
                gain_ref[k, first : first + 4] = jnp.zeros((4, bx, by), F32)

        return carry

    lax.fori_loop(0, views, view, 0)

    lane = lax.broadcasted_iota(jnp.int32, (8, by), 1)
    owner = lax.div(lane, 2 * PAD)
    col_y = lax.rem(lane, 2 * PAD)
    col_y = jnp.where(col_y < PAD, col_y - PAD, by + col_y - PAD) + lax.axis_index("by") * by

    def by_lane(value, start):
        for k in range(views):
            start = jnp.where(owner == k, value(k), start)
        return start

    taps = [by_lane(lambda k: prof_ref[(k * 3 + 0) * TAPS + tap], jnp.zeros((8, by), F32)) for tap in range(TAPS)]
    box = [by_lane(lambda k: box_ref[k * 6 + i], jnp.zeros((8, by), jnp.int32)) for i in range(6)]
    within_y = (col_y >= box[4]) & (col_y < box[5])
    step = 5
    for first in range(1, deep - 1, step):
        at = slice(first * bx, (first + step) * bx)
        mixed = jnp.dot(blurred_x[0, at, :], yh_ref[0], preferred_element_type=F32)
        for k in range(1, views):
            mixed = mixed + jnp.dot(blurred_x[k, at, :], yh_ref[k], preferred_element_type=F32)
        rows[first : first + step] = (mixed[:, :by] + mixed[:, by:]).reshape(step, bx, by)

    def beside_plane(plane, carry):
        at_z = plane + start_z
        within_z = within_y & (at_z >= box[0]) & (at_z < box[1])
        for tile in range(0, bx, 8):
            at_x = row_x + tile
            total = taps[0] * rows[plane + 1, tile : tile + 8, :]
            for tap in range(1, TAPS):
                total = total + taps[tap] * rows[plane + 1 + tap, tile : tile + 8, :]
            within = within_z & (at_x >= box[2]) & (at_x < box[3])
            gain_ref[views, plane, tile : tile + 8, :] = jnp.where(within, 1.0, 0.0) / (total + BACKGROUND)
        return carry

    lax.fori_loop(0, bz, beside_plane, 0)


def half_of(slot, paired):
    return lax.div(lax.axis_index("by"), 2) ^ slot if paired else slot


def half_body(views, block, slot, paired, count, prof_ref, box_ref, gain_ref, yr_ref, *refs):
    parts = refs[:count]
    high_ref, low_ref, quot, held, rows = refs[count:]
    bz, bx, by = block
    deep = bz + 2 * REACH
    half_rows = bx // 2
    part_rows = half_rows // count
    begin = half_of(slot, paired) * half_rows
    start_z = lax.axis_index("bz") * bz

    def quotient(k, carry):
        for i, part_ref in enumerate(parts):
            at = lax.rem(lax.axis_index("by") ^ i, 2) * part_rows if count == 2 else 0
            gain = gain_ref[k, :, pl.ds(pl.multiple_of(begin + at, 8), part_rows), :]
            at = pl.ds(pl.multiple_of(at, 8), part_rows)
            held[:, at, :] = gain * part_ref[k].astype(F32)
        quot[k] = held[...].astype(BF16)
        return carry

    lax.fori_loop(0, views + 1, quotient, 0)

    def view(k, carry):
        cells = [quot[i].reshape(bz * half_rows, by) for i in (k, views)]
        cells = jnp.concatenate(cells, axis=1)
        mixed = jnp.dot(cells, yr_ref[k], preferred_element_type=F32)
        rows[...] = (mixed[:, :by] + mixed[:, by:]).reshape(bz, half_rows, by)
        taps = [prof_ref[(k * 3 + 0) * TAPS + tap] for tap in range(TAPS)]
        at = pl.ds(pl.multiple_of(k * half_rows, half_rows), half_rows)
        low_z = box_ref[k * 6 + 0] - start_z + REACH
        high_z = box_ref[k * 6 + 1] - start_z + REACH
        for first in range(0, deep, GROUP):
            some = (first + GROUP > low_z) & (first < high_z)

            @pl.when(some)
            def _():
                for out in range(first, first + GROUP):
                    plane = out - REACH
                    parts = []
                    for tile in range(0, half_rows, 8):
                        part = None
                        for source in range(max(0, plane - REACH), min(bz, plane + REACH + 1)):
                            term = taps[REACH - source + plane] * rows[source, tile : tile + 8, :]
                            part = term if part is None else part + term
                        parts.append(part)
                    here = jnp.where((out >= low_z) & (out < high_z), 1.0, 0.0)
                    high, low = halves(here * jnp.concatenate(parts, axis=0))
                    high_ref[out, at, :] = high
                    low_ref[out, at, :] = low

            @pl.when(jnp.logical_not(some))
            def _():
                high_ref[first : first + GROUP, at, :] = jnp.zeros((GROUP, half_rows, by), BF16)
                low_ref[first : first + GROUP, at, :] = jnp.zeros((GROUP, half_rows, by), BF16)

        return carry

    lax.fori_loop(0, views, view, 0)


def return_body(block, links, xr_ref, *refs):
    rows_refs, mid_ref, link_refs, total = refs[:4], refs[4], refs[5:-1], refs[-1]
    bz, bx, by = block
    ext = bx + 2 * PAD
    deep = bz + 2 * REACH

    def both(first_ref, second_ref, out):
        planes = [
            jnp.concatenate([first_ref[i], second_ref[i]], axis=0) for i in (out, out + 1)
        ]
        return jnp.concatenate(planes, axis=1)

    for out in range(0, deep, 2):
        high = both(rows_refs[0], rows_refs[2], out)
        low = both(rows_refs[1], rows_refs[3], out)
        mixed = jnp.dot(xr_ref[...], high, preferred_element_type=F32)
        mixed = mixed[:ext] + mixed[ext:] + jnp.dot(xr_ref[:ext], low, preferred_element_type=F32)
        total[out] = mixed[:, :by]
        total[out + 1] = mixed[:, by:]
    mid_ref[...] = total[REACH : REACH + bz, PAD : PAD + bx, :]
    for (x, z), link_ref in zip(links, link_refs):
        at_x, at_z = slice(PAD, PAD + bx), slice(REACH, REACH + bz)
        if x is not None:
            begin = jnp.where(meets_next(lax.axis_index("bx"), x), PAD + bx, 0)
            at_x = pl.ds(pl.multiple_of(begin, PAD), PAD)
        if z is not None:
            at_z = pl.ds(jnp.where(meets_next(lax.axis_index("bz"), z), REACH + bz, 0), REACH)
        link_ref[...] = total[at_z, at_x, :]


def finish_body(counts, links, share_ref, mid_ref, *refs):
    bz, bx, by = share_ref.shape
    link_refs, out_ref = refs[: len(links)], refs[len(links)]
    out_ref[...] = share_ref[...] * mid_ref[...]
    for (x, z), link_ref in zip(links, link_refs):
        at_x, at_z, known = slice(None), slice(None), None
        if x is not None:
            index = lax.axis_index("bx")
            begin = jnp.where(meets_next(index, x), bx - PAD, 0)
            at_x = pl.ds(pl.multiple_of(begin, PAD), PAD)
            known = has_partner(index, counts[0], x)
        if z is not None:
            index = lax.axis_index("bz")
            at_z = pl.ds(jnp.where(meets_next(index, z), bz - REACH, 0), REACH)
            there = has_partner(index, counts[1], z)
            known = there if known is None else known & there

        @pl.when(known)
        def _():
            out_ref[at_z, at_x, :] = out_ref[at_z, at_x, :] + share_ref[at_z, at_x, :] * link_ref[...]


def local(estimate, recorded, profiles, view_boxes):
    block = estimate.shape
    bz, bx, by = block
    views = recorded.shape[0]
    part_rows = recorded.shape[2]
    count = lax.axis_size("by")
    counts = (lax.axis_size("bx"), lax.axis_size("bz"))
    links = links_of(*counts)
    ext = bx + 2 * PAD
    deep = bz + 2 * PAD
    shape = jax.ShapeDtypeStruct
    profiles, view_boxes = profiles.reshape(-1), view_boxes.reshape(-1)

    def link_shape(link, reach, dtype):
        x, z = link
        return shape((bz if z is None else reach, bx if x is None else PAD, by), dtype)

    side = shape((SIDE, bz * bx), BF16)
    own, order, second = call(
        columns_body,
        [shape(block, BF16), side, side],
        [VMEM],
        nbytes=bz * bx * by * 4,
        name="columns",
    )(estimate)
    first, second = exchange_y(order, second)

    if count == 4 and part_rows % 8 == 0:
        parts = [*call(
            pieces_body,
            [shape((views + 1, bz, part_rows, by), BF16)] * count,
            [ANY, VMEM],
            nbytes=views * bz * bx * by * 4,
            name="pieces",
        )(order, recorded)]
        parts[1] = lax.ppermute(parts[1], "by", [(i, i ^ 1) for i in range(count)])
        parts[2:], first, second = lax.optimization_barrier((parts[2:], first, second))
        for other in range(2, count):
            parts[other] = lax.ppermute(parts[other], "by", [(i, i ^ other) for i in range(count)])
    else:
        tiles = jnp.moveaxis(recorded.reshape(views, bz, part_rows, count, by), 3, 0)
        before = jnp.roll(tiles[..., by - PAD :], 1, axis=0)
        after = jnp.roll(tiles[..., :PAD], -1, axis=0)
        beside = jnp.moveaxis(jnp.concatenate([before, after], axis=-1), 1, 3)
        beside = beside.reshape(count, 1, bz, part_rows, views * 2 * PAD)
        beside = jnp.pad(beside, [(0, 0)] * 4 + [(0, by - views * 2 * PAD)])
        tiles = jnp.concatenate([tiles, beside], axis=1)
        tiles = lax.all_to_all(tiles, "by", split_axis=0, concat_axis=0, tiled=True)
        parts = [jnp.moveaxis(tiles, 0, 2).reshape(views + 1, bz, bx, by)]

    paired = len(parts) == 4
    if paired:
        halves_of = [parts[:2], parts[2:]]
    else:
        halves_of = [[parts[0][:, :, : bx // 2]], [parts[0][:, :, bx // 2 :]]]

    along_x, along_z = swaps_of(counts[0]), swaps_of(counts[1])
    halo, *edges = call(
        functools.partial(edges_body, count),
        [shape((bz * bx, 2 * SIDE), BF16)]
        + [shape((PAD + PAD * bx // by, bx, by), BF16)] * len(along_z),
        [VMEM] * 3,
        nbytes=bz * bx * by * 4,
        name="edges",
    )(own, first, second)
    edges = [exchange(cells, (None, swap), *counts) for swap, cells in zip(along_z, edges)]

    cells, halos, *edges = call(
        functools.partial(deep_body, counts, len(along_z)),
        [shape((deep, bx, by), F32), shape((deep, bx, 2 * SIDE), F32)]
        + [shape((deep + 2 * SIDE * deep // by, PAD, by), BF16)] * len(along_x),
        [ANY] + [VMEM] * (2 + len(along_z)),
        nbytes=deep * bx * by * 4,
        name="deep",
    )(own, own, halo, *edges)
    edges = [exchange(cells, (swap, None), *counts) for swap, cells in zip(along_x, edges)]

    yf, yh, xf = call(
        functools.partial(forward_bands_body, views, block),
        [
            shape((views, by + 2 * SIDE, 2 * by), BF16),
            shape((views, by + 2 * SIDE, 2 * by), BF16),
            shape((views * bx, 2 * ext), BF16),
        ],
        [ANY, SMEM],
        flops=views * 32 * by * by,
        nbytes=views * by * by * 4,
        name="forward_bands",
    )(order, profiles)

    gain = call(
        functools.partial(forward_body, views, block, counts, len(along_x)),
        shape((views + 1, bz, bx, by), F32),
        [SMEM] * 2 + [VMEM] * (5 + len(along_x)),
        [
            pltpu.VMEM((max(1, len(along_x)), deep, PAD, 2 * SIDE), F32),
            pltpu.VMEM((views, deep * bx, by + 2 * SIDE), BF16),
            pltpu.VMEM((deep, bx, by), F32),
        ],
        flops=views * deep * ext * by * 600,
        nbytes=views * bz * bx * by * 8,
        name="forward",
    )(profiles, view_boxes, cells, halos, yf, yh, xf, *edges)

    yr, xr, share = call(
        functools.partial(return_bands_body, views, paired),
        [
            shape((views, 2 * by, 2 * by), BF16),
            shape((2 * ext, views * bx), BF16),
            shape(block, F32),
        ],
        [ANY] + [SMEM] * 2 + [VMEM],
        flops=views * 32 * by * by,
        nbytes=views * by * by * 4,
        name="return_bands",
    )(gain, profiles, view_boxes, estimate)
    half_rows = shape((bz + 2 * REACH, views * bx // 2, by), BF16)
    half_sums = []
    for slot, cells in enumerate(halves_of):
        half_sums += call(
            functools.partial(half_body, views, block, slot, paired, len(cells)),
            [half_rows, half_rows],
            [SMEM] * 2 + [VMEM] * (2 + len(cells)),
            [
                pltpu.VMEM((views + 1, bz, bx // 2, by), BF16),
                pltpu.VMEM((bz, bx // 2, by), F32),
                pltpu.VMEM((bz, bx // 2, by), F32),
            ],
            flops=views * bz * ext * by * 300,
            nbytes=views * bz * bx * by * 4,
            name="half" + str(slot),
        )(profiles, view_boxes, gain, yr, *cells)

    mid, *sums = call(
        functools.partial(return_body, block, links),
        [shape(block, F32)] + [link_shape(link, REACH, F32) for link in links],
        [VMEM] * 5,
        [pltpu.VMEM((bz + 2 * REACH, ext, by), F32)],
        flops=views * bz * ext * by * 100,
        nbytes=views * bz * bx * by * 4,
        name="returned",
    )(xr, *half_sums)
    sums = [exchange(cells, link, *counts) for link, cells in zip(links, sums)]
    return call(
        functools.partial(finish_body, counts, links),
        shape(block, F32),
        [VMEM] * (2 + len(links)),
        nbytes=bz * bx * by * 12,
        name="finish",
    )(share, mid, *sums)


def solution(mesh):
    placed = (
        P(("groups", "bz"), "bx", "by"),
        P(None, ("groups", "bz"), ("bx", "by"), None),
        P(),
        P("groups", None),
    )
    return jax.shard_map(
        local,
        mesh=mesh,
        in_specs=placed,
        out_specs=P(("groups", "bz"), "bx", "by"),
        check_vma=False,
    )
```

```python
import functools

import jax
import jax.numpy as jnp
from jax import lax
from jax.experimental import pallas as pl
from jax.experimental.pallas import tpu as pltpu
from jax.sharding import PartitionSpec as P

TAPS = 15
REACH = TAPS // 2
PAD = 8
SIDE = 2 * PAD
BACKGROUND = 0.05
GROUP = 6
WEIGHT = 0.5

F32 = jnp.float32
BF16 = jnp.bfloat16

VMEM = pl.BlockSpec(memory_space=pltpu.VMEM)
SMEM = pl.BlockSpec(memory_space=pltpu.SMEM)
ANY = pl.BlockSpec(memory_space=pl.ANY)
HBM = pl.BlockSpec(memory_space=pltpu.HBM)


def call(body, out_shape, in_specs, scratch=(), flops=0, nbytes=0, name=None):
    many = isinstance(out_shape, (list, tuple))
    return pl.pallas_call(
        body,
        out_shape=out_shape,
        in_specs=in_specs,
        out_specs=[VMEM] * len(out_shape) if many else VMEM,
        scratch_shapes=list(scratch),
        compiler_params=pltpu.CompilerParams(vmem_limit_bytes=40 * 1024 * 1024),
        cost_estimate=pl.CostEstimate(
            flops=int(WEIGHT * flops), bytes_accessed=int(WEIGHT * nbytes), transcendentals=0
        ),
        name=name,
    )


def partner(index, count, swap):
    other = index ^ 1 if swap == 0 else ((index + 1) ^ 1) - 1
    return other if 0 <= other < count else index


def swaps_of(count):
    return {1: [], 2: [0]}.get(count, [0, 1])


def meets_next(index, swap):
    return lax.rem(index + swap, 2) == 0


def has_partner(index, count, swap):
    after = meets_next(index, swap)
    return jnp.where(after, index < count - 1, index > 0)


def links_of(count_x, count_z):
    along_x, along_z = [None, *swaps_of(count_x)], [None, *swaps_of(count_z)]
    return [(x, z) for x in along_x for z in along_z if (x, z) != (None, None)]


def exchange(cells, link, count_x, count_z):
    x, z = link
    pairs = []
    for i in range(count_x):
        for j in range(count_z):
            to_x = i if x is None else partner(i, count_x, x)
            to_z = j if z is None else partner(j, count_z, z)
            pairs.append((i * count_z + j, to_x * count_z + to_z))
    return lax.ppermute(cells, ("bx", "bz"), pairs)


def exchange_y(first, second):
    count = lax.axis_size("by")
    return [
        lax.ppermute(cells, "by", [(i, partner(i, count, swap)) for i in range(count)])
        for swap, cells in enumerate((first, second))
    ]


def banded(offset, tap_of):
    matrix = jnp.zeros(offset.shape, F32)
    for tap in range(TAPS):
        matrix = jnp.where(offset == tap, tap_of(tap), matrix)
    return matrix


def halves(matrix):
    high = matrix.astype(BF16)
    return high, (matrix - high.astype(F32)).astype(BF16)


def packed(cells, begin):
    by = cells.shape[1]
    row = lax.broadcasted_iota(jnp.int32, (SIDE, by), 0)
    col = lax.broadcasted_iota(jnp.int32, (SIDE, by), 1)
    pick = jnp.where(col == row + begin, 1.0, 0.0).astype(BF16)
    return lax.dot_general(
        pick, cells, (((1,), (1,)), ((), ())), preferred_element_type=F32
    ).astype(BF16)


def unpack_both(count, first_ref, second_ref):
    mine = lax.axis_index("by")
    first, second = first_ref[...].astype(F32), second_ref[...].astype(F32)
    even = meets_next(mine, 0)
    before = jnp.where(even, second, first)
    after = jnp.where(even, first, second)
    before = jnp.where(mine > 0, before, 0.0)
    after = jnp.where(mine < count - 1, after, 0.0)
    return jnp.concatenate([before, after], axis=0).T.astype(BF16)


def columns_body(est_ref, cells_ref, first_ref, second_ref):
    bz, bx, by = est_ref.shape
    cells_ref[...] = est_ref[...].astype(BF16)
    cells = cells_ref[...].reshape(bz * bx, by)
    mine = lax.axis_index("by")
    first_ref[...] = packed(cells, jnp.where(meets_next(mine, 0), by - SIDE, 0))
    second_ref[...] = packed(cells, jnp.where(meets_next(mine, 1), by - SIDE, 0))


def pieces_body(order_ref, rec_ref, *out_refs):
    views, bz, rows, width = rec_ref.shape
    count = len(out_refs)
    by = width // count
    row = lax.broadcasted_iota(jnp.int32, (by, by), 0)
    col = lax.broadcasted_iota(jnp.int32, (by, by), 1)
    picks = []
    for k in range(views):
        lane = col - 2 * PAD * k
        picks.append((lane >= 0) & (lane < PAD) & (row == by - PAD + lane))
        picks.append((lane >= PAD) & (lane < 2 * PAD) & (row == lane - PAD))
    picks = jnp.concatenate([jnp.where(pick, 1.0, 0.0).astype(BF16) for pick in picks], axis=0)
    for other, out_ref in enumerate(out_refs):
        target = lax.axis_index("by") ^ other

        def columns(tile):
            return pl.ds(pl.multiple_of(jnp.clip(tile, 0, count - 1) * by, by), by)

        out_ref[:views] = rec_ref[:, :, :, columns(target)]
        beside = []
        for k in range(views):
            for tile in (target - 1, target + 1):
                cells = rec_ref[k, :, :, columns(tile)]
                beside.append(cells.astype(F32).reshape(bz * rows, by).astype(BF16))
        beside = jnp.dot(jnp.concatenate(beside, axis=1), picks, preferred_element_type=F32)
        out_ref[views] = beside.reshape(bz, rows, by).astype(BF16)


def upright(cells):
    return cells.astype(F32).T


def lying(cells):
    wide = cells.shape[1]
    row = lax.broadcasted_iota(jnp.int32, (wide, wide), 0)
    col = lax.broadcasted_iota(jnp.int32, (wide, wide), 1)
    same = jnp.where(row == col, 1.0, 0.0).astype(BF16)
    return lax.dot_general(
        same, cells.astype(BF16), (((1,), (1,)), ((), ())), preferred_element_type=F32
    )


def edges_body(count, est_ref, first_ref, second_ref, halo_ref, *out_refs):
    bz, bx, by = est_ref.shape
    halo_ref[...] = unpack_both(count, first_ref, second_ref)
    for swap, out_ref in enumerate(out_refs):
        begin = jnp.where(meets_next(lax.axis_index("bz"), swap), bz - PAD, 0)
        out_ref[:PAD] = est_ref[pl.ds(begin, PAD)]
        rows = halo_ref[pl.ds(pl.multiple_of(begin * bx, PAD * bx), PAD * bx), :]
        flat = lying(rows).astype(BF16)
        for i in range(PAD * bx // by):
            out_ref[PAD + i, : 2 * SIDE, :] = flat[:, i * by : (i + 1) * by]


def deep_body(counts, count_z, order_ref, est_ref, halo_ref, *refs):
    bz, bx, by = est_ref.shape
    deep = bz + 2 * PAD
    z_refs, (cells_ref, halos_ref, *out_refs) = refs[:count_z], refs[count_z:]
    cells_ref[...] = jnp.zeros_like(cells_ref)
    halos_ref[...] = jnp.zeros_like(halos_ref)
    cells_ref[PAD : PAD + bz] = est_ref[...].astype(F32)
    halos_ref[PAD : PAD + bz] = halo_ref[...].astype(F32).reshape(bz, bx, 2 * SIDE)
    for swap, z_ref in enumerate(z_refs):
        index = lax.axis_index("bz")
        at = pl.ds(jnp.where(meets_next(index, swap), PAD + bz, 0), PAD)

        @pl.when(has_partner(index, counts[1], swap))
        def _():
            cells_ref[at] = z_ref[:PAD].astype(F32)
            flat = jnp.concatenate(
                [z_ref[PAD + i, : 2 * SIDE, :] for i in range(PAD * bx // by)], axis=1
            )
            halos_ref[at] = upright(flat).reshape(PAD, bx, 2 * SIDE)

    for swap, out_ref in enumerate(out_refs):
        begin = jnp.where(meets_next(lax.axis_index("bx"), swap), bx - PAD, 0)
        at = pl.ds(pl.multiple_of(begin, PAD), PAD)
        out_ref[:deep] = cells_ref[:, at, :].astype(BF16)
        flat = lying(halos_ref[:, at, :].reshape(deep * PAD, 2 * SIDE))
        groups = 2 * SIDE // PAD
        for i in range(deep * PAD // by):
            for j in range(groups):
                part = flat[j * PAD : (j + 1) * PAD, i * by : (i + 1) * by]
                out_ref[deep + groups * i + j] = part.astype(BF16)


def iota(shape, dim):
    return lax.broadcasted_iota(jnp.int32, shape, dim)


def forward_bands_body(views, block, order_ref, prof_ref, yf_ref, yh_ref, xf_ref):
    bz, bx, by = block
    ext = bx + 2 * PAD
    shape_y = (by + 2 * SIDE, by)
    row = iota(shape_y, 0)
    source = jnp.where(row < by, row, jnp.where(row < by + SIDE, row - by - SIDE, row - SIDE))
    target = iota(shape_y, 1)
    beside_view = lax.div(target, 2 * PAD)
    beside = lax.rem(target, 2 * PAD)
    beside = jnp.where(beside < PAD, beside - PAD, by + beside - PAD)
    shape_x = (bx, 2 * ext)
    col = iota(shape_x, 1)
    is_low = col >= ext
    forward_x = jnp.where(is_low, col - ext, col) - PAD - iota(shape_x, 0)

    def view(k, carry):
        forward = banded(source - target + REACH, lambda tap: prof_ref[(k * 3 + 2) * TAPS + tap])
        high, low = halves(forward)
        yf_ref[k, :, :by] = high
        yf_ref[k, :, by:] = low
        forward = banded(source - beside + REACH, lambda tap: prof_ref[(k * 3 + 2) * TAPS + tap])
        high, low = halves(jnp.where(beside_view == k, forward, 0.0))
        yh_ref[k, :, :by] = high
        yh_ref[k, :, by:] = low
        high, low = halves(banded(forward_x + REACH, lambda tap: prof_ref[(k * 3 + 1) * TAPS + tap]))
        at = pl.ds(pl.multiple_of(k * bx, bx), bx)
        xf_ref[at, :] = jnp.where(is_low, low.astype(F32), high.astype(F32)).astype(BF16)
        return carry

    lax.fori_loop(0, views, view, 0)


def return_bands_body(views, paired, order_ref, prof_ref, box_ref, est_ref, yr_ref, xr_ref, share_ref):
    bz, bx, by = est_ref.shape
    ext = bx + 2 * PAD
    start_z = lax.axis_index("bz") * bz
    start_x = lax.axis_index("bx") * bx
    start_y = lax.axis_index("by") * by
    back_row, back_target = iota((by, by), 0), iota((by, by), 1)
    side_row, side_target = iota((2 * PAD, by), 0), iota((2 * PAD, by), 1)
    side_row = jnp.where(side_row < PAD, side_row - PAD, by + side_row - PAD)

    def view(k, carry):
        def back(row, target):
            within = (target >= box_ref[k * 6 + 4] - start_y) & (target < box_ref[k * 6 + 5] - start_y)
            matrix = banded(REACH - row + target, lambda tap: prof_ref[(k * 3 + 2) * TAPS + tap])
            return halves(jnp.where(within, matrix, 0.0))

        high, low = back(back_row, back_target)
        yr_ref[k, :by, :by] = high
        yr_ref[k, :by, by:] = low
        yr_ref[k, by:, :] = jnp.zeros((by, 2 * by), BF16)
        at = pl.ds(pl.multiple_of(by + 2 * PAD * k, 2 * PAD), 2 * PAD)
        high, low = back(side_row, side_target)
        yr_ref[k, at, :by] = high
        yr_ref[k, at, by:] = low
        return carry

    lax.fori_loop(0, views, view, 0)

    half_rows = bx // 2
    shape_x = (ext, views * bx)
    target = iota(shape_x, 0) - PAD
    col = iota(shape_x, 1)
    slot = lax.div(col, views * half_rows)
    half = jnp.where(slot == 0, half_of(0, paired), half_of(1, paired))
    owner = lax.div(lax.rem(col, views * half_rows), half_rows)
    source = half * half_rows + lax.rem(col, half_rows)

    def back_view(k, matrix):
        back = banded(REACH - source + target, lambda tap: prof_ref[(k * 3 + 1) * TAPS + tap])
        within = (target >= box_ref[k * 6 + 2] - start_x) & (target < box_ref[k * 6 + 3] - start_x)
        return jnp.where(owner == k, jnp.where(within, back, 0.0), matrix)

    high, low = halves(lax.fori_loop(0, views, back_view, jnp.zeros(shape_x, F32)))
    xr_ref[:ext] = high
    xr_ref[ext:] = low

    row_x = iota((bx, by), 0) + start_x
    col_y = iota((bx, by), 1) + start_y
    flat = []
    for k in range(views):
        within = (col_y >= box_ref[k * 6 + 4]) & (col_y < box_ref[k * 6 + 5])
        within = within & (row_x >= box_ref[k * 6 + 2]) & (row_x < box_ref[k * 6 + 3])
        flat.append(jnp.where(within, 1.0, 0.0))
    for plane in range(bz):
        coverage = jnp.zeros((bx, by), F32)
        for k in range(views):
            at = plane + start_z
            here = (at >= box_ref[k * 6 + 0]) & (at < box_ref[k * 6 + 1])
            coverage = coverage + jnp.where(here, 1.0, 0.0) * flat[k]
        share_ref[plane] = est_ref[plane] / coverage


def forward_body(views, block, counts, count_x, prof_ref, box_ref, cells_ref, halos_ref, yf_ref, yh_ref, xf_ref, *refs):
    x_refs, (gain_ref, side_halo, blurred_x, rows) = refs[:count_x], refs[count_x:]
    bz, bx, by = block
    deep = bz + 2 * PAD
    sides = []
    for swap, x_ref in enumerate(x_refs):
        index = lax.axis_index("bx")
        known = has_partner(index, counts[0], swap)
        after = meets_next(index, swap)
        sides.append((known & jnp.logical_not(after), known & after))
        groups = 2 * SIDE // PAD
        flat = [
            jnp.concatenate([x_ref[deep + groups * i + j].astype(F32) for j in range(groups)], axis=0)
            for i in range(deep * PAD // by)
        ]
        side_halo[swap] = jnp.concatenate(flat, axis=1).T.reshape(deep, PAD, 2 * SIDE)
    for plane in range(1, deep - 1):
        left = right = jnp.zeros((PAD, by), F32)
        left_halo = right_halo = jnp.zeros((PAD, 2 * SIDE), F32)
        for swap, (is_left, is_right) in enumerate(sides):
            came, came_halo = x_refs[swap][plane].astype(F32), side_halo[swap, plane]
            left = jnp.where(is_left, came, left)
            right = jnp.where(is_right, came, right)
            left_halo = jnp.where(is_left, came_halo, left_halo)
            right_halo = jnp.where(is_right, came_halo, right_halo)
        cells = jnp.concatenate([left, cells_ref[plane], right], axis=0).astype(BF16)
        halo = jnp.concatenate([left_halo, halos_ref[plane], right_halo], axis=0).astype(BF16)
        cells = jnp.concatenate([cells, halo], axis=1)
        cells = jnp.concatenate([cells, cells], axis=0)
        mixed = jnp.dot(xf_ref[...], cells, preferred_element_type=F32).astype(BF16)
        for k in range(views):
            blurred_x[k, plane * bx : (plane + 1) * bx, :] = mixed[k * bx : (k + 1) * bx]
    row_x = lax.broadcasted_iota(jnp.int32, (8, by), 0) + lax.axis_index("bx") * bx
    col_y = lax.broadcasted_iota(jnp.int32, (8, by), 1) + lax.axis_index("by") * by
    start_z = lax.axis_index("bz") * bz
    step = 10

    def view(k, carry):
        along_y = yf_ref[k]
        for first in range(1, deep - 1, step):
            mixed = jnp.dot(
                blurred_x[k, first * bx : (first + step) * bx, :], along_y, preferred_element_type=F32
            )
            rows[first : first + step] = (mixed[:, :by] + mixed[:, by:]).reshape(step, bx, by)
        taps = [prof_ref[(k * 3 + 0) * TAPS + tap] for tap in range(TAPS)]
        within_y = (col_y >= box_ref[k * 6 + 4]) & (col_y < box_ref[k * 6 + 5])
        inside = []
        for tile in range(0, bx, 8):
            at = row_x + tile
            inside.append(jnp.where(within_y & (at >= box_ref[k * 6 + 2]) & (at < box_ref[k * 6 + 3]), 1.0, 0.0))
        low_z = box_ref[k * 6 + 0] - start_z
        high_z = box_ref[k * 6 + 1] - start_z
        for first in range(0, bz, 4):
            some = (first + 4 > low_z) & (first < high_z)

            @pl.when(some)
            def _():
                for tile in range(0, bx, 8):
                    for plane in range(first, first + 4):
                        total = taps[0] * rows[plane + 1, tile : tile + 8, :]
                        for tap in range(1, TAPS):
                            total = total + taps[tap] * rows[plane + 1 + tap, tile : tile + 8, :]
                        here = jnp.where((plane >= low_z) & (plane < high_z), 1.0, 0.0)
                        gain_ref[k, plane, tile : tile + 8, :] = here * inside[tile // 8] / (total + BACKGROUND)

            @pl.when(jnp.logical_not(some))
            def _():
                gain_ref[k, first : first + 4] = jnp.zeros((4, bx, by), F32)

        return carry

    lax.fori_loop(0, views, view, 0)

    lane = lax.broadcasted_iota(jnp.int32, (8, by), 1)
    owner = lax.div(lane, 2 * PAD)
    col_y = lax.rem(lane, 2 * PAD)
    col_y = jnp.where(col_y < PAD, col_y - PAD, by + col_y - PAD) + lax.axis_index("by") * by

    def by_lane(value, start):
        for k in range(views):
            start = jnp.where(owner == k, value(k), start)
        return start

    taps = [by_lane(lambda k: prof_ref[(k * 3 + 0) * TAPS + tap], jnp.zeros((8, by), F32)) for tap in range(TAPS)]
    box = [by_lane(lambda k: box_ref[k * 6 + i], jnp.zeros((8, by), jnp.int32)) for i in range(6)]
    within_y = (col_y >= box[4]) & (col_y < box[5])
    step = 5
    for first in range(1, deep - 1, step):
        at = slice(first * bx, (first + step) * bx)
        mixed = jnp.dot(blurred_x[0, at, :], yh_ref[0], preferred_element_type=F32)
        for k in range(1, views):
            mixed = mixed + jnp.dot(blurred_x[k, at, :], yh_ref[k], preferred_element_type=F32)
        rows[first : first + step] = (mixed[:, :by] + mixed[:, by:]).reshape(step, bx, by)

    def beside_plane(plane, carry):
        at_z = plane + start_z
        within_z = within_y & (at_z >= box[0]) & (at_z < box[1])
        for tile in range(0, bx, 8):
            at_x = row_x + tile
            total = taps[0] * rows[plane + 1, tile : tile + 8, :]
            for tap in range(1, TAPS):
                total = total + taps[tap] * rows[plane + 1 + tap, tile : tile + 8, :]
            within = within_z & (at_x >= box[2]) & (at_x < box[3])
            gain_ref[views, plane, tile : tile + 8, :] = jnp.where(within, 1.0, 0.0) / (total + BACKGROUND)
        return carry

    lax.fori_loop(0, bz, beside_plane, 0)


def half_of(slot, paired):
    return lax.div(lax.axis_index("by"), 2) ^ slot if paired else slot


def half_body(views, block, slot, paired, count, prof_ref, box_ref, gain_ref, yr_ref, *refs):
    parts = refs[:count]
    high_ref, low_ref, quot, held, rows = refs[count:]
    bz, bx, by = block
    deep = bz + 2 * REACH
    half_rows = bx // 2
    part_rows = half_rows // count
    begin = half_of(slot, paired) * half_rows
    start_z = lax.axis_index("bz") * bz
    start_x = lax.axis_index("bx") * bx + begin
    start_y = lax.axis_index("by") * by

    def quotient(k, carry):
        for i, part_ref in enumerate(parts):
            at = lax.rem(lax.axis_index("by") ^ i, 2) * part_rows if count == 2 else 0
            gain = gain_ref[k, :, pl.ds(pl.multiple_of(begin + at, 8), part_rows), :]
            at = pl.ds(pl.multiple_of(at, 8), part_rows)
            held[:, at, :] = gain * part_ref[k].astype(F32)
        quot[k] = held[...].astype(BF16)
        return carry

    lax.fori_loop(0, views + 1, quotient, 0)

    def view(k, carry):
        meets = (box_ref[k * 6 + 2] < start_x + half_rows) & (box_ref[k * 6 + 3] > start_x)
        meets = meets & (box_ref[k * 6 + 4] < start_y + by) & (box_ref[k * 6 + 5] > start_y)

        @pl.when(meets)
        def _():
            cells = [quot[i].reshape(bz * half_rows, by) for i in (k, views)]
            cells = jnp.concatenate(cells, axis=1)
            mixed = jnp.dot(cells, yr_ref[k], preferred_element_type=F32)
            rows[...] = (mixed[:, :by] + mixed[:, by:]).reshape(bz, half_rows, by)

        taps = [prof_ref[(k * 3 + 0) * TAPS + tap] for tap in range(TAPS)]
        at = pl.ds(pl.multiple_of(k * half_rows, half_rows), half_rows)
        low_z = box_ref[k * 6 + 0] - start_z + REACH
        high_z = box_ref[k * 6 + 1] - start_z + REACH
        for first in range(0, deep, GROUP):
            some = meets & (first + GROUP > low_z) & (first < high_z)

            @pl.when(some)
            def _():
                for out in range(first, first + GROUP):
                    plane = out - REACH
                    parts = []
                    for tile in range(0, half_rows, 8):
                        part = None
                        for source in range(max(0, plane - REACH), min(bz, plane + REACH + 1)):
                            term = taps[REACH - source + plane] * rows[source, tile : tile + 8, :]
                            part = term if part is None else part + term
                        parts.append(part)
                    here = jnp.where((out >= low_z) & (out < high_z), 1.0, 0.0)
                    high, low = halves(here * jnp.concatenate(parts, axis=0))
                    high_ref[out, at, :] = high
                    low_ref[out, at, :] = low

            @pl.when(jnp.logical_not(some))
            def _():
                high_ref[first : first + GROUP, at, :] = jnp.zeros((GROUP, half_rows, by), BF16)
                low_ref[first : first + GROUP, at, :] = jnp.zeros((GROUP, half_rows, by), BF16)

        return carry

    lax.fori_loop(0, views, view, 0)


def return_body(block, links, xr_ref, *refs):
    rows_refs, mid_ref, link_refs, total = refs[:4], refs[4], refs[5:-1], refs[-1]
    bz, bx, by = block
    ext = bx + 2 * PAD
    deep = bz + 2 * REACH

    def both(first_ref, second_ref, out):
        planes = [
            jnp.concatenate([first_ref[i], second_ref[i]], axis=0) for i in (out, out + 1)
        ]
        return jnp.concatenate(planes, axis=1)

    for out in range(0, deep, 2):
        high = both(rows_refs[0], rows_refs[2], out)
        low = both(rows_refs[1], rows_refs[3], out)
        mixed = jnp.dot(xr_ref[...], high, preferred_element_type=F32)
        mixed = mixed[:ext] + mixed[ext:] + jnp.dot(xr_ref[:ext], low, preferred_element_type=F32)
        total[out] = mixed[:, :by]
        total[out + 1] = mixed[:, by:]
    mid_ref[...] = total[REACH : REACH + bz, PAD : PAD + bx, :]
    for (x, z), link_ref in zip(links, link_refs):
        at_x, at_z = slice(PAD, PAD + bx), slice(REACH, REACH + bz)
        if x is not None:
            begin = jnp.where(meets_next(lax.axis_index("bx"), x), PAD + bx, 0)
            at_x = pl.ds(pl.multiple_of(begin, PAD), PAD)
        if z is not None:
            at_z = pl.ds(jnp.where(meets_next(lax.axis_index("bz"), z), REACH + bz, 0), REACH)
        link_ref[...] = total[at_z, at_x, :]


def finish_body(counts, links, share_ref, mid_ref, *refs):
    bz, bx, by = share_ref.shape
    link_refs, out_ref = refs[: len(links)], refs[len(links)]
    out_ref[...] = share_ref[...] * mid_ref[...]
    for (x, z), link_ref in zip(links, link_refs):
        at_x, at_z, known = slice(None), slice(None), None
        if x is not None:
            index = lax.axis_index("bx")
            begin = jnp.where(meets_next(index, x), bx - PAD, 0)
            at_x = pl.ds(pl.multiple_of(begin, PAD), PAD)
            known = has_partner(index, counts[0], x)
        if z is not None:
            index = lax.axis_index("bz")
            at_z = pl.ds(jnp.where(meets_next(index, z), bz - REACH, 0), REACH)
            there = has_partner(index, counts[1], z)
            known = there if known is None else known & there

        @pl.when(known)
        def _():
            out_ref[at_z, at_x, :] = out_ref[at_z, at_x, :] + share_ref[at_z, at_x, :] * link_ref[...]


def local(estimate, recorded, profiles, view_boxes):
    block = estimate.shape
    bz, bx, by = block
    views = recorded.shape[0]
    part_rows = recorded.shape[2]
    count = lax.axis_size("by")
    counts = (lax.axis_size("bx"), lax.axis_size("bz"))
    links = links_of(*counts)
    ext = bx + 2 * PAD
    deep = bz + 2 * PAD
    shape = jax.ShapeDtypeStruct
    profiles, view_boxes = profiles.reshape(-1), view_boxes.reshape(-1)

    def link_shape(link, reach, dtype):
        x, z = link
        return shape((bz if z is None else reach, bx if x is None else PAD, by), dtype)

    side = shape((SIDE, bz * bx), BF16)
    own, order, second = call(
        columns_body,
        [shape(block, BF16), side, side],
        [VMEM],
        nbytes=bz * bx * by * 4,
        name="columns",
    )(estimate)
    first, second = exchange_y(order, second)

    if count == 4 and part_rows % 8 == 0:
        parts = [*call(
            pieces_body,
            [shape((views + 1, bz, part_rows, by), BF16)] * count,
            [ANY, VMEM],
            nbytes=views * bz * bx * by * 4,
            name="pieces",
        )(order, recorded)]
        parts[1] = lax.ppermute(parts[1], "by", [(i, i ^ 1) for i in range(count)])
        parts[2:], first, second = lax.optimization_barrier((parts[2:], first, second))
        for other in range(2, count):
            parts[other] = lax.ppermute(parts[other], "by", [(i, i ^ other) for i in range(count)])
    else:
        tiles = jnp.moveaxis(recorded.reshape(views, bz, part_rows, count, by), 3, 0)
        before = jnp.roll(tiles[..., by - PAD :], 1, axis=0)
        after = jnp.roll(tiles[..., :PAD], -1, axis=0)
        beside = jnp.moveaxis(jnp.concatenate([before, after], axis=-1), 1, 3)
        beside = beside.reshape(count, 1, bz, part_rows, views * 2 * PAD)
        beside = jnp.pad(beside, [(0, 0)] * 4 + [(0, by - views * 2 * PAD)])
        tiles = jnp.concatenate([tiles, beside], axis=1)
        tiles = lax.all_to_all(tiles, "by", split_axis=0, concat_axis=0, tiled=True)
        parts = [jnp.moveaxis(tiles, 0, 2).reshape(views + 1, bz, bx, by)]

    paired = len(parts) == 4
    if paired:
        halves_of = [parts[:2], parts[2:]]
    else:
        halves_of = [[parts[0][:, :, : bx // 2]], [parts[0][:, :, bx // 2 :]]]

    along_x, along_z = swaps_of(counts[0]), swaps_of(counts[1])
    halo, *edges = call(
        functools.partial(edges_body, count),
        [shape((bz * bx, 2 * SIDE), BF16)]
        + [shape((PAD + PAD * bx // by, bx, by), BF16)] * len(along_z),
        [VMEM] * 3,
        nbytes=bz * bx * by * 4,
        name="edges",
    )(own, first, second)
    edges = [exchange(cells, (None, swap), *counts) for swap, cells in zip(along_z, edges)]

    cells, halos, *edges = call(
        functools.partial(deep_body, counts, len(along_z)),
        [shape((deep, bx, by), F32), shape((deep, bx, 2 * SIDE), F32)]
        + [shape((deep + 2 * SIDE * deep // by, PAD, by), BF16)] * len(along_x),
        [ANY] + [VMEM] * (2 + len(along_z)),
        nbytes=deep * bx * by * 4,
        name="deep",
    )(own, own, halo, *edges)
    edges = [exchange(cells, (swap, None), *counts) for swap, cells in zip(along_x, edges)]

    yf, yh, xf = call(
        functools.partial(forward_bands_body, views, block),
        [
            shape((views, by + 2 * SIDE, 2 * by), BF16),
            shape((views, by + 2 * SIDE, 2 * by), BF16),
            shape((views * bx, 2 * ext), BF16),
        ],
        [ANY, SMEM],
        flops=views * 32 * by * by,
        nbytes=views * by * by * 4,
        name="forward_bands",
    )(order, profiles)

    gain = call(
        functools.partial(forward_body, views, block, counts, len(along_x)),
        shape((views + 1, bz, bx, by), F32),
        [SMEM] * 2 + [VMEM] * (5 + len(along_x)),
        [
            pltpu.VMEM((max(1, len(along_x)), deep, PAD, 2 * SIDE), F32),
            pltpu.VMEM((views, deep * bx, by + 2 * SIDE), BF16),
            pltpu.VMEM((deep, bx, by), F32),
        ],
        flops=views * deep * ext * by * 600,
        nbytes=views * bz * bx * by * 8,
        name="forward",
    )(profiles, view_boxes, cells, halos, yf, yh, xf, *edges)

    yr, xr, share = call(
        functools.partial(return_bands_body, views, paired),
        [
            shape((views, 2 * by, 2 * by), BF16),
            shape((2 * ext, views * bx), BF16),
            shape(block, F32),
        ],
        [ANY] + [SMEM] * 2 + [VMEM],
        flops=views * 32 * by * by,
        nbytes=views * by * by * 4,
        name="return_bands",
    )(gain, profiles, view_boxes, estimate)
    half_rows = shape((bz + 2 * REACH, views * bx // 2, by), BF16)
    half_sums = []
    for slot, cells in enumerate(halves_of):
        half_sums += call(
            functools.partial(half_body, views, block, slot, paired, len(cells)),
            [half_rows, half_rows],
            [SMEM] * 2 + [VMEM] * (2 + len(cells)),
            [
                pltpu.VMEM((views + 1, bz, bx // 2, by), BF16),
                pltpu.VMEM((bz, bx // 2, by), F32),
                pltpu.VMEM((bz, bx // 2, by), F32),
            ],
            flops=views * bz * ext * by * 300,
            nbytes=views * bz * bx * by * 4,
            name="half" + str(slot),
        )(profiles, view_boxes, gain, yr, *cells)

    mid, *sums = call(
        functools.partial(return_body, block, links),
        [shape(block, F32)] + [link_shape(link, REACH, F32) for link in links],
        [VMEM] * 5,
        [pltpu.VMEM((bz + 2 * REACH, ext, by), F32)],
        flops=views * bz * ext * by * 100,
        nbytes=views * bz * bx * by * 4,
        name="returned",
    )(xr, *half_sums)
    sums = [exchange(cells, link, *counts) for link, cells in zip(links, sums)]
    return call(
        functools.partial(finish_body, counts, links),
        shape(block, F32),
        [VMEM] * (2 + len(links)),
        nbytes=bz * bx * by * 12,
        name="finish",
    )(share, mid, *sums)


def solution(mesh):
    placed = (
        P(("groups", "bz"), "bx", "by"),
        P(None, ("groups", "bz"), ("bx", "by"), None),
        P(),
        P("groups", None),
    )
    return jax.shard_map(
        local,
        mesh=mesh,
        in_specs=placed,
        out_specs=P(("groups", "bz"), "bx", "by"),
        check_vma=False,
    )
```
